128 devices in a mesh: region: 16 (over y_lo, z, core), group: 8 (over y_hi, x).
Axes of the slice: x: 4, y: 4 (y_hi: 2, y_lo: 2; y = y_hi * 2 + y_lo), z: 4, core: 2. Of those that a mesh axis runs over, the one named last changes fastest.
Arguments:
- object_slab: float32 [8192, 2, 4096], P('region', None, 'group'), may hold values from -6 to 6
- probe: float32 [4, 2, 256, 256], replicated, may hold values from -6 to 6
- diffraction: float32 [512, 256, 256], P(('region', 'group')), may hold values from 0.25 to 16
- positions: int32 [512, 2], P(('region', 'group')), may hold values from 0 to 7936, as said below
- slot_counts: int32 [8, 16], P('group', 'region'), may hold values from 1 to 4, 40 in all within a row
Outputs:
- new_object: float32 [8192, 2, 4096], P('region', None, 'group')
- new_probe: float32 [4, 2, 256, 256], replicated
The draws below stay inside these ranges and needn't reach their ends.
Inputs may be any that keep to these rules, and one draw needn't show every extreme that they name: `positions`: A slot of region index r has its row in r * 512 to min(r * 512 + 511, 7936); columns lie in 0 to 256; rows 0 and 7936 and columns 0 and 256 are each taken by some slot.
All inputs are finite; a program needn't handle non-finite values. No bound on the sum of `slot_counts` on one device may be relied on, other than what follows from the above.
Results may differ from the reference program's by a relative error of at most 0.0003.
Values sent between devices are 32-bit elements; how exact they have to be, the bound alone decides.
A program may use at most 128 MiB of HBM per device.

```python
import math
import jax
import jax.numpy as jnp
import numpy as np
from jax import lax

P_SIZE = 256
MODES = 4
CAP = 4
TH = 512
SW = 512
ITERS = 1
OH = 8192
OW = 4096
PATTERNS = 512
LIVE = 40
N_REGION = 16
N_GROUP = 8


def draw_positions(key, part):
    k_rows, k_cols, k_pick = jax.random.split(key, 3)
    index = jnp.arange(PATTERNS, dtype=jnp.int32)
    region_of = index // (N_GROUP * CAP)
    offsets = jax.random.randint(k_rows, (PATTERNS,), 0, TH)
    rows = jnp.minimum(region_of * TH + offsets, OH - P_SIZE)
    rows = rows.at[0].set(0).at[PATTERNS - 1].set(OH - P_SIZE)
    cols = jax.random.randint(k_cols, (PATTERNS,), 0, SW - P_SIZE + 1)
    picks = jax.random.permutation(k_pick, PATTERNS)
    cols = cols.at[picks[0]].set(0).at[picks[1]].set(SW - P_SIZE)
    return jnp.stack([rows, cols], axis=1).astype(jnp.int32)


def shard_levels(stream_key, shape, shards, low, high):
    loudness = 1.0
    for axis_at, parts in shards:
        heights = jax.random.uniform(jax.random.fold_in(jax.random.fold_in(stream_key, 6), axis_at), (parts,), jnp.float32, low / len(shards), high / len(shards))
        loudness = loudness * jnp.repeat(jnp.exp(heights), shape[axis_at] // parts).reshape((-1,) + (1,) * (len(shape) - 1 - axis_at))
    return loudness


def length_profile(amount, total, most, lean):
    weights = [(1 << 20) // math.isqrt(grade ** lean) + 1 for grade in range(2, amount + 1)]
    surplus, holding = total - most - (amount - 1), [1] * (amount - 1)
    while surplus > 0:
        free = [i for i in range(amount - 1) if holding[i] < most]
        mass, remaining = sum([weights[i] for i in free]), surplus
        for i in free:
            more = min(most - holding[i], max(1, remaining * weights[i] // mass), surplus)
            holding[i] = holding[i] + more
            surplus = surplus - more
    return np.array([most] + holding)


def ragged(own_key, count, total, most, skew):
    if count == 2:
        one = jax.random.randint(own_key, (), max(1, total - most), min(most, total - 1) + 1)
        return jnp.stack([one, total - one])
    sizes = jnp.asarray(length_profile(count, total, most, skew), jnp.int32)
    couples = (count - 1) // 2
    donor, taker = sizes[1:1 + 2 * couples:2], sizes[2:2 + 2 * couples:2]
    slack = jnp.minimum(donor - 1, most - taker)
    shifted = jax.random.randint(jax.random.fold_in(own_key, 1), (couples,), 0, 1 << 20) % (slack + 1)
    sizes = sizes.at[1:1 + 2 * couples:2].set(donor - shifted).at[2:2 + 2 * couples:2].set(taker + shifted)
    return sizes[jax.random.permutation(jax.random.fold_in(own_key, 2), count)]


def noise(stream_key, dims, width, bound, cuts=(), kind=jnp.bfloat16):
    factor_of = shard_levels(stream_key, dims, cuts, -0.22, 0.18) if cuts else 1.0
    array = jax.random.normal(stream_key, dims, jnp.float32) * width * factor_of
    return jnp.minimum(jnp.maximum(array, -bound), bound).astype(kind)


def setup_inputs(seed: int = 0) -> dict:
    key_of = jax.random.split(jax.random.key(seed), 6)
    object_slab = noise(key_of[0], (OH, 2, OW), 1.0, 6.0, ((0, 16), (2, 8)), jnp.float32)
    probe = noise(key_of[1], (MODES, 2, P_SIZE, P_SIZE), 1.0, 6.0, (), jnp.float32)
    diffraction = jnp.clip(jnp.exp(math.log(16.0) - 4.158883 * jax.random.uniform(key_of[2], (PATTERNS, P_SIZE, P_SIZE), jnp.float32) ** shard_levels(key_of[2], (PATTERNS, P_SIZE, P_SIZE), ((0, 128),), -0.2, 0.2)), 0.25, 16.0)
    positions = draw_positions(jax.random.fold_in(key_of[5], 71), 0)
    slot_counts = jax.vmap(lambda own: ragged(own, N_REGION, LIVE, CAP, 2))(jax.random.split(key_of[4], N_GROUP)).reshape((N_GROUP, N_REGION)).astype(jnp.int32)
    return {"object_slab": object_slab, "probe": probe, "diffraction": diffraction, "positions": positions, "slot_counts": slot_counts}


def reference(object_slab, probe, diffraction, positions, slot_counts):
    obj = object_slab
    prb = probe
    for step in range(ITERS):
        probe_c = lax.complex(prb[:, 0], prb[:, 1])
        peak = jnp.max(lax.optimization_barrier(jnp.sum(prb[:, 0] * prb[:, 0] + prb[:, 1] * prb[:, 1], axis=0)))

        def one(carry, index):
            ograd, pgrad, cover = carry
            position_entry = index % CAP
            device = index // CAP
            grp = device % N_GROUP
            reg = device // N_GROUP
            live = (position_entry < slot_counts[grp, reg]).astype(jnp.float32)
            row = positions[index, 0].astype(jnp.int32)
            col = (positions[index, 1] + grp * SW).astype(jnp.int32)
            win = lax.dynamic_slice(obj, (row, jnp.int32(0), col), (P_SIZE, 2, P_SIZE))
            win_c = lax.complex(win[:, 0, :], win[:, 1, :])
            far = jnp.fft.fft2(probe_c * win_c[None], norm='ortho')
            model_intensity = lax.optimization_barrier(jnp.sum(far.real * far.real + far.imag * far.imag, axis=0))
            update_ratio = 1.0 - jnp.sqrt(diffraction[index]) / jnp.sqrt(jnp.maximum(model_intensity, 1.0))
            chi = jnp.fft.ifft2(far * update_ratio[None], norm='ortho')
            chi_r = chi.real * live
            chi_i = chi.imag * live
            pr = probe_c.real
            pim = probe_c.imag
            go_r = lax.optimization_barrier(jnp.sum(pr * chi_r + pim * chi_i, axis=0))
            go_i = lax.optimization_barrier(jnp.sum(pr * chi_i - pim * chi_r, axis=0))
            wr = win_c.real
            wi = win_c.imag
            gp = jnp.stack([wr[None] * chi_r + wi[None] * chi_i, wr[None] * chi_i - wi[None] * chi_r], axis=1)
            current = lax.dynamic_slice(ograd, (row, jnp.int32(0), col), (P_SIZE, 2, P_SIZE))
            ograd = lax.dynamic_update_slice(ograd, current + jnp.stack([go_r, go_i], axis=1), (row, jnp.int32(0), col))
            return ((ograd, pgrad + gp, cover + live * (wr * wr + wi * wi)), None)
        start = (jnp.zeros(obj.shape, jnp.float32), jnp.zeros(prb.shape, jnp.float32), jnp.zeros((P_SIZE, P_SIZE), jnp.float32))
        (ograd, pgrad, cover), unused = lax.scan(one, start, jnp.arange(PATTERNS, dtype=jnp.int32))
        obj = obj - ograd / peak
        prb = prb - pgrad / (cover + 1e-06)[None, None]
    return (obj, prb)
```

```python
import functools
import math

import jax
import jax.numpy as jnp
import ml_dtypes
import numpy as np
from jax import lax
from jax.experimental import pallas as pl
from jax.experimental.pallas import tpu as pltpu
from jax.sharding import PartitionSpec as P

F32 = jnp.float32
BF16 = jnp.bfloat16
HALF = 128


def split_table(table):
    high = table.astype(np.float32).astype(ml_dtypes.bfloat16)
    low = (table - high.astype(np.float64)).astype(np.float32).astype(ml_dtypes.bfloat16)
    return high, low


def tables():
    n = np.arange(HALF)[:, None].astype(np.float64)
    k = np.arange(HALF)[None, :].astype(np.float64)
    out = {}
    for parity in (0, 1):
        angle = -2.0 * math.pi * ((n * (2 * k + parity)) % 256) / 256
        re, im = np.cos(angle) / 16, np.sin(angle) / 16
        full = np.block([[re, im], [-im, re]])
        high, low = split_table(full)
        out["r", parity] = np.concatenate([high, high, low], axis=0)
        out["rt", parity] = np.concatenate([high.T, high.T, low.T], axis=0)
        out["l", parity] = np.concatenate([high, high, low], axis=1)
        out["lt", parity] = np.concatenate([high.T, high.T, low.T], axis=1)
    perm = np.zeros((256, 256), np.float32)
    for c in range(256):
        perm[c, (c % 2) * HALF + c // 2] = 1
    perm = perm.astype(ml_dtypes.bfloat16)
    return (
        np.stack([out["r", 0], out["r", 1]]),
        np.stack([out["rt", 0], out["rt", 1]]),
        np.stack([out["l", 0], out["l", 1]]),
        np.stack([out["lt", 0], out["lt", 1]]),
        np.concatenate([perm, perm], axis=0),
    )


def parts_of(x):
    high = x.astype(BF16)
    low = (x - high.astype(F32)).astype(BF16)
    return high, low


def mul_right(x, table):
    high, low = parts_of(x)
    return jnp.dot(jnp.concatenate([high, low, high], axis=1), table, preferred_element_type=F32)


def mul_left(table, x):
    high, low = parts_of(x)
    return jnp.dot(table, jnp.concatenate([high, low, high], axis=0), preferred_element_type=F32)


def swap_blocks(a, b):
    return jnp.concatenate(
        [
            jnp.concatenate([a[:, :HALF], b[:, :HALF]], axis=1),
            jnp.concatenate([a[:, HALF:], b[:, HALF:]], axis=1),
        ],
        axis=0,
    )


def compute_kernel(
    rows_ref, cols_ref, count_ref, object_ref, halo_ref, probe_ref, diff_ref,
    r_ref, rt_ref, l_ref, lt_ref, perm_ref,
    part_ref, spill_ref, pgrad_ref, cover_ref,
    ext_ref, acc_ref, win_ref, far_ref, go_ref, factor_ref,
):
    modes = probe_ref.shape[0]
    own = object_ref.shape[0]
    ext_ref[:own] = object_ref[...]
    ext_ref[own:] = halo_ref[...]
    acc_ref[...] = jnp.zeros_like(acc_ref)
    pgrad_ref[...] = jnp.zeros_like(pgrad_ref)
    cover_ref[...] = jnp.zeros_like(cover_ref)

    total = jnp.zeros((256, 256), F32)
    for m in range(modes):
        total = total + probe_ref[m, 0] * probe_ref[m, 0] + probe_ref[m, 1] * probe_ref[m, 1]
    peak = jnp.max(total)

    lane = lax.broadcasted_iota(jnp.int32, (256, HALF), 1)

    def slot_body(s, carry):
        row, col = rows_ref[s], cols_ref[s]
        q, shift = col // HALF, lax.rem(col, HALF)

        def where_at(c, k):
            return pl.ds(row * 8 + jnp.minimum(q + k, 3) * 2 + c, 256, stride=8)

        back = lax.rem(HALF - shift, HALF)
        for c in (0, 1):
            t = [pltpu.roll(ext_ref[where_at(c, k), :], back, axis=1) for k in range(3)]
            for k in (0, 1):
                win_ref[c, :, k * HALF : (k + 1) * HALF] = jnp.where(lane < HALF - shift, t[k], t[k + 1])
        wr, wi = win_ref[0], win_ref[1]
        cover_ref[...] += wr * wr + wi * wi

        def forward(m, carry):
            pr, pi = probe_ref[m, 0], probe_ref[m, 1]
            wr, wi = win_ref[0], win_ref[1]
            er = pr * wr - pi * wi
            ei = pr * wi + pi * wr
            a = jnp.concatenate([er[:, :HALF] + er[:, HALF:], ei[:, :HALF] + ei[:, HALF:]], axis=1)
            b = jnp.concatenate([er[:, :HALF] - er[:, HALF:], ei[:, :HALF] - ei[:, HALF:]], axis=1)
            ye = mul_right(a, r_ref[0])
            yo = mul_right(b, r_ref[1])
            plus = swap_blocks(ye[:HALF] + ye[HALF:], yo[:HALF] + yo[HALF:])
            minus = swap_blocks(ye[:HALF] - ye[HALF:], yo[:HALF] - yo[HALF:])
            far_ref[m, 0] = mul_left(lt_ref[0], plus)
            far_ref[m, 1] = mul_left(lt_ref[1], minus)
            return carry

        lax.fori_loop(0, modes, forward, 0)

        for p in (0, 1):
            intensity = jnp.zeros((HALF, 256), F32)
            for m in range(modes):
                fr, fi = far_ref[m, p, :HALF], far_ref[m, p, HALF:]
                intensity = intensity + (fr * fr + fi * fi)
            wanted = jnp.sqrt(
                jnp.concatenate(
                    [
                        diff_ref[s, h, pl.ds(p, HALF, stride=2), :]
                        for h in (0, 1)
                    ],
                    axis=1,
                )
            )
            high, low = parts_of(wanted)
            wanted = jnp.dot(
                jnp.concatenate([high, low], axis=1), perm_ref[...], preferred_element_type=F32
            )
            factor_ref[p] = 1.0 - wanted / jnp.sqrt(jnp.maximum(intensity, 1.0))

        go_ref[...] = jnp.zeros_like(go_ref)

        def inverse(m, carry):
            ge = far_ref[m, 0] * jnp.concatenate([factor_ref[0], factor_ref[0]], axis=0)
            gd = far_ref[m, 1] * jnp.concatenate([factor_ref[1], factor_ref[1]], axis=0)
            e = mul_left(l_ref[0], ge)
            o = mul_left(l_ref[1], gd)
            top, bottom = e + o, e - o
            ae, ao = [
                jnp.concatenate(
                    [
                        jnp.concatenate([x[:HALF, at : at + HALF], x[HALF:, at : at + HALF]], axis=1)
                        for x in (top, bottom)
                    ],
                    axis=0,
                )
                for at in (0, HALF)
            ]
            e = mul_right(ae, rt_ref[0])
            o = mul_right(ao, rt_ref[1])
            left, right = e + o, e - o
            cr = jnp.concatenate([left[:, :HALF], right[:, :HALF]], axis=1)
            ci = jnp.concatenate([left[:, HALF:], right[:, HALF:]], axis=1)
            pr, pi = probe_ref[m, 0], probe_ref[m, 1]
            wr, wi = win_ref[0], win_ref[1]
            go_ref[0] += pr * cr + pi * ci
            go_ref[1] += pr * ci - pi * cr
            pgrad_ref[m, 0] += wr * cr + wi * ci
            pgrad_ref[m, 1] += wr * ci - wi * cr
            return carry

        lax.fori_loop(0, modes, inverse, 0)

        for c in (0, 1):
            g = [pltpu.roll(go_ref[c, :, k * HALF : (k + 1) * HALF], shift, axis=1) for k in (0, 1)]
            zero = jnp.zeros_like(g[0])
            for k, (here, wrapped) in enumerate(((g[0], zero), (g[1], g[0]), (zero, g[1]))):
                acc_ref[where_at(c, k), :] += jnp.where(lane >= shift, here, wrapped)
        return carry

    lax.fori_loop(0, count_ref[0], slot_body, 0)
    part_ref[...] = object_ref[...] - acc_ref[:own] / peak
    spill_ref[...] = acc_ref[own:] / peak


def compute(rows, cols, count, view, halo, probe, diffraction):
    modes = probe.shape[0]
    slots = diffraction.shape[0]
    consts = [jnp.asarray(t) for t in tables()]
    smem = pl.BlockSpec(memory_space=pltpu.SMEM)
    vmem = pl.BlockSpec(memory_space=pltpu.VMEM)
    diffraction = diffraction.reshape(slots, 256, 2, HALF).transpose(0, 2, 1, 3)
    return pl.pallas_call(
        compute_kernel,
        out_shape=(
            jax.ShapeDtypeStruct(view.shape, F32),
            jax.ShapeDtypeStruct(halo.shape, F32),
            jax.ShapeDtypeStruct(probe.shape, F32),
            jax.ShapeDtypeStruct((256, 256), F32),
        ),
        in_specs=[smem] * 3 + [vmem] * (4 + len(consts)),
        out_specs=[vmem] * 4,
        scratch_shapes=[
            pltpu.VMEM((view.shape[0] + halo.shape[0], HALF), F32),
            pltpu.VMEM((view.shape[0] + halo.shape[0], HALF), F32),
            pltpu.VMEM((2, 256, 256), F32),
            pltpu.VMEM((modes, 2, 256, 256), F32),
            pltpu.VMEM((2, 256, 256), F32),
            pltpu.VMEM((2, HALF, 256), F32),
        ],
        compiler_params=pltpu.CompilerParams(vmem_limit_bytes=48 << 20),
        name="slots",
    )(rows, cols, count, view, halo, probe, diffraction, *consts)


def shifted(block, axis, distance):
    devices = range(lax.axis_size(axis))
    route = [(i - distance, i) for i in devices if i - distance in devices]
    return lax.ppermute(block, axis, route)


def on_device(object_slab, probe, diffraction, positions, slot_counts):
    tile_rows, _, tile_cols = object_slab.shape
    side = probe.shape[2]
    blocks = tile_cols // HALF
    view = (
        object_slab.reshape(tile_rows, 2, blocks, HALF)
        .transpose(0, 2, 1, 3)
        .reshape(tile_rows * blocks * 2, HALF)
    )
    edge = side * blocks * 2
    rows = positions[:, 0] - lax.axis_index("region") * tile_rows
    cols = positions[:, 1]
    halo = shifted(view[:edge], "region", -1)
    part, spill, pgrad, cover = compute(rows, cols, slot_counts[0], view, halo, probe, diffraction)
    pgrad, cover = lax.psum((pgrad, cover), ("region", "group"))
    arrived = shifted(spill, "region", 1)
    part = jnp.concatenate([part[:edge] - arrived, part[edge:]], axis=0)
    obj = (
        part.reshape(tile_rows, blocks, 2, HALF)
        .transpose(0, 2, 1, 3)
        .reshape(tile_rows, 2, tile_cols)
    )
    prb = probe - pgrad / (cover + 1e-06)[None, None]
    return (obj, prb)


def solution(mesh):
    placed = (
        P("region", None, "group"),
        P(),
        P(("region", "group"), None, None),
        P(("region", "group"), None),
        P("group", "region"),
    )
    return jax.shard_map(
        on_device,
        mesh=mesh,
        in_specs=placed,
        out_specs=(P("region", None, "group"), P()),
        check_vma=False,
    )
```

```python
import functools
import math

import jax
import jax.numpy as jnp
import ml_dtypes
import numpy as np
from jax import lax
from jax.experimental import pallas as pl
from jax.experimental.pallas import tpu as pltpu
from jax.sharding import PartitionSpec as P

F32 = jnp.float32
BF16 = jnp.bfloat16
HALF = 128


def split_table(table):
    high = table.astype(np.float32).astype(ml_dtypes.bfloat16)
    low = (table - high.astype(np.float64)).astype(np.float32).astype(ml_dtypes.bfloat16)
    return high, low


def tables():
    n = np.arange(HALF)[:, None].astype(np.float64)
    k = np.arange(HALF)[None, :].astype(np.float64)
    out = {}
    for parity in (0, 1):
        angle = -2.0 * math.pi * ((n * (2 * k + parity)) % 256) / 256
        re, im = np.cos(angle) / 16, np.sin(angle) / 16
        full = np.block([[re, im], [-im, re]])
        high, low = split_table(full)
        out["r", parity] = np.concatenate([high, high, low], axis=0)
        out["rt", parity] = np.concatenate([high.T, high.T, low.T], axis=0)
        out["l", parity] = np.concatenate([high, high, low], axis=1)
        out["lt", parity] = np.concatenate([high.T, high.T, low.T], axis=1)
    perm = np.zeros((256, 256), np.float32)
    for c in range(256):
        perm[c, (c % 2) * HALF + c // 2] = 1
    perm = perm.astype(ml_dtypes.bfloat16)
    return (
        np.stack([out["r", 0], out["r", 1]]),
        np.stack([out["rt", 0], out["rt", 1]]),
        np.stack([out["l", 0], out["l", 1]]),
        np.stack([out["lt", 0], out["lt", 1]]),
        np.concatenate([perm, perm], axis=0),
    )


def parts_of(x):
    high = x.astype(BF16)
    low = (x - high.astype(F32)).astype(BF16)
    return high, low


def mul_right(x, table):
    high, low = parts_of(x)
    return jnp.dot(jnp.concatenate([high, low, high], axis=1), table, preferred_element_type=F32)


def mul_left(table, x):
    high, low = parts_of(x)
    return jnp.dot(table, jnp.concatenate([high, low, high], axis=0), preferred_element_type=F32)


def swap_blocks(a, b):
    return jnp.concatenate(
        [
            jnp.concatenate([a[:, :HALF], b[:, :HALF]], axis=1),
            jnp.concatenate([a[:, HALF:], b[:, HALF:]], axis=1),
        ],
        axis=0,
    )


def compute_kernel(
    rows_ref, cols_ref, count_ref, object_ref, halo_ref, probe_ref, diff_ref,
    r_ref, rt_ref, l_ref, lt_ref, perm_ref,
    part_ref, spill_ref, pgrad_ref, cover_ref,
    ext_ref, acc_ref, win_ref, far_ref, go_ref, factor_ref,
):
    modes = probe_ref.shape[0]
    own = object_ref.shape[0]
    ext_ref[:own] = object_ref[...]
    ext_ref[own:] = halo_ref[...]
    acc_ref[...] = jnp.zeros_like(acc_ref)
    pgrad_ref[...] = jnp.zeros_like(pgrad_ref)
    cover_ref[...] = jnp.zeros_like(cover_ref)

    total = jnp.zeros((256, 256), F32)
    for m in range(modes):
        total = total + probe_ref[m, 0] * probe_ref[m, 0] + probe_ref[m, 1] * probe_ref[m, 1]
    peak = jnp.max(total)

    lane = lax.broadcasted_iota(jnp.int32, (256, HALF), 1)

    def slot_body(s, carry):
        row, col = rows_ref[s], cols_ref[s]
        q, shift = col // HALF, lax.rem(col, HALF)

        def where_at(c, k):
            return pl.ds(row * 8 + jnp.minimum(q + k, 3) * 2 + c, 256, stride=8)

        back = lax.rem(HALF - shift, HALF)
        for c in (0, 1):
            t = [pltpu.roll(ext_ref[where_at(c, k), :], back, axis=1) for k in range(3)]
            for k in (0, 1):
                win_ref[c, :, k * HALF : (k + 1) * HALF] = jnp.where(lane < HALF - shift, t[k], t[k + 1])
        wr, wi = win_ref[0], win_ref[1]
        cover_ref[...] += wr * wr + wi * wi

        def forward(m, carry):
            pr, pi = probe_ref[m, 0], probe_ref[m, 1]
            wr, wi = win_ref[0], win_ref[1]
            er = pr * wr - pi * wi
            ei = pr * wi + pi * wr
            a = jnp.concatenate([er[:, :HALF] + er[:, HALF:], ei[:, :HALF] + ei[:, HALF:]], axis=1)
            b = jnp.concatenate([er[:, :HALF] - er[:, HALF:], ei[:, :HALF] - ei[:, HALF:]], axis=1)
            ye = mul_right(a, r_ref[0])
            yo = mul_right(b, r_ref[1])
            plus = swap_blocks(ye[:HALF] + ye[HALF:], yo[:HALF] + yo[HALF:])
            minus = swap_blocks(ye[:HALF] - ye[HALF:], yo[:HALF] - yo[HALF:])
            far_ref[m, 0] = mul_left(lt_ref[0], plus)
            far_ref[m, 1] = mul_left(lt_ref[1], minus)
            return carry

        lax.fori_loop(0, modes, forward, 0)

        for p in (0, 1):
            intensity = jnp.zeros((HALF, 256), F32)
            for m in range(modes):
                fr, fi = far_ref[m, p, :HALF], far_ref[m, p, HALF:]
                intensity = intensity + (fr * fr + fi * fi)
            wanted = jnp.sqrt(
                jnp.concatenate(
                    [
                        diff_ref[s, h, pl.ds(p, HALF, stride=2), :]
                        for h in (0, 1)
                    ],
                    axis=1,
                )
            )
            high, low = parts_of(wanted)
            wanted = jnp.dot(
                jnp.concatenate([high, low], axis=1), perm_ref[...], preferred_element_type=F32
            )
            factor_ref[p] = 1.0 - wanted / jnp.sqrt(jnp.maximum(intensity, 1.0))

        go_ref[...] = jnp.zeros_like(go_ref)

        def inverse(m, carry):
            ge = far_ref[m, 0] * jnp.concatenate([factor_ref[0], factor_ref[0]], axis=0)
            gd = far_ref[m, 1] * jnp.concatenate([factor_ref[1], factor_ref[1]], axis=0)
            e = mul_left(l_ref[0], ge)
            o = mul_left(l_ref[1], gd)
            top, bottom = e + o, e - o
            ae, ao = [
                jnp.concatenate(
                    [
                        jnp.concatenate([x[:HALF, at : at + HALF], x[HALF:, at : at + HALF]], axis=1)
                        for x in (top, bottom)
                    ],
                    axis=0,
                )
                for at in (0, HALF)
            ]
            e = mul_right(ae, rt_ref[0])
            o = mul_right(ao, rt_ref[1])
            left, right = e + o, e - o
            cr = jnp.concatenate([left[:, :HALF], right[:, :HALF]], axis=1)
            ci = jnp.concatenate([left[:, HALF:], right[:, HALF:]], axis=1)
            pr, pi = probe_ref[m, 0], probe_ref[m, 1]
            wr, wi = win_ref[0], win_ref[1]
            go_ref[0] += pr * cr + pi * ci
            go_ref[1] += pr * ci - pi * cr
            pgrad_ref[m, 0] += wr * cr + wi * ci
            pgrad_ref[m, 1] += wr * ci - wi * cr
            return carry

        lax.fori_loop(0, modes, inverse, 0)

        for c in (0, 1):
            g = [pltpu.roll(go_ref[c, :, k * HALF : (k + 1) * HALF], shift, axis=1) for k in (0, 1)]
            zero = jnp.zeros_like(g[0])
            for k, (here, wrapped) in enumerate(((g[0], zero), (g[1], g[0]), (zero, g[1]))):
                acc_ref[where_at(c, k), :] += jnp.where(lane >= shift, here, wrapped)
        return carry

    lax.fori_loop(0, count_ref[0], slot_body, 0)
    part_ref[...] = object_ref[...] - acc_ref[:own] / peak
    spill_ref[...] = acc_ref[own:] / peak


def compute(rows, cols, count, view, halo, probe, diffraction):
    modes = probe.shape[0]
    slots = diffraction.shape[0]
    consts = [jnp.asarray(t) for t in tables()]
    smem = pl.BlockSpec(memory_space=pltpu.SMEM)
    vmem = pl.BlockSpec(memory_space=pltpu.VMEM)
    diffraction = diffraction.reshape(slots, 256, 2, HALF).transpose(0, 2, 1, 3)
    return pl.pallas_call(
        compute_kernel,
        out_shape=(
            jax.ShapeDtypeStruct(view.shape, F32),
            jax.ShapeDtypeStruct(halo.shape, F32),
            jax.ShapeDtypeStruct(probe.shape, F32),
            jax.ShapeDtypeStruct((256, 256), F32),
        ),
        in_specs=[smem] * 3 + [vmem] * (4 + len(consts)),
        out_specs=[vmem] * 4,
        scratch_shapes=[
            pltpu.VMEM((view.shape[0] + halo.shape[0], HALF), F32),
            pltpu.VMEM((view.shape[0] + halo.shape[0], HALF), F32),
            pltpu.VMEM((2, 256, 256), F32),
            pltpu.VMEM((modes, 2, 256, 256), F32),
            pltpu.VMEM((2, 256, 256), F32),
            pltpu.VMEM((2, HALF, 256), F32),
        ],
        compiler_params=pltpu.CompilerParams(vmem_limit_bytes=48 << 20),
        name="slots",
    )(rows, cols, count, view, halo, probe, diffraction, *consts)


MESH = pl.DeviceIdType.MESH
ORDERS = (("x", "y", "z"), ("y", "z", "x"), ("z", "x", "y"))


def place():
    region, group = lax.axis_index("region"), lax.axis_index("group")
    core = lax.rem(region, 2)
    z = lax.rem(region // 2, 4)
    y = (group // 4) * 2 + region // 8
    x = lax.rem(group, 4)
    return {"x": x, "y": y, "z": z}, core


def device(at, core):
    region = (lax.rem(at["y"], 2) * 4 + at["z"]) * 2 + core
    return (region, (at["y"] // 2) * 4 + at["x"])


def index(fixed):
    return tuple(fixed.get(axis, slice(None)) for axis in ("x", "y", "z"))


def reduce_kernel(
    pgrad_ref, cover_ref, probe_ref, spill_ref,
    new_ref, arrived_ref,
    mate_ref, sum_ref, got1, got2, got3, sum1, sum2, send_sem, recv_sem,
):
    me, core = place()
    regions = lax.axis_size("region")
    region, group = lax.axis_index("region"), lax.axis_index("group")
    mate = device(me, 1 - core)
    up = (lax.rem(region + 1, regions), group)
    down = (lax.rem(region + regions - 1, regions), group)

    def along(axis, distance):
        return {**me, axis: lax.rem(me[axis] + distance, 4)}

    barrier = pltpu.get_barrier_semaphore()
    partners = [mate, up, down]
    partners += [device(along(axis, d), core) for axis in ("x", "y", "z") for d in (1, 2, 3)]
    for partner in partners:
        pl.semaphore_signal(barrier, inc=1, device_id=partner, device_id_type=MESH)
    pl.semaphore_wait(barrier, len(partners))

    started = []

    def send(src, dst, to):
        n = len(started)
        copy = pltpu.make_async_remote_copy(
            src_ref=src, dst_ref=dst, send_sem=send_sem.at[n], recv_sem=recv_sem.at[n],
            device_id=to, device_id_type=MESH,
        )
        copy.start()
        started.append(copy)
        return copy

    planes = ((0, 2), (2, 4), (4, 5))
    mine, theirs = 4 * core, 4 * (1 - core)
    first = []
    for p, (lo, hi) in enumerate(planes):
        src = cover_ref if p == 2 else pgrad_ref.at[pl.ds(theirs + lo, hi - lo)]
        first.append(send(src, mate_ref.at[lo:hi], mate))
    spilled = send(spill_ref, arrived_ref, up)

    def exchange(p, axis, source, target):
        copies = []
        for d in (1, 2, 3):
            to = along(axis, d)
            copies.append(send(source(to[axis]), target.at[d - 1], device(to, core)))
        return copies

    copies = []
    for p, (lo, hi) in enumerate(planes):
        first[p].wait_recv()
        own = cover_ref[...] if p == 2 else pgrad_ref[pl.ds(mine + lo, hi - lo)]
        sum_ref[lo:hi] = own + mate_ref[lo:hi]
        a = ORDERS[p][0]
        copies.append(
            exchange(p, a, lambda q: sum_ref.at[(slice(lo, hi), *index({a: q}))], got1.at[:, lo:hi])
        )
    later = []
    for p, (lo, hi) in enumerate(planes):
        a, b, _ = ORDERS[p]
        for copy in copies[p]:
            copy.wait_recv()
        sum1[lo:hi] = (
            sum_ref[(slice(lo, hi), *index({a: me[a]}))]
            + got1[0, lo:hi] + got1[1, lo:hi] + got1[2, lo:hi]
        )
        rest = [axis for axis in ("x", "y", "z") if axis != a]

        def part1(q, lo=lo, hi=hi, b=b, rest=rest):
            return (slice(lo, hi), *(q if axis == b else slice(None) for axis in rest))

        later.append((part1, exchange(p, b, lambda q: sum1.at[part1(q)], got2.at[:, lo:hi])))
    last = []
    for p, (lo, hi) in enumerate(planes):
        _, b, c = ORDERS[p]
        part1, arriving = later[p]
        for copy in arriving:
            copy.wait_recv()
        sum2[lo:hi] = sum1[part1(me[b])] + got2[0, lo:hi] + got2[1, lo:hi] + got2[2, lo:hi]
        last.append(exchange(p, c, lambda q: sum2.at[lo:hi, q], got3.at[:, lo:hi]))
    reduced = {}
    for p in (2, 0, 1):
        lo, hi = planes[p]
        c = ORDERS[p][2]
        for copy in last[p]:
            copy.wait_recv()
        reduced[p] = sum2[lo:hi, me[c]] + got3[0, lo:hi] + got3[1, lo:hi] + got3[2, lo:hi]
    here = index(me)
    steps = []
    for p in (0, 1):
        at = pl.ds(mine + 2 * p, 2)
        new_ref[(at, *here)] = probe_ref[(at, *here)] - reduced[p] / (reduced[2] + 1e-06)

    def spread(p, axis, fixed):
        at = (pl.ds(mine + 2 * p, 2), *index({f: me[f] for f in fixed}))
        return [
            send(new_ref.at[at], new_ref.at[at], device(along(axis, d), core)) for d in (1, 2, 3)
        ]

    copies = [spread(p, ORDERS[p][2], ORDERS[p]) for p in (0, 1)]
    for level in (1, 0):
        following = []
        for p in (0, 1):
            for copy in copies[p]:
                copy.wait_recv()
            following.append(spread(p, ORDERS[p][level], ORDERS[p][: level + 1]))
        copies = following
    final = []
    for p in (0, 1):
        a = ORDERS[p][0]
        planes_at = pl.ds(mine + 2 * p, 2)
        at = (planes_at, *index({a: me[a]}))
        final.append(send(new_ref.at[at], new_ref.at[at], mate))
    for d in (1, 2, 3):
        for p in (0, 1):
            a = ORDERS[p][0]
            copies[p][d - 1].wait_recv()
            at = (pl.ds(mine + 2 * p, 2), *index({a: lax.rem(me[a] + 4 - d, 4)}))
            final.append(send(new_ref.at[at], new_ref.at[at], mate))
    for copy in final:
        copy.wait_recv()
    spilled.wait_recv()
    for copy in started:
        copy.wait_send()


def tiled(planes):
    return (
        planes.reshape(-1, 32, 8, 2, HALF).transpose(0, 1, 3, 2, 4).reshape(-1, 4, 4, 4, 8, HALF)
    )


def untiled(tiles, shape):
    return tiles.reshape(-1, 32, 2, 8, HALF).transpose(0, 1, 3, 2, 4).reshape(shape)


def reduce(pgrad, cover, probe, spill):
    vmem = pl.BlockSpec(memory_space=pltpu.VMEM)
    count = 3 + 1 + 27 + 18 + 8
    new, arrived = pl.pallas_call(
        reduce_kernel,
        out_shape=(
            jax.ShapeDtypeStruct((8, 4, 4, 4, 8, HALF), F32),
            jax.ShapeDtypeStruct(spill.shape, F32),
        ),
        in_specs=[vmem] * 4,
        out_specs=[vmem] * 2,
        scratch_shapes=[
            pltpu.VMEM((5, 4, 4, 4, 8, HALF), F32),
            pltpu.VMEM((5, 4, 4, 4, 8, HALF), F32),
            pltpu.VMEM((3, 5, 4, 4, 8, HALF), F32),
            pltpu.VMEM((3, 5, 4, 8, HALF), F32),
            pltpu.VMEM((3, 5, 8, HALF), F32),
            pltpu.VMEM((5, 4, 4, 8, HALF), F32),
            pltpu.VMEM((5, 4, 8, HALF), F32),
            pltpu.SemaphoreType.DMA((count,)),
            pltpu.SemaphoreType.DMA((count,)),
        ],
        compiler_params=pltpu.CompilerParams(
            vmem_limit_bytes=40 << 20, collective_id=0, has_side_effects=True
        ),
        name="reduce",
    )(tiled(pgrad), tiled(cover), tiled(probe), spill)
    return untiled(new, probe.shape), arrived


def shifted(block, axis, distance):
    devices = range(lax.axis_size(axis))
    route = [(i - distance, i) for i in devices if i - distance in devices]
    return lax.ppermute(block, axis, route)


def on_device(object_slab, probe, diffraction, positions, slot_counts):
    tile_rows, _, tile_cols = object_slab.shape
    side = probe.shape[2]
    blocks = tile_cols // HALF
    view = (
        object_slab.reshape(tile_rows, 2, blocks, HALF)
        .transpose(0, 2, 1, 3)
        .reshape(tile_rows * blocks * 2, HALF)
    )
    edge = side * blocks * 2
    rows = positions[:, 0] - lax.axis_index("region") * tile_rows
    cols = positions[:, 1]
    halo = shifted(view[:edge], "region", -1)
    part, spill, pgrad, cover = compute(rows, cols, slot_counts[0], view, halo, probe, diffraction)
    prb, arrived = reduce(pgrad, cover, probe, spill)
    part = jnp.concatenate([part[:edge] - arrived, part[edge:]], axis=0)
    obj = (
        part.reshape(tile_rows, blocks, 2, HALF)
        .transpose(0, 2, 1, 3)
        .reshape(tile_rows, 2, tile_cols)
    )
    return (obj, prb)


def solution(mesh):
    placed = (
        P("region", None, "group"),
        P(),
        P(("region", "group"), None, None),
        P(("region", "group"), None),
        P("group", "region"),
    )
    return jax.shard_map(
        on_device,
        mesh=mesh,
        in_specs=placed,
        out_specs=(P("region", None, "group"), P()),
        check_vma=False,
    )
```

```python
import math

import jax
import jax.numpy as jnp
import ml_dtypes
import numpy as np
from jax import lax
from jax.experimental import pallas as pl
from jax.experimental.pallas import tpu as pltpu
from jax.sharding import PartitionSpec as P

F32 = jnp.float32
BF16 = jnp.bfloat16
HALF = 128
SLOTS = 4
MODES = 4
PAD = 64
MESH = pl.DeviceIdType.MESH
AXES = ("x", "y", "z")
ORDERS = (("x", "y", "z"), ("y", "z", "x"), ("x", "y", "z"), ("y", "z", "x"), ("z", "x", "y"))
DIMS = {"x": (4,), "y": (4,), "z": (2, 2)}


def split_table(table):
    high = table.astype(np.float32).astype(ml_dtypes.bfloat16)
    low = (table - high.astype(np.float64)).astype(np.float32).astype(ml_dtypes.bfloat16)
    return high, low


def tables():
    n = np.arange(HALF)[:, None].astype(np.float64)
    k = np.arange(HALF)[None, :].astype(np.float64)
    direct, turned = [], []
    for parity in (0, 1):
        angle = -2.0 * math.pi * ((n * (2 * k + parity)) % 256) / 256
        re, im = np.cos(angle) / 16, np.sin(angle) / 16
        high, low = split_table(np.block([[re, im], [-im, re]]))
        direct.append(np.stack([high, low]))
        turned.append(np.stack([high.T, low.T]))
    perm = np.zeros((256, 256), np.float32)
    for c in range(256):
        perm[c, (c % 2) * HALF + c // 2] = 1
    return np.stack(direct), np.stack(turned), perm.astype(ml_dtypes.bfloat16)


def parts_of(x):
    high = x.astype(BF16)
    low = (x - high.astype(F32)).astype(BF16)
    return high, low


def mul_right(x, table, p):
    high, low = parts_of(x)
    table = jnp.concatenate([table[p, 0], table[p, 0], table[p, 1]], axis=0)
    return jnp.dot(jnp.concatenate([high, low, high], axis=1), table, preferred_element_type=F32)


def mul_left(table, p, x):
    high, low = parts_of(x)
    table = jnp.concatenate([table[p, 0], table[p, 0], table[p, 1]], axis=1)
    return jnp.dot(table, jnp.concatenate([high, low, high], axis=0), preferred_element_type=F32)


def swap_blocks(a, b):
    return jnp.concatenate(
        [
            jnp.concatenate([a[:, :HALF], b[:, :HALF]], axis=1),
            jnp.concatenate([a[:, HALF:], b[:, HALF:]], axis=1),
        ],
        axis=0,
    )


def place():
    region, group = lax.axis_index("region"), lax.axis_index("group")
    core = lax.rem(region, 2)
    z = lax.rem(region // 2, 4)
    y = (group // 4) * 2 + region // 8
    x = lax.rem(group, 4)
    return {"x": x, "y": y, "z": z}, core


def device(at, core):
    region = (lax.rem(at["y"], 2) * 4 + at["z"]) * 2 + core
    return (region, (at["y"] // 2) * 4 + at["x"])


def dims(axes):
    return sum((DIMS[axis] for axis in AXES if axis in axes), ())


def tile(axes, fixed):
    out = ()
    for axis in AXES:
        if axis in axes and axis in fixed:
            q = fixed[axis]
            out += (q // 2, lax.rem(q, 2)) if axis == "z" else (q,)
        elif axis in axes:
            out += (slice(None),) * len(DIMS[axis])
    return out


def step_kernel(
    pos_ref, count_ref, object_hbm, probe_hbm, diff_hbm, direct_hbm, turned_hbm, perm_hbm,
    out_ref, new_ref,
    ext, win, far, wanted, probe, pgrad, cov, go, hx, strips, direct, turned, perm, diff,
    spill, arrived, mate, total, *rest,
):
    got, part = rest[:15], rest[15:25]
    local_sem, send_sem, recv_sem = rest[25:]
    me, core = place()
    regions = lax.axis_size("region")
    region, group = lax.axis_index("region"), lax.axis_index("group")
    sibling = device(me, 1 - core)
    up = (lax.rem(region + 1, regions), group)
    down = (lax.rem(region + regions - 1, regions), group)
    own = object_hbm.shape[0]
    edge = spill.shape[0]

    loads = [
        pltpu.make_async_copy(src, dst, local_sem.at[n])
        for n, (src, dst) in enumerate(
            [
                (object_hbm, ext.at[:own]),
                (diff_hbm, diff),
                (perm_hbm, perm),
                (probe_hbm, probe),
                (direct_hbm, direct),
                (turned_hbm, turned),
            ]
        )
    ]
    for load in loads:
        load.start()

    def along(axis, distance):
        return {**me, axis: lax.rem(me[axis] + distance, 4)}

    barrier = pltpu.get_barrier_semaphore()
    partners = [sibling, up, down]
    partners += [device(along(axis, d), core) for axis in AXES for d in (1, 2, 3)]
    for partner in partners:
        pl.semaphore_signal(barrier, inc=1, device_id=partner, device_id_type=MESH)
    pl.semaphore_wait(barrier, len(partners))

    builders = {}

    def remote(key, build=None):
        if build is not None:
            builders[key] = (len(builders), build)
        n, build = builders[key]
        src, dst, to = build()
        return pltpu.make_async_remote_copy(
            src_ref=src, dst_ref=dst, send_sem=send_sem.at[n], recv_sem=recv_sem.at[n],
            device_id=to, device_id_type=MESH,
        )

    def send(key, build):
        remote(key, build).start()

    def arrive(key):
        remote(key).wait_recv()

    send("halo", lambda: (object_hbm.at[:edge], ext.at[own:], down))

    def plane_of(u, c):
        return 4 * c + u

    def start_core(u):
        send(
            ("core", u),
            lambda: (cov if u == 4 else pgrad.at[plane_of(u, 1 - core)], mate.at[u], sibling),
        )

    def scatter(u, level, source, lead, axes):
        axis = ORDERS[u][level]

        def build(d):
            to = along(axis, d)
            src = source.at[(*lead, *tile(axes, {axis: to[axis]}))]
            return src, got[3 * u + level].at[d - 1], device(to, core)

        for d in (1, 2, 3):
            send(("rs", u, level, d), lambda d=d: build(d))

    def start_first(u):
        arrive(("core", u))
        total[u] = (cov[...] if u == 4 else pgrad[plane_of(u, core)]) + mate[u]
        scatter(u, 0, total, (u,), AXES)

    def gathered(u, level):
        axis = ORDERS[u][level]
        axes = [f for f in AXES if f not in ORDERS[u][:level]]
        for d in (1, 2, 3):
            arrive(("rs", u, level, d))
        source, lead = (total, (u,)) if level == 0 else (part[2 * u + level - 1], ())
        pieces = got[3 * u + level]
        return source[(*lead, *tile(axes, {axis: me[axis]}))] + pieces[0] + pieces[1] + pieces[2]

    def start_next(u, level):
        part[2 * u + level - 1][...] = gathered(u, level - 1)
        axes = [f for f in AXES if f not in ORDERS[u][:level]]
        scatter(u, level, part[2 * u + level - 1], (), axes)

    def renew(u, coverage):
        at = (plane_of(u, core), *tile(AXES, me))
        new_ref[at] = probe[at] - gathered(u, 2) / (coverage + 1e-06)

    def spread(u, level):
        axis = ORDERS[u][level]
        if level < 2:
            for d in (1, 2, 3):
                arrive(("ag", u, level + 1, d))

        def block():
            known = {f: me[f] for f in ORDERS[u][: level + 1]}
            return new_ref.at[(plane_of(u, core), *tile(AXES, known))]

        for d in (1, 2, 3):
            send(
                ("ag", u, level, d),
                lambda d=d: (block(), block(), device(along(axis, d), core)),
            )
        if level == 0:
            send(("back", u, 0), lambda: (block(), block(), sibling))

    def hand_over(u):
        axis = ORDERS[u][0]

        def block(d):
            known = {axis: lax.rem(me[axis] + 4 - d, 4)}
            return new_ref.at[(plane_of(u, core), *tile(AXES, known))]

        for d in (1, 2, 3):
            arrive(("ag", u, 0, d))
            send(("back", u, d), lambda d=d: (block(d), block(d), sibling))

    def tiles_of(x):
        return x.reshape(4, 4, 2, 8, HALF)

    pgrad[...] = jnp.zeros_like(pgrad)
    cov[...] = jnp.zeros_like(cov)
    go[...] = jnp.zeros_like(go)
    hx[:, :PAD] = jnp.zeros((SLOTS, PAD, 8, HALF), F32)
    hx[:, PAD + 256 :] = jnp.zeros((SLOTS, PAD, 8, HALF), F32)
    loads[1].wait()
    loads[2].wait()

    def prepare(s, carry):
        high, low = parts_of(jnp.sqrt(diff[s]))
        root = jnp.dot(high, perm[...], preferred_element_type=F32) + jnp.dot(
            low, perm[...], preferred_element_type=F32
        )
        for h in (0, 1):
            wanted[s, h] = root[:, h * HALF : (h + 1) * HALF]
        return carry

    lax.fori_loop(0, SLOTS, prepare, 0)

    loads[3].wait()

    def probe_at(m, c):
        return jnp.concatenate(
            [probe[2 * m + c, :, :, :, h].reshape(256, HALF) for h in (0, 1)], axis=1
        )

    power = jnp.zeros((256, 256), F32)
    for m in range(MODES):
        pr, pi = probe_at(m, 0), probe_at(m, 1)
        power = power + pr * pr + pi * pi
    peak = jnp.max(power)
    for load in (loads[0], loads[4], loads[5]):
        load.wait()
    arrive("halo")

    base = region * own

    def spot(s):
        return jnp.clip(pos_ref[s, 0] - base, 0, own - 1), pos_ref[s, 1]

    def pick_columns(col, shape, wide):
        at = lax.broadcasted_iota(jnp.int32, shape, wide)
        narrow = lax.broadcasted_iota(jnp.int32, shape, 1 - wide)
        return jnp.where(at - narrow == col, 1.0, 0.0).astype(BF16)

    def live(s, shape):
        return jnp.where(jnp.full(shape, s, jnp.int32) < count_ref[0, 0], 1.0, 0.0).astype(F32)

    def cut(s, carry):
        row, col = spot(s)
        strips[...] = ext[pl.ds(row, 256)].reshape(256 * 8, HALF)
        pick = pick_columns(col, (512, 256), 0)
        for c in (0, 1):
            strip = jnp.concatenate(
                [strips[pl.ds(2 * k + c, 256, stride=8), :] for k in range(4)], axis=1
            )
            high, low = parts_of(strip)
            win[s, c] = jnp.dot(high, pick, preferred_element_type=F32) + jnp.dot(
                low, pick, preferred_element_type=F32
            )
        wr, wi = win[s, 0], win[s, 1]
        power = live(s, (256, 256)) * (wr * wr + wi * wi)
        for h in (0, 1):
            cov[:, :, :, h] += tiles_of(power[:, h * HALF : (h + 1) * HALF])
        return carry

    lax.fori_loop(0, SLOTS, cut, 0)
    start_core(4)

    def forward(s, carry):
        @pl.when(s == 1)
        def _():
            start_first(4)

        @pl.when(s == 2)
        def _():
            start_next(4, 1)

        @pl.when(s == 3)
        def _():
            start_next(4, 2)

        wr, wi = win[s, 0], win[s, 1]
        for m in range(MODES):
            pr, pi = probe_at(m, 0), probe_at(m, 1)
            er = pr * wr - pi * wi
            ei = pr * wi + pi * wr
            a = jnp.concatenate([er[:, :HALF] + er[:, HALF:], ei[:, :HALF] + ei[:, HALF:]], axis=1)
            b = jnp.concatenate([er[:, :HALF] - er[:, HALF:], ei[:, :HALF] - ei[:, HALF:]], axis=1)
            ye = mul_right(a, direct, 0)
            yo = mul_right(b, direct, 1)
            plus = swap_blocks(ye[:HALF] + ye[HALF:], yo[:HALF] + yo[HALF:])
            minus = swap_blocks(ye[:HALF] - ye[HALF:], yo[:HALF] - yo[HALF:])
            far[s, m, 0] = mul_left(turned, 0, plus)
            far[s, m, 1] = mul_left(turned, 1, minus)
        for p in (0, 1):
            intensity = jnp.zeros((HALF, 256), F32)
            for m in range(MODES):
                fr, fi = far[s, m, p, :HALF], far[s, m, p, HALF:]
                intensity = intensity + (fr * fr + fi * fi)
            root = jnp.concatenate(
                [wanted[s, h, pl.ds(p, HALF, stride=2), :] for h in (0, 1)], axis=1
            )
            factor = live(s, (HALF, 256)) * (1.0 - root / jnp.sqrt(jnp.maximum(intensity, 1.0)))
            for m in range(MODES):
                far[s, m, p, :HALF] = far[s, m, p, :HALF] * factor
                far[s, m, p, HALF:] = far[s, m, p, HALF:] * factor
        return carry

    lax.fori_loop(0, SLOTS, forward, 0)

    def inverse(s, pair):
        wr, wi = win[s, 0], win[s, 1]
        for m in pair:
            e = mul_left(direct, 0, far[s, m, 0])
            o = mul_left(direct, 1, far[s, m, 1])
            top, bottom = e + o, e - o
            ae, ao = [
                jnp.concatenate(
                    [
                        jnp.concatenate([x[:HALF, at : at + HALF], x[HALF:, at : at + HALF]], axis=1)
                        for x in (top, bottom)
                    ],
                    axis=0,
                )
                for at in (0, HALF)
            ]
            e = mul_right(ae, turned, 0)
            o = mul_right(ao, turned, 1)
            left, right = e + o, e - o
            cr = jnp.concatenate([left[:, :HALF], right[:, :HALF]], axis=1)
            ci = jnp.concatenate([left[:, HALF:], right[:, HALF:]], axis=1)
            pr, pi = probe_at(m, 0), probe_at(m, 1)
            go[s, 0] += pr * cr + pi * ci
            go[s, 1] += pr * ci - pi * cr
            for c, g in enumerate((wr * cr + wi * ci, wr * ci - wi * cr)):
                for h in (0, 1):
                    pgrad[2 * m + c, :, :, :, h] += tiles_of(g[:, h * HALF : (h + 1) * HALF])

    def first_pair(s, carry):
        inverse(s, (0, 2))
        return carry

    lax.fori_loop(0, SLOTS, first_pair, 0)
    start_core(0)
    start_core(1)
    coverage = gathered(4, 2)

    def second_pair(s, carry):
        @pl.when(s == 1)
        def _():
            start_first(0)
            start_first(1)

        @pl.when(s == 2)
        def _():
            start_next(0, 1)
            start_next(1, 1)

        @pl.when(s == 3)
        def _():
            start_next(0, 2)
            start_next(1, 2)

        inverse(s, (1, 3))
        return carry

    lax.fori_loop(0, SLOTS, second_pair, 0)
    start_core(2)
    start_core(3)
    for u in (0, 1):
        renew(u, coverage)
        spread(u, 2)

    def turn(s, carry):
        pick = pick_columns(spot(s)[1], (256, 512), 1)
        for c in (0, 1):
            high, low = parts_of(go[s, c])
            strip = jnp.dot(high, pick, preferred_element_type=F32) + jnp.dot(
                low, pick, preferred_element_type=F32
            )
            for k in range(4):
                strips[pl.ds(2 * k + c, 256, stride=8), :] = strip[:, k * HALF : (k + 1) * HALF]
        hx[s, PAD : PAD + 256] = strips[...].reshape(256, 8, HALF)
        return carry

    lax.fori_loop(0, SLOTS, turn, 0)

    def added(block):
        out = None
        for s in range(SLOTS):
            start = jnp.clip(block * PAD - spot(s)[0] + PAD, 0, PAD + 256)
            piece = hx[s, pl.ds(start, PAD)]
            out = piece if out is None else out + piece
        return out / peak

    blocks = own // PAD

    def below(i, carry):
        spill[pl.ds(i * PAD, PAD)] = added(blocks + i)
        return carry

    lax.fori_loop(0, edge // PAD, below, 0)
    send("spill", lambda: (spill, arrived, up))
    start_first(2)
    start_first(3)

    def within(i, carry):
        at = pl.ds(i * PAD, PAD)
        out_ref[at] = ext[at] - added(i)
        return carry

    lax.fori_loop(0, blocks, within, 0)
    for u in (0, 1):
        spread(u, 1)
    for u in (2, 3):
        start_next(u, 1)
    for u in (0, 1):
        spread(u, 0)
    for u in (2, 3):
        start_next(u, 2)
    for u in (2, 3):
        renew(u, coverage)
        spread(u, 2)
    for u in (0, 1):
        hand_over(u)
    for u in (2, 3):
        spread(u, 1)
    arrive("spill")

    def rest_of(i, carry):
        at = pl.ds(i * PAD, PAD)
        out_ref[at] = out_ref[at] - arrived[at]
        return carry

    lax.fori_loop(0, edge // PAD, rest_of, 0)
    for u in (2, 3):
        spread(u, 0)
    for u in (2, 3):
        hand_over(u)
    for u in range(4):
        for d in range(4):
            arrive(("back", u, d))
    for key in builders:
        remote(key).wait_send()


def tiled(planes):
    return (
        planes.reshape(-1, 32, 8, 2, HALF)
        .transpose(0, 1, 3, 2, 4)
        .reshape(-1, *dims(AXES), 8, HALF)
    )


def untiled(tiles, shape):
    return tiles.reshape(-1, 32, 2, 8, HALF).transpose(0, 1, 3, 2, 4).reshape(shape)


def step(positions, slot_counts, view, probe, diffraction):
    smem = pl.BlockSpec(memory_space=pltpu.SMEM)
    anywhere = pl.BlockSpec(memory_space=pl.ANY)
    vmem = pl.BlockSpec(memory_space=pltpu.VMEM)
    direct, turned, perm = (jnp.asarray(t) for t in tables())
    own = view.shape[0]
    edge = own // 2
    planes = dims(AXES) + (8, HALF)
    got, part = [], []
    for order in ORDERS:
        for level in range(3):
            left = dims([a for a in AXES if a not in order[: level + 1]]) + (8, HALF)
            got.append(pltpu.VMEM((3, *left), F32))
            if level < 2:
                part.append(pltpu.VMEM(left, F32))
    copies = 2 + 5 + 45 + 36 + 16
    return pl.pallas_call(
        step_kernel,
        out_shape=(
            jax.ShapeDtypeStruct(view.shape, F32),
            jax.ShapeDtypeStruct((8, *planes), F32),
        ),
        in_specs=[smem] * 2 + [anywhere] * 6,
        out_specs=[vmem] * 2,
        scratch_shapes=[
            pltpu.VMEM((own + edge, 8, HALF), F32),
            pltpu.VMEM((SLOTS, 2, 256, 256), F32),
            pltpu.VMEM((SLOTS, MODES, 2, 256, 256), F32),
            pltpu.VMEM((SLOTS, 2, 256, HALF), F32),
            pltpu.VMEM((8, *planes), F32),
            pltpu.VMEM((8, *planes), F32),
            pltpu.VMEM(planes, F32),
            pltpu.VMEM((SLOTS, 2, 256, 256), F32),
            pltpu.VMEM((SLOTS, 256 + 2 * PAD, 8, HALF), F32),
            pltpu.VMEM((256 * 8, HALF), F32),
            pltpu.VMEM(direct.shape, BF16),
            pltpu.VMEM(turned.shape, BF16),
            pltpu.VMEM(perm.shape, BF16),
            pltpu.VMEM(diffraction.shape, F32),
            pltpu.VMEM((edge, 8, HALF), F32),
            pltpu.VMEM((edge, 8, HALF), F32),
            pltpu.VMEM((5, *planes), F32),
            pltpu.VMEM((5, *planes), F32),
            *got,
            *part,
            pltpu.SemaphoreType.DMA((6,)),
            pltpu.SemaphoreType.DMA((copies,)),
            pltpu.SemaphoreType.DMA((copies,)),
        ],
        compiler_params=pltpu.CompilerParams(
            vmem_limit_bytes=60 << 20, collective_id=0, has_side_effects=True
        ),
        name="step",
    )(positions, slot_counts, view, tiled(probe), diffraction, direct, turned, perm)


def on_device(object_slab, probe, diffraction, positions, slot_counts):
    tile_rows, _, tile_cols = object_slab.shape
    blocks = tile_cols // HALF
    view = (
        object_slab.reshape(tile_rows, 2, blocks, HALF)
        .transpose(0, 2, 1, 3)
        .reshape(tile_rows, blocks * 2, HALF)
    )
    view, new = step(positions, slot_counts, view, probe, diffraction)
    obj = (
        view.reshape(tile_rows, blocks, 2, HALF)
        .transpose(0, 2, 1, 3)
        .reshape(tile_rows, 2, tile_cols)
    )
    return (obj, untiled(new, probe.shape))


def solution(mesh):
    placed = (
        P("region", None, "group"),
        P(),
        P(("region", "group"), None, None),
        P(("region", "group"), None),
        P("group", "region"),
    )
    return jax.shard_map(
        on_device,
        mesh=mesh,
        in_specs=placed,
        out_specs=(P("region", None, "group"), P()),
        check_vma=False,
    )
```

```python
import math

import jax
import jax.numpy as jnp
import ml_dtypes
import numpy as np
from jax import lax
from jax.experimental import pallas as pl
from jax.experimental.pallas import tpu as pltpu
from jax.sharding import PartitionSpec as P

F32 = jnp.float32
BF16 = jnp.bfloat16
HALF = 128
SLOTS = 4
MODES = 4
PAD = 64
MESH = pl.DeviceIdType.MESH
AXES = ("x", "y", "z")
ORDERS = (("x", "y", "z"), ("y", "z", "x"), ("x", "y", "z"), ("y", "z", "x"), ("z", "x", "y"))
DIMS = {"x": (4,), "y": (4,), "z": (2, 2)}


def split_table(table):
    high = table.astype(np.float32).astype(ml_dtypes.bfloat16)
    low = (table - high.astype(np.float64)).astype(np.float32).astype(ml_dtypes.bfloat16)
    return high, low


def tables():
    n = np.arange(HALF)[:, None].astype(np.float64)
    k = np.arange(HALF)[None, :].astype(np.float64)
    direct, turned = [], []
    for parity in (0, 1):
        angle = -2.0 * math.pi * ((n * (2 * k + parity)) % 256) / 256
        re, im = np.cos(angle) / 16, np.sin(angle) / 16
        high, low = split_table(np.block([[re, im], [-im, re]]))
        direct.append(np.stack([high, low]))
        turned.append(np.stack([high.T, low.T]))
    perm = np.zeros((256, 256), np.float32)
    for c in range(256):
        perm[c, (c % 2) * HALF + c // 2] = 1
    return np.stack(direct), np.stack(turned), perm.astype(ml_dtypes.bfloat16)


def parts_of(x):
    high = x.astype(BF16)
    low = (x - high.astype(F32)).astype(BF16)
    return high, low


def mul_right(x, table, p):
    high, low = parts_of(x)
    table = jnp.concatenate([table[p, 0], table[p, 0], table[p, 1]], axis=0)
    return jnp.dot(jnp.concatenate([high, low, high], axis=1), table, preferred_element_type=F32)


def mul_left(table, p, x):
    high, low = parts_of(x)
    table = jnp.concatenate([table[p, 0], table[p, 0], table[p, 1]], axis=1)
    return jnp.dot(table, jnp.concatenate([high, low, high], axis=0), preferred_element_type=F32)


def swap_blocks(a, b):
    return jnp.concatenate(
        [
            jnp.concatenate([a[:, :HALF], b[:, :HALF]], axis=1),
            jnp.concatenate([a[:, HALF:], b[:, HALF:]], axis=1),
        ],
        axis=0,
    )


def place():
    region, group = lax.axis_index("region"), lax.axis_index("group")
    core = lax.rem(region, 2)
    z = lax.rem(region // 2, 4)
    y = (group // 4) * 2 + region // 8
    x = lax.rem(group, 4)
    return {"x": x, "y": y, "z": z}, core


def device(at, core):
    region = (lax.rem(at["y"], 2) * 4 + at["z"]) * 2 + core
    return (region, (at["y"] // 2) * 4 + at["x"])


def dims(axes):
    return sum((DIMS[axis] for axis in AXES if axis in axes), ())


def tile(axes, fixed):
    out = ()
    for axis in AXES:
        if axis in axes and axis in fixed:
            q = fixed[axis]
            out += (q // 2, lax.rem(q, 2)) if axis == "z" else (q,)
        elif axis in axes:
            out += (slice(None),) * len(DIMS[axis])
    return out


def step_kernel(
    pos_ref, count_ref, object_hbm, probe_hbm, diff_hbm, direct_hbm, turned_hbm, perm_hbm,
    out_ref, arrived, new_ref,
    ext, win, far, wanted, probe, pgrad, cov, go, hx, strips, direct, turned, perm, diff,
    spill, mate, total, factor, covered, *rest,
):
    got, part = rest[:15], rest[15:25]
    local_sem, send_sem, recv_sem = rest[25:]
    me, core = place()
    regions = lax.axis_size("region")
    region, group = lax.axis_index("region"), lax.axis_index("group")
    sibling = device(me, 1 - core)
    up = (lax.rem(region + 1, regions), group)
    down = (lax.rem(region + regions - 1, regions), group)
    own = object_hbm.shape[0]
    edge = spill.shape[0]

    loads = [
        pltpu.make_async_copy(src, dst, local_sem.at[n])
        for n, (src, dst) in enumerate(
            [
                (object_hbm, ext.at[:own]),
                (diff_hbm, diff),
                (perm_hbm, perm),
                (probe_hbm, probe),
                (direct_hbm, direct),
                (turned_hbm, turned),
            ]
        )
    ]
    def along(axis, distance):
        return {**me, axis: lax.rem(me[axis] + distance, 4)}

    barrier = pltpu.get_barrier_semaphore()
    partners = [sibling, up, down]
    partners += [device(along(axis, d), core) for axis in AXES for d in (1, 2, 3)]
    for partner in partners:
        pl.semaphore_signal(barrier, inc=1, device_id=partner, device_id_type=MESH)
    for load in loads:
        load.start()
    pl.semaphore_wait(barrier, len(partners))

    builders = {}

    def remote(key, build=None):
        if build is not None:
            builders[key] = (len(builders), build)
        n, build = builders[key]
        src, dst, to = build()
        return pltpu.make_async_remote_copy(
            src_ref=src, dst_ref=dst, send_sem=send_sem.at[n], recv_sem=recv_sem.at[n],
            device_id=to, device_id_type=MESH,
        )

    def send(key, build):
        remote(key, build).start()

    def arrive(key):
        remote(key).wait_recv()

    send("halo", lambda: (object_hbm.at[:edge], ext.at[own:], down))

    def plane_of(u, c):
        return 4 * c + u

    def start_core(u):
        send(
            ("core", u),
            lambda: (cov if u == 4 else pgrad.at[plane_of(u, 1 - core)], mate.at[u], sibling),
        )

    def scatter(u, level, source, lead, axes):
        axis = ORDERS[u][level]

        def build(d):
            to = along(axis, d)
            if level == 2:
                return source, got[3 * u + 2].at[me[axis]], device(to, core)
            src = source.at[(*lead, *tile(axes, {axis: to[axis]}))]
            return src, got[3 * u + level].at[d - 1], device(to, core)

        for d in (1, 2, 3):
            send(("rs", u, level, d), lambda d=d: build(d))

    def start_first(u):
        arrive(("core", u))
        total[u] = (cov[...] if u == 4 else pgrad[plane_of(u, core)]) + mate[u]
        scatter(u, 0, total, (u,), AXES)

    def gathered(u, level):
        axis = ORDERS[u][level]
        axes = [f for f in AXES if f not in ORDERS[u][:level]]
        for d in (1, 2, 3):
            arrive(("rs", u, level, d))
        source, lead = (total, (u,)) if level == 0 else (part[2 * u + level - 1], ())
        pieces = got[3 * u + level]
        return source[(*lead, *tile(axes, {axis: me[axis]}))] + pieces[0] + pieces[1] + pieces[2]

    def start_next(u, level):
        part[2 * u + level - 1][...] = gathered(u, level - 1)
        axes = [f for f in AXES if f not in ORDERS[u][:level]]
        scatter(u, level, part[2 * u + level - 1], (), axes)

    def finish(u):
        axis = ORDERS[u][2]
        pieces = got[3 * u + 2]
        pieces[me[axis]] = part[2 * u + 1][...]
        for d in (1, 2, 3):
            arrive(("rs", u, 2, d))
        reduced = (pieces[0] + pieces[1]) + (pieces[2] + pieces[3])
        at = tile(AXES, {f: me[f] for f in ORDERS[u][:2]})
        if u == 4:
            covered[at] = reduced
        else:
            here = (plane_of(u, core), *at)
            new_ref[here] = probe[here] - reduced / (covered[at] + 1e-06)

    def spread(u, level):
        axis = ORDERS[u][level]
        if level < 1:
            for d in (1, 2, 3):
                arrive(("ag", u, level + 1, d))

        def block():
            at = tile(AXES, {f: me[f] for f in ORDERS[u][: level + 1]})
            return covered.at[at] if u == 4 else new_ref.at[(plane_of(u, core), *at)]

        for d in (1, 2, 3):
            send(
                ("ag", u, level, d),
                lambda d=d: (block(), block(), device(along(axis, d), core)),
            )
        if level == 0 and u < 4:
            send(("back", u, 0), lambda: (block(), block(), sibling))

    def hand_over(u):
        axis = ORDERS[u][0]

        def block(d):
            known = {axis: lax.rem(me[axis] + 4 - d, 4)}
            return new_ref.at[(plane_of(u, core), *tile(AXES, known))]

        for d in (1, 2, 3):
            arrive(("ag", u, 0, d))
            send(("back", u, d), lambda d=d: (block(d), block(d), sibling))

    def tiles_of(x):
        return x.reshape(4, 4, 2, 8, HALF)

    pgrad[...] = jnp.zeros_like(pgrad)
    cov[...] = jnp.zeros_like(cov)
    go[...] = jnp.zeros_like(go)
    hx[:, :PAD] = jnp.zeros((SLOTS, PAD, 8, HALF), F32)
    hx[:, PAD + 256 :] = jnp.zeros((SLOTS, PAD, 8, HALF), F32)
    loads[1].wait()
    loads[2].wait()

    def prepare(s, carry):
        high, low = parts_of(jnp.sqrt(diff[s]))
        root = jnp.dot(high, perm[...], preferred_element_type=F32) + jnp.dot(
            low, perm[...], preferred_element_type=F32
        )
        for h in (0, 1):
            wanted[s, h] = root[:, h * HALF : (h + 1) * HALF]
        return carry

    lax.fori_loop(0, SLOTS, prepare, 0)

    loads[3].wait()

    def probe_at(m, c):
        return jnp.concatenate(
            [probe[2 * m + c, :, :, :, h].reshape(256, HALF) for h in (0, 1)], axis=1
        )

    power = jnp.zeros((256, 256), F32)
    for m in range(MODES):
        pr, pi = probe_at(m, 0), probe_at(m, 1)
        power = power + pr * pr + pi * pi
    peak = jnp.max(power)
    for load in (loads[0], loads[4], loads[5]):
        load.wait()
    arrive("halo")

    base = region * own

    def spot(s):
        return jnp.clip(pos_ref[0, s] - base, 0, own - 1), pos_ref[1, s]

    def pick_columns(col, shape, wide):
        at = lax.broadcasted_iota(jnp.int32, shape, wide)
        narrow = lax.broadcasted_iota(jnp.int32, shape, 1 - wide)
        return jnp.where(at - narrow == col, 1.0, 0.0).astype(BF16)

    def live(s, shape):
        return jnp.where(jnp.full(shape, s, jnp.int32) < count_ref[0, 0], 1.0, 0.0).astype(F32)

    def cut(s, carry):
        row, col = spot(s)
        strips[...] = ext[pl.ds(row, 256)].reshape(256 * 8, HALF)
        pick = pick_columns(col, (512, 256), 0)
        for c in (0, 1):
            strip = jnp.concatenate(
                [strips[pl.ds(2 * k + c, 256, stride=8), :] for k in range(4)], axis=1
            )
            high, low = parts_of(strip)
            win[s, c] = jnp.dot(high, pick, preferred_element_type=F32) + jnp.dot(
                low, pick, preferred_element_type=F32
            )
        wr, wi = win[s, 0], win[s, 1]
        power = live(s, (256, 256)) * (wr * wr + wi * wi)
        for h in (0, 1):
            cov[:, :, :, h] += tiles_of(power[:, h * HALF : (h + 1) * HALF])
        return carry

    lax.fori_loop(0, SLOTS, cut, 0)
    start_core(4)

    def forward(s, carry):
        @pl.when(s == 1)
        def _():
            start_first(4)

        @pl.when(s == 2)
        def _():
            start_next(4, 1)

        @pl.when(s == 3)
        def _():
            start_next(4, 2)

        wr, wi = win[s, 0], win[s, 1]
        for m in range(MODES):
            pr, pi = probe_at(m, 0), probe_at(m, 1)
            er = pr * wr - pi * wi
            ei = pr * wi + pi * wr
            a = jnp.concatenate([er[:, :HALF] + er[:, HALF:], ei[:, :HALF] + ei[:, HALF:]], axis=1)
            b = jnp.concatenate([er[:, :HALF] - er[:, HALF:], ei[:, :HALF] - ei[:, HALF:]], axis=1)
            ye = mul_right(a, direct, 0)
            yo = mul_right(b, direct, 1)
            plus = swap_blocks(ye[:HALF] + ye[HALF:], yo[:HALF] + yo[HALF:])
            minus = swap_blocks(ye[:HALF] - ye[HALF:], yo[:HALF] - yo[HALF:])
            far[s, m, 0] = mul_left(turned, 0, plus)
            far[s, m, 1] = mul_left(turned, 1, minus)
        for p in (0, 1):
            intensity = jnp.zeros((HALF, 256), F32)
            for m in range(MODES):
                fr, fi = far[s, m, p, :HALF], far[s, m, p, HALF:]
                intensity = intensity + (fr * fr + fi * fi)
            root = jnp.concatenate(
                [wanted[s, h, pl.ds(p, HALF, stride=2), :] for h in (0, 1)], axis=1
            )
            factor[s, p] = live(s, (HALF, 256)) * (
                1.0 - root / jnp.sqrt(jnp.maximum(intensity, 1.0))
            )
        return carry

    lax.fori_loop(0, SLOTS, forward, 0)

    def inverse(s, pair):
        wr, wi = win[s, 0], win[s, 1]
        for m in pair:
            e, o = [
                mul_left(
                    direct,
                    p,
                    far[s, m, p] * jnp.concatenate([factor[s, p], factor[s, p]], axis=0),
                )
                for p in (0, 1)
            ]
            top, bottom = e + o, e - o
            ae, ao = [
                jnp.concatenate(
                    [
                        jnp.concatenate([x[:HALF, at : at + HALF], x[HALF:, at : at + HALF]], axis=1)
                        for x in (top, bottom)
                    ],
                    axis=0,
                )
                for at in (0, HALF)
            ]
            e = mul_right(ae, turned, 0)
            o = mul_right(ao, turned, 1)
            left, right = e + o, e - o
            cr = jnp.concatenate([left[:, :HALF], right[:, :HALF]], axis=1)
            ci = jnp.concatenate([left[:, HALF:], right[:, HALF:]], axis=1)
            pr, pi = probe_at(m, 0), probe_at(m, 1)
            go[s, 0] += pr * cr + pi * ci
            go[s, 1] += pr * ci - pi * cr
            for c, g in enumerate((wr * cr + wi * ci, wr * ci - wi * cr)):
                for h in (0, 1):
                    pgrad[2 * m + c, :, :, :, h] += tiles_of(g[:, h * HALF : (h + 1) * HALF])

    def first_pair(s, carry):
        @pl.when(s == 0)
        def _():
            finish(4)
            spread(4, 1)

        @pl.when(s == 2)
        def _():
            spread(4, 0)

        inverse(s, (0, 2))
        return carry

    lax.fori_loop(0, SLOTS, first_pair, 0)
    start_core(0)
    start_core(1)

    def second_pair(s, carry):
        @pl.when(s == 3)
        def _():
            start_first(0)
            start_first(1)

        inverse(s, (1, 3))
        return carry

    lax.fori_loop(0, SLOTS, second_pair, 0)
    start_core(2)
    start_core(3)

    def turn(s, carry):
        pick = pick_columns(spot(s)[1], (256, 512), 1)
        for c in (0, 1):
            high, low = parts_of(go[s, c])
            strip = jnp.dot(high, pick, preferred_element_type=F32) + jnp.dot(
                low, pick, preferred_element_type=F32
            )
            for k in range(4):
                strips[pl.ds(2 * k + c, 256, stride=8), :] = strip[:, k * HALF : (k + 1) * HALF]
        hx[s, PAD : PAD + 256] = strips[...].reshape(256, 8, HALF)
        return carry

    lax.fori_loop(0, SLOTS, turn, 0)
    for u in (2, 3):
        start_first(u)
    for u in (0, 1):
        start_next(u, 1)

    def added(block):
        out = None
        for s in range(SLOTS):
            start = jnp.clip(block * PAD - spot(s)[0] + PAD, 0, PAD + 256)
            piece = hx[s, pl.ds(start, PAD)]
            out = piece if out is None else out + piece
        return out / peak

    blocks = own // PAD

    def below(i, carry):
        spill[pl.ds(i * PAD, PAD)] = added(blocks + i)
        return carry

    lax.fori_loop(0, edge // PAD, below, 0)
    send("spill", lambda: (spill, arrived, up))
    for u in (0, 1):
        start_next(u, 2)
    for u in (2, 3):
        start_next(u, 1)

    def within(i, carry):
        at = pl.ds(i * PAD, PAD)
        out_ref[at] = ext[at] - added(i)
        return carry

    lax.fori_loop(0, blocks, within, 0)
    for d in (1, 2, 3):
        arrive(("ag", 4, 0, d))
    for u in (0, 1):
        finish(u)
        spread(u, 1)
    for u in (2, 3):
        start_next(u, 2)
    for u in (0, 1):
        spread(u, 0)
    for u in (2, 3):
        finish(u)
        spread(u, 1)
    for u in (0, 1):
        hand_over(u)
    for u in (2, 3):
        spread(u, 0)
    arrive("spill")
    for u in (2, 3):
        hand_over(u)
    for u in range(4):
        for d in range(4):
            arrive(("back", u, d))
    for key in builders:
        remote(key).wait_send()


def tiled(planes):
    return (
        planes.reshape(-1, 32, 8, 2, HALF)
        .transpose(0, 1, 3, 2, 4)
        .reshape(-1, *dims(AXES), 8, HALF)
    )


def untiled(tiles, shape):
    return tiles.reshape(-1, 32, 2, 8, HALF).transpose(0, 1, 3, 2, 4).reshape(shape)


def step(positions, slot_counts, view, probe, diffraction):
    smem = pl.BlockSpec(memory_space=pltpu.SMEM)
    anywhere = pl.BlockSpec(memory_space=pl.ANY)
    vmem = pl.BlockSpec(memory_space=pltpu.VMEM)
    direct, turned, perm = (jnp.asarray(t) for t in tables())
    own = view.shape[0]
    edge = own // 2
    planes = dims(AXES) + (8, HALF)
    got, part = [], []
    for order in ORDERS:
        for level in range(3):
            left = dims([a for a in AXES if a not in order[: level + 1]]) + (8, HALF)
            if level < 2:
                got.append(pltpu.VMEM((3, *left), F32))
                part.append(pltpu.VMEM(left, F32))
            else:
                got.append(pltpu.VMEM((4, *part[-1].shape), F32))
    copies = 2 + 5 + 45 + 30 + 16
    return pl.pallas_call(
        step_kernel,
        out_shape=(
            jax.ShapeDtypeStruct(view.shape, F32),
            jax.ShapeDtypeStruct((edge, 8, HALF), F32),
            jax.ShapeDtypeStruct((8, *planes), F32),
        ),
        in_specs=[smem] * 2 + [anywhere] * 6,
        out_specs=[vmem] * 3,
        scratch_shapes=[
            pltpu.VMEM((own + edge, 8, HALF), F32),
            pltpu.VMEM((SLOTS, 2, 256, 256), F32),
            pltpu.VMEM((SLOTS, MODES, 2, 256, 256), F32),
            pltpu.VMEM((SLOTS, 2, 256, HALF), F32),
            pltpu.VMEM((8, *planes), F32),
            pltpu.VMEM((8, *planes), F32),
            pltpu.VMEM(planes, F32),
            pltpu.VMEM((SLOTS, 2, 256, 256), F32),
            pltpu.VMEM((SLOTS, 256 + 2 * PAD, 8, HALF), F32),
            pltpu.VMEM((256 * 8, HALF), F32),
            pltpu.VMEM(direct.shape, BF16),
            pltpu.VMEM(turned.shape, BF16),
            pltpu.VMEM(perm.shape, BF16),
            pltpu.VMEM(diffraction.shape, F32),
            pltpu.VMEM((edge, 8, HALF), F32),
            pltpu.VMEM((5, *planes), F32),
            pltpu.VMEM((5, *planes), F32),
            pltpu.VMEM((SLOTS, 2, HALF, 256), F32),
            pltpu.VMEM(planes, F32),
            *got,
            *part,
            pltpu.SemaphoreType.DMA((6,)),
            pltpu.SemaphoreType.DMA((copies,)),
            pltpu.SemaphoreType.DMA((copies,)),
        ],
        compiler_params=pltpu.CompilerParams(
            vmem_limit_bytes=46 << 20, collective_id=0, has_side_effects=True
        ),
        name="step",
    )(positions, slot_counts, view, tiled(probe), diffraction, direct, turned, perm)


def on_device(object_slab, probe, diffraction, positions, slot_counts):
    tile_rows, _, tile_cols = object_slab.shape
    blocks = tile_cols // HALF
    view = (
        object_slab.reshape(tile_rows, 2, blocks, HALF)
        .transpose(0, 2, 1, 3)
        .reshape(tile_rows, blocks * 2, HALF)
    )
    view, arrived, new = step(positions.T, slot_counts, view, probe, diffraction)
    edge = arrived.shape[0]
    view = jnp.concatenate([view[:edge] - arrived, view[edge:]], axis=0)
    obj = (
        view.reshape(tile_rows, blocks, 2, HALF)
        .transpose(0, 2, 1, 3)
        .reshape(tile_rows, 2, tile_cols)
    )
    return (obj, untiled(new, probe.shape))


def solution(mesh):
    placed = (
        P("region", None, "group"),
        P(),
        P(("region", "group"), None, None),
        P(("region", "group"), None),
        P("group", "region"),
    )
    return jax.shard_map(
        on_device,
        mesh=mesh,
        in_specs=placed,
        out_specs=(P("region", None, "group"), P()),
        check_vma=False,
    )
```

```python
import math

import jax
import jax.numpy as jnp
import ml_dtypes
import numpy as np
from jax import lax
from jax.experimental import pallas as pl
from jax.experimental.pallas import tpu as pltpu
from jax.sharding import PartitionSpec as P

F32 = jnp.float32
BF16 = jnp.bfloat16
HALF = 128
SLOTS = 4
MODES = 4
PAD = 64
MESH = pl.DeviceIdType.MESH
PLANE = (4, 4, 2, 2, 8, HALF)
COVERAGE = MODES
OTHERS = tuple((i, j) for i in range(4) for j in range(4) if (i, j) != (0, 0))


def split_table(table):
    high = table.astype(np.float32).astype(ml_dtypes.bfloat16)
    low = (table - high.astype(np.float64)).astype(np.float32).astype(ml_dtypes.bfloat16)
    return high, low


def tables():
    n = np.arange(HALF)[:, None].astype(np.float64)
    k = np.arange(HALF)[None, :].astype(np.float64)
    direct, turned = [], []
    for parity in (0, 1):
        angle = -2.0 * math.pi * ((n * (2 * k + parity)) % 256) / 256
        re, im = np.cos(angle) / 16, np.sin(angle) / 16
        high, low = split_table(np.block([[re, im], [-im, re]]))
        direct.append(np.stack([high, low]))
        turned.append(np.stack([high.T, low.T]))
    perm = np.zeros((256, 256), np.float32)
    for c in range(256):
        perm[c, (c % 2) * HALF + c // 2] = 1
    return np.stack(direct), np.stack(turned), perm.astype(ml_dtypes.bfloat16)


def parts_of(x):
    high = x.astype(BF16)
    low = (x - high.astype(F32)).astype(BF16)
    return high, low


def mul_right(x, table, p):
    high, low = parts_of(x)
    table = jnp.concatenate([table[p, 0], table[p, 0], table[p, 1]], axis=0)
    return jnp.dot(jnp.concatenate([high, low, high], axis=1), table, preferred_element_type=F32)


def mul_left(table, p, x):
    high, low = parts_of(x)
    table = jnp.concatenate([table[p, 0], table[p, 0], table[p, 1]], axis=1)
    return jnp.dot(table, jnp.concatenate([high, low, high], axis=0), preferred_element_type=F32)


def swap_blocks(a, b):
    return jnp.concatenate(
        [
            jnp.concatenate([a[:, :HALF], b[:, :HALF]], axis=1),
            jnp.concatenate([a[:, HALF:], b[:, HALF:]], axis=1),
        ],
        axis=0,
    )


def place():
    region, group = lax.axis_index("region"), lax.axis_index("group")
    core = lax.rem(region, 2)
    z = lax.rem(region // 2, 4)
    y = (group // 4) * 2 + region // 8
    x = lax.rem(group, 4)
    turned = ((x, y), (y, z), (z, x))
    return tuple(a + core * (b - a) for a, b in turned), core


def device(at, core, counted):
    a, b, c = at
    x, y, z = a + counted * (c - a), b + counted * (a - b), c + counted * (b - c)
    return ((lax.rem(y, 2) * 4 + z) * 2 + core, (y // 2) * 4 + x)


def step_kernel(
    pos_ref, count_ref, object_hbm, probe_hbm, diff_hbm, direct_hbm, turned_hbm, perm_hbm,
    out_ref, arrived, new_ref,
    ext, win, far, wanted, probe, pgrad, cov, go, hx, strips, direct, turned, perm, diff,
    spill, mate, total, factor, covered, *rest,
):
    got, pieces, local_sem, send_sem, recv_sem = rest
    me, core = place()
    regions = lax.axis_size("region")
    region, group = lax.axis_index("region"), lax.axis_index("group")
    sibling = device(me, 1 - core, core)
    up = (lax.rem(region + 1, regions), group)
    down = (lax.rem(region + regions - 1, regions), group)
    own = object_hbm.shape[0]
    edge = spill.shape[0]

    loads = [
        pltpu.make_async_copy(src, dst, local_sem.at[n])
        for n, (src, dst) in enumerate(
            [
                (object_hbm, ext.at[:own]),
                (diff_hbm, diff),
                (perm_hbm, perm),
                (probe_hbm, probe),
                (direct_hbm, direct),
                (turned_hbm, turned),
            ]
        )
    ]
    def shift(n, distance):
        return lax.rem(me[n] + distance, 4)

    plane_peers = [(shift(0, i), shift(1, j)) for i, j in OTHERS]
    plane_devices = [device((p, q, me[2]), core, core) for p, q in plane_peers]
    last_devices = [device((me[0], me[1], shift(2, d)), core, core) for d in (1, 2, 3)]

    barrier = pltpu.get_barrier_semaphore()
    partners = [sibling, up, down, *plane_devices, *last_devices]
    for partner in partners:
        pl.semaphore_signal(barrier, inc=1, device_id=partner, device_id_type=MESH)
    for load in loads:
        load.start()
    pl.semaphore_wait(barrier, len(partners))

    builders = {}

    def remote(key, build=None):
        if build is not None:
            builders[key] = (len(builders), build)
        n, build = builders[key]
        src, dst, to = build()
        return pltpu.make_async_remote_copy(
            src_ref=src, dst_ref=dst, send_sem=send_sem.at[n], recv_sem=recv_sem.at[n],
            device_id=to, device_id_type=MESH,
        )

    def send(key, build):
        remote(key, build).start()

    def arrive(key):
        remote(key).wait_recv()

    send("halo", lambda: (object_hbm.at[:edge], ext.at[own:], down))

    def result(u):
        return covered if u == COVERAGE else new_ref.at[2 * u + core]

    def start_core(u):
        send(
            ("core", u),
            lambda: (cov if u == COVERAGE else pgrad.at[2 * u + 1 - core], mate.at[u], sibling),
        )

    def start_plane(u):
        arrive(("core", u))
        total[u] = (cov[...] if u == COVERAGE else pgrad[2 * u + core]) + mate[u]
        for n, (p, q) in enumerate(plane_peers):
            send(
                ("plane", u, n),
                lambda n=n, p=p, q=q: (total.at[u, p, q], got.at[u, n], plane_devices[n]),
            )

    def start_last(u):
        for n in range(len(OTHERS)):
            arrive(("plane", u, n))
        value = total[u, me[0], me[1]]
        for n in range(len(OTHERS)):
            value = value + got[u, n]
        pieces[u, me[2]] = value
        for n in range(3):
            send(
                ("last", u, n),
                lambda n=n: (pieces.at[u, me[2]], pieces.at[u, me[2]], last_devices[n]),
            )

    def finish(u):
        for n in range(3):
            arrive(("last", u, n))
        reduced = (pieces[u, 0] + pieces[u, 1]) + (pieces[u, 2] + pieces[u, 3])
        if u == COVERAGE:
            covered[me[0], me[1]] = reduced
        else:
            here = (2 * u + core, me[0], me[1])
            new_ref[here] = probe[here] - reduced / (covered[me[0], me[1]] + 1e-06)
        for n in range(len(OTHERS)):
            send(
                ("back", u, n),
                lambda n=n: (
                    result(u).at[me[0], me[1]],
                    result(u).at[me[0], me[1]],
                    plane_devices[n],
                ),
            )

    def collect(u):
        for n in range(len(OTHERS)):
            arrive(("back", u, n))

    def hand_over(u):
        collect(u)
        send(("over", u), lambda: (result(u), result(u), sibling))

    def tiles_of(x):
        return x.reshape(4, 4, 2, 8, HALF)

    pgrad[...] = jnp.zeros_like(pgrad)
    cov[...] = jnp.zeros_like(cov)
    go[...] = jnp.zeros_like(go)
    hx[:, :PAD] = jnp.zeros((SLOTS, PAD, 8, HALF), F32)
    hx[:, PAD + 256 :] = jnp.zeros((SLOTS, PAD, 8, HALF), F32)
    loads[1].wait()
    loads[2].wait()

    def prepare(s, carry):
        high, low = parts_of(jnp.sqrt(diff[s]))
        root = jnp.dot(high, perm[...], preferred_element_type=F32) + jnp.dot(
            low, perm[...], preferred_element_type=F32
        )
        for h in (0, 1):
            wanted[s, h] = root[:, h * HALF : (h + 1) * HALF]
        return carry

    lax.fori_loop(0, SLOTS, prepare, 0)

    loads[3].wait()

    def probe_at(m, c):
        return jnp.concatenate(
            [probe[2 * m + c, :, :, :, h].reshape(256, HALF) for h in (0, 1)], axis=1
        )

    power = jnp.zeros((256, 256), F32)
    for m in range(MODES):
        pr, pi = probe_at(m, 0), probe_at(m, 1)
        power = power + pr * pr + pi * pi
    peak = jnp.max(power)
    for load in (loads[0], loads[4], loads[5]):
        load.wait()
    arrive("halo")

    base = region * own

    def spot(s):
        return jnp.clip(pos_ref[0, s] - base, 0, own - 1), pos_ref[1, s]

    def pick_columns(col, shape, wide):
        at = lax.broadcasted_iota(jnp.int32, shape, wide)
        narrow = lax.broadcasted_iota(jnp.int32, shape, 1 - wide)
        return jnp.where(at - narrow == col, 1.0, 0.0).astype(BF16)

    def live(s, shape):
        return jnp.where(jnp.full(shape, s, jnp.int32) < count_ref[0, 0], 1.0, 0.0).astype(F32)

    def cut(s, carry):
        row, col = spot(s)
        strips[...] = ext[pl.ds(row, 256)].reshape(256 * 8, HALF)
        pick = pick_columns(col, (512, 256), 0)
        for c in (0, 1):
            strip = jnp.concatenate(
                [strips[pl.ds(2 * k + c, 256, stride=8), :] for k in range(4)], axis=1
            )
            high, low = parts_of(strip)
            win[s, c] = jnp.dot(high, pick, preferred_element_type=F32) + jnp.dot(
                low, pick, preferred_element_type=F32
            )
        wr, wi = win[s, 0], win[s, 1]
        power = live(s, (256, 256)) * (wr * wr + wi * wi)
        for h in (0, 1):
            cov[:, :, :, h] += tiles_of(power[:, h * HALF : (h + 1) * HALF])
        return carry

    lax.fori_loop(0, SLOTS, cut, 0)
    start_core(COVERAGE)

    def forward(s, carry):
        @pl.when(s == 1)
        def _():
            start_plane(COVERAGE)

        @pl.when(s == 3)
        def _():
            start_last(COVERAGE)

        wr, wi = win[s, 0], win[s, 1]
        for m in range(MODES):
            pr, pi = probe_at(m, 0), probe_at(m, 1)
            er = pr * wr - pi * wi
            ei = pr * wi + pi * wr
            a = jnp.concatenate([er[:, :HALF] + er[:, HALF:], ei[:, :HALF] + ei[:, HALF:]], axis=1)
            b = jnp.concatenate([er[:, :HALF] - er[:, HALF:], ei[:, :HALF] - ei[:, HALF:]], axis=1)
            ye = mul_right(a, direct, 0)
            yo = mul_right(b, direct, 1)
            plus = swap_blocks(ye[:HALF] + ye[HALF:], yo[:HALF] + yo[HALF:])
            minus = swap_blocks(ye[:HALF] - ye[HALF:], yo[:HALF] - yo[HALF:])
            far[s, m, 0] = mul_left(turned, 0, plus)
            far[s, m, 1] = mul_left(turned, 1, minus)
        for p in (0, 1):
            intensity = jnp.zeros((HALF, 256), F32)
            for m in range(MODES):
                fr, fi = far[s, m, p, :HALF], far[s, m, p, HALF:]
                intensity = intensity + (fr * fr + fi * fi)
            root = jnp.concatenate(
                [wanted[s, h, pl.ds(p, HALF, stride=2), :] for h in (0, 1)], axis=1
            )
            factor[s, p] = live(s, (HALF, 256)) * (
                1.0 - root / jnp.sqrt(jnp.maximum(intensity, 1.0))
            )
        return carry

    lax.fori_loop(0, SLOTS, forward, 0)

    def inverse(m, slots):
        for s in slots:
            wr, wi = win[s, 0], win[s, 1]
            e, o = [
                mul_left(
                    direct,
                    p,
                    far[s, m, p] * jnp.concatenate([factor[s, p], factor[s, p]], axis=0),
                )
                for p in (0, 1)
            ]
            top, bottom = e + o, e - o
            ae, ao = [
                jnp.concatenate(
                    [
                        jnp.concatenate([x[:HALF, at : at + HALF], x[HALF:, at : at + HALF]], axis=1)
                        for x in (top, bottom)
                    ],
                    axis=0,
                )
                for at in (0, HALF)
            ]
            e = mul_right(ae, turned, 0)
            o = mul_right(ao, turned, 1)
            left, right = e + o, e - o
            cr = jnp.concatenate([left[:, :HALF], right[:, :HALF]], axis=1)
            ci = jnp.concatenate([left[:, HALF:], right[:, HALF:]], axis=1)
            pr, pi = probe_at(m, 0), probe_at(m, 1)
            go[s, 0] += pr * cr + pi * ci
            go[s, 1] += pr * ci - pi * cr
            for c, g in enumerate((wr * cr + wi * ci, wr * ci - wi * cr)):
                for h in (0, 1):
                    pgrad[2 * m + c, :, :, :, h] += tiles_of(g[:, h * HALF : (h + 1) * HALF])

    for m in range(MODES):

        def of_mode(i, carry, m=m):
            @pl.when(i == 1)
            def _():
                if m == 0:
                    finish(COVERAGE)
                else:
                    start_plane(m - 1)

            inverse(m, (2 * i, 2 * i + 1))
            return carry

        lax.fori_loop(0, SLOTS // 2, of_mode, 0)
        start_core(m)

    def turn(s, carry):
        pick = pick_columns(spot(s)[1], (256, 512), 1)
        for c in (0, 1):
            high, low = parts_of(go[s, c])
            strip = jnp.dot(high, pick, preferred_element_type=F32) + jnp.dot(
                low, pick, preferred_element_type=F32
            )
            for k in range(4):
                strips[pl.ds(2 * k + c, 256, stride=8), :] = strip[:, k * HALF : (k + 1) * HALF]
        hx[s, PAD : PAD + 256] = strips[...].reshape(256, 8, HALF)
        return carry

    lax.fori_loop(0, SLOTS, turn, 0)
    start_plane(3)
    start_last(0)

    def added(block):
        out = None
        for s in range(SLOTS):
            start = jnp.clip(block * PAD - spot(s)[0] + PAD, 0, PAD + 256)
            piece = hx[s, pl.ds(start, PAD)]
            out = piece if out is None else out + piece
        return out / peak

    blocks = own // PAD

    def below(i, carry):
        spill[pl.ds(i * PAD, PAD)] = added(blocks + i)
        return carry

    lax.fori_loop(0, edge // PAD, below, 0)
    send("spill", lambda: (spill, arrived, up))
    start_last(1)

    def within(i, carry):
        at = pl.ds(i * PAD, PAD)
        out_ref[at] = ext[at] - added(i)
        return carry

    lax.fori_loop(0, blocks, within, 0)
    start_last(2)
    finish(0)
    start_last(3)
    for u in (1, 2, 3):
        finish(u)
    for u in range(MODES):
        hand_over(u)
    collect(COVERAGE)
    arrive("spill")
    for u in range(MODES):
        arrive(("over", u))
    for key in builders:
        remote(key).wait_send()


def tiled(planes):
    return (
        planes.reshape(-1, 32, 8, 2, HALF)
        .transpose(0, 1, 3, 2, 4)
        .reshape(-1, *PLANE)
    )


def untiled(tiles, shape):
    return tiles.reshape(-1, 32, 2, 8, HALF).transpose(0, 1, 3, 2, 4).reshape(shape)


def step(positions, slot_counts, view, probe, diffraction):
    smem = pl.BlockSpec(memory_space=pltpu.SMEM)
    hbm = pl.BlockSpec(memory_space=pltpu.HBM)
    vmem = pl.BlockSpec(memory_space=pltpu.VMEM)
    direct, turned, perm = (jnp.asarray(t) for t in tables())
    own = view.shape[0]
    edge = own // 2
    copies = 2 + (MODES + 1) * (1 + 15 + 3 + 15) + MODES
    return pl.pallas_call(
        step_kernel,
        out_shape=(
            jax.ShapeDtypeStruct(view.shape, F32),
            jax.ShapeDtypeStruct((edge, 8, HALF), F32),
            jax.ShapeDtypeStruct((8, *PLANE), F32),
        ),
        in_specs=[smem] * 2 + [hbm] * 6,
        out_specs=[vmem] * 3,
        scratch_shapes=[
            pltpu.VMEM((own + edge, 8, HALF), F32),
            pltpu.VMEM((SLOTS, 2, 256, 256), F32),
            pltpu.VMEM((SLOTS, MODES, 2, 256, 256), F32),
            pltpu.VMEM((SLOTS, 2, 256, HALF), F32),
            pltpu.VMEM((8, *PLANE), F32),
            pltpu.VMEM((8, *PLANE), F32),
            pltpu.VMEM(PLANE, F32),
            pltpu.VMEM((SLOTS, 2, 256, 256), F32),
            pltpu.VMEM((SLOTS, 256 + 2 * PAD, 8, HALF), F32),
            pltpu.VMEM((256 * 8, HALF), F32),
            pltpu.VMEM(direct.shape, BF16),
            pltpu.VMEM(turned.shape, BF16),
            pltpu.VMEM(perm.shape, BF16),
            pltpu.VMEM(diffraction.shape, F32),
            pltpu.VMEM((edge, 8, HALF), F32),
            pltpu.VMEM((5, *PLANE), F32),
            pltpu.VMEM((5, *PLANE), F32),
            pltpu.VMEM((SLOTS, 2, HALF, 256), F32),
            pltpu.VMEM(PLANE, F32),
            pltpu.VMEM((5, len(OTHERS), *PLANE[2:]), F32),
            pltpu.VMEM((5, 4, *PLANE[2:]), F32),
            pltpu.SemaphoreType.DMA((6,)),
            pltpu.SemaphoreType.DMA((copies,)),
            pltpu.SemaphoreType.DMA((copies,)),
        ],
        compiler_params=pltpu.CompilerParams(
            vmem_limit_bytes=54 << 20, collective_id=0, has_side_effects=True
        ),
        name="step",
    )(positions, slot_counts, view, tiled(probe), diffraction, direct, turned, perm)


def on_device(object_slab, probe, diffraction, positions, slot_counts):
    tile_rows, _, tile_cols = object_slab.shape
    blocks = tile_cols // HALF
    view = (
        object_slab.reshape(tile_rows, 2, blocks, HALF)
        .transpose(0, 2, 1, 3)
        .reshape(tile_rows, blocks * 2, HALF)
    )
    view, arrived, new = step(positions.T, slot_counts, view, probe, diffraction)
    edge = arrived.shape[0]
    view = jnp.concatenate([view[:edge] - arrived, view[edge:]], axis=0)
    obj = (
        view.reshape(tile_rows, blocks, 2, HALF)
        .transpose(0, 2, 1, 3)
        .reshape(tile_rows, 2, tile_cols)
    )
    return (obj, untiled(new, probe.shape))


def solution(mesh):
    placed = (
        P("region", None, "group"),
        P(),
        P(("region", "group"), None, None),
        P(("region", "group"), None),
        P("group", "region"),
    )
    return jax.shard_map(
        on_device,
        mesh=mesh,
        in_specs=placed,
        out_specs=(P("region", None, "group"), P()),
        check_vma=False,
    )
```

```python
import math

import jax
import jax.numpy as jnp
import ml_dtypes
import numpy as np
from jax import lax
from jax.experimental import pallas as pl
from jax.experimental.pallas import tpu as pltpu
from jax.sharding import PartitionSpec as P

F32 = jnp.float32
BF16 = jnp.bfloat16
HALF = 128
SLOTS = 4
MODES = 4
PAD = 64
MESH = pl.DeviceIdType.MESH
PLANE = (4, 4, 2, 2, 8, HALF)
UNITS = ((0, 3), (3, 4), (4, 5))
OTHERS = tuple((i, j) for i in range(4) for j in range(4) if (i, j) != (0, 0))


def split_table(table):
    high = table.astype(np.float32).astype(ml_dtypes.bfloat16)
    low = (table - high.astype(np.float64)).astype(np.float32).astype(ml_dtypes.bfloat16)
    return high, low


def tables():
    n = np.arange(HALF)[:, None].astype(np.float64)
    k = np.arange(HALF)[None, :].astype(np.float64)
    direct, turned = [], []
    for parity in (0, 1):
        angle = -2.0 * math.pi * ((n * (2 * k + parity)) % 256) / 256
        re, im = np.cos(angle) / 16, np.sin(angle) / 16
        high, low = split_table(np.block([[re, im], [-im, re]]))
        direct.append(np.stack([high, low]))
        turned.append(np.stack([high.T, low.T]))
    perm = np.zeros((256, 256), np.float32)
    for c in range(256):
        perm[c, (c % 2) * HALF + c // 2] = 1
    return np.stack(direct), np.stack(turned), perm.astype(ml_dtypes.bfloat16)


def parts_of(x):
    high = x.astype(BF16)
    low = (x - high.astype(F32)).astype(BF16)
    return high, low


def mul_right(x, table, p):
    high, low = parts_of(x)
    table = jnp.concatenate([table[p, 0], table[p, 0], table[p, 1]], axis=0)
    return jnp.dot(jnp.concatenate([high, low, high], axis=1), table, preferred_element_type=F32)


def mul_left(table, p, x):
    high, low = parts_of(x)
    table = jnp.concatenate([table[p, 0], table[p, 0], table[p, 1]], axis=1)
    return jnp.dot(table, jnp.concatenate([high, low, high], axis=0), preferred_element_type=F32)


def swap_blocks(a, b):
    return jnp.concatenate(
        [
            jnp.concatenate([a[:, :HALF], b[:, :HALF]], axis=1),
            jnp.concatenate([a[:, HALF:], b[:, HALF:]], axis=1),
        ],
        axis=0,
    )


def place():
    region, group = lax.axis_index("region"), lax.axis_index("group")
    core = lax.rem(region, 2)
    z = lax.rem(region // 2, 4)
    y = (group // 4) * 2 + region // 8
    x = lax.rem(group, 4)
    turned = ((x, y), (y, z), (z, x))
    return tuple(a + core * (b - a) for a, b in turned), core


def device(at, core, counted):
    a, b, c = at
    x, y, z = a + counted * (c - a), b + counted * (a - b), c + counted * (b - c)
    return ((lax.rem(y, 2) * 4 + z) * 2 + core, (y // 2) * 4 + x)


def step_kernel(
    pos_ref, count_ref, object_hbm, probe_hbm, diff_hbm, direct_hbm, turned_hbm, perm_hbm,
    out_ref, new_ref,
    ext, win, far, wanted, probe, pgrad, cov, go, hx, strips, direct, turned, perm, diff,
    spill, arrived, mate, total, factor, covered, *rest,
):
    got, pieces, local_sem, send_sem, recv_sem = rest
    me, core = place()
    regions = lax.axis_size("region")
    region, group = lax.axis_index("region"), lax.axis_index("group")
    sibling = device(me, 1 - core, core)
    up = (lax.rem(region + 1, regions), group)
    down = (lax.rem(region + regions - 1, regions), group)
    own = object_hbm.shape[0]
    edge = spill.shape[0]

    loads = [
        pltpu.make_async_copy(src, dst, local_sem.at[n])
        for n, (src, dst) in enumerate(
            [
                (object_hbm, ext.at[:own]),
                (diff_hbm, diff),
                (perm_hbm, perm),
                (probe_hbm, probe),
                (direct_hbm, direct),
                (turned_hbm, turned),
            ]
        )
    ]
    def shift(n, distance):
        return lax.rem(me[n] + distance, 4)

    plane_peers = [(shift(0, i), shift(1, j)) for i, j in OTHERS]
    plane_devices = [device((p, q, me[2]), core, core) for p, q in plane_peers]
    last_devices = [device((me[0], me[1], shift(2, d)), core, core) for d in (1, 2, 3)]

    barrier = pltpu.get_barrier_semaphore()
    partners = [sibling, up, down, *plane_devices, *last_devices]
    for partner in partners:
        pl.semaphore_signal(barrier, inc=1, device_id=partner, device_id_type=MESH)
    pl.semaphore_wait(barrier, len(partners))

    builders = {}

    def remote(key, build=None):
        if build is not None:
            builders[key] = (len(builders), build)
        n, build = builders[key]
        src, dst, to = build()
        return pltpu.make_async_remote_copy(
            src_ref=src, dst_ref=dst, send_sem=send_sem.at[n], recv_sem=recv_sem.at[n],
            device_id=to, device_id_type=MESH,
        )

    def send(key, build):
        remote(key, build).start()

    def arrive(key):
        remote(key).wait_recv()

    send("halo", lambda: (object_hbm.at[:edge], ext.at[own:], down))
    for load in loads:
        load.start()

    def start_core(v):
        send(
            ("core", v),
            lambda: (cov if v == 0 else pgrad.at[2 * v - 1 - core], mate.at[v], sibling),
        )

    def start_plane(u):
        lo, hi = UNITS[u]
        for v in range(lo, hi):
            arrive(("core", v))
            total[v] = (cov[...] if v == 0 else pgrad[2 * v - 2 + core]) + mate[v]
        for n, (p, q) in enumerate(plane_peers):
            send(
                ("plane", u, n),
                lambda n=n, p=p, q=q: (
                    total.at[lo:hi, p, q],
                    got.at[n, lo:hi],
                    plane_devices[n],
                ),
            )

    def start_last(u):
        lo, hi = UNITS[u]
        for n in range(len(OTHERS)):
            arrive(("plane", u, n))
        value = total[lo:hi, me[0], me[1]]
        for n in range(len(OTHERS)):
            value = value + got[n, lo:hi]
        pieces[me[2], lo:hi] = value
        for n in range(3):
            send(
                ("last", u, n),
                lambda n=n: (
                    pieces.at[me[2], lo:hi],
                    pieces.at[me[2], lo:hi],
                    last_devices[n],
                ),
            )

    def finish(u):
        lo, hi = UNITS[u]
        for n in range(3):
            arrive(("last", u, n))
        for v in range(lo, hi):
            reduced = (pieces[0, v] + pieces[1, v]) + (pieces[2, v] + pieces[3, v])
            if v == 0:
                covered[...] = reduced + 1e-06
            else:
                old = probe[2 * v - 2 + core, me[0], me[1]]
                new_ref[v - 1, core, me[0], me[1]] = old - reduced / covered[...]
        here = (slice(max(lo, 1) - 1, hi - 1), core, me[0], me[1])
        for n in range(len(OTHERS)):
            send(
                ("back", u, n),
                lambda n=n: (new_ref.at[here], new_ref.at[here], plane_devices[n]),
            )

    def hand_over(u):
        lo, hi = UNITS[u]
        for n in range(len(OTHERS)):
            arrive(("back", u, n))
        whole = (slice(max(lo, 1) - 1, hi - 1), core)
        send(("over", u), lambda: (new_ref.at[whole], new_ref.at[whole], sibling))

    def tiles_of(x):
        return x.reshape(4, 4, 2, 8, HALF)

    pgrad[...] = jnp.zeros_like(pgrad)
    cov[...] = jnp.zeros_like(cov)
    go[...] = jnp.zeros_like(go)
    hx[:, :PAD] = jnp.zeros((SLOTS, PAD, 8, HALF), F32)
    hx[:, PAD + 256 :] = jnp.zeros((SLOTS, PAD, 8, HALF), F32)
    loads[1].wait()
    loads[2].wait()

    def prepare(s, carry):
        high, low = parts_of(jnp.sqrt(diff[s]))
        root = jnp.dot(high, perm[...], preferred_element_type=F32) + jnp.dot(
            low, perm[...], preferred_element_type=F32
        )
        for h in (0, 1):
            wanted[s, h] = root[:, h * HALF : (h + 1) * HALF]
        return carry

    lax.fori_loop(0, SLOTS, prepare, 0)

    loads[3].wait()

    def probe_at(m, c):
        return jnp.concatenate(
            [probe[2 * m + c, :, :, :, h].reshape(256, HALF) for h in (0, 1)], axis=1
        )

    power = jnp.zeros((256, 256), F32)
    for m in range(MODES):
        pr, pi = probe_at(m, 0), probe_at(m, 1)
        power = power + pr * pr + pi * pi
    peak = jnp.max(power)
    for load in (loads[0], loads[4], loads[5]):
        load.wait()
    arrive("halo")

    base = region * own

    def spot(s):
        return jnp.clip(pos_ref[0, s] - base, 0, own - 1), pos_ref[1, s]

    def pick_columns(col, shape, wide):
        at = lax.broadcasted_iota(jnp.int32, shape, wide)
        narrow = lax.broadcasted_iota(jnp.int32, shape, 1 - wide)
        return jnp.where(at - narrow == col, 1.0, 0.0).astype(BF16)

    def live(s, shape):
        return jnp.where(jnp.full(shape, s, jnp.int32) < count_ref[0, 0], 1.0, 0.0).astype(F32)

    def cut(s, carry):
        row, col = spot(s)
        strips[...] = ext[pl.ds(row, 256)].reshape(256 * 8, HALF)
        pick = pick_columns(col, (512, 256), 0)
        for c in (0, 1):
            strip = jnp.concatenate(
                [strips[pl.ds(2 * k + c, 256, stride=8), :] for k in range(4)], axis=1
            )
            high, low = parts_of(strip)
            win[s, c] = jnp.dot(high, pick, preferred_element_type=F32) + jnp.dot(
                low, pick, preferred_element_type=F32
            )
        wr, wi = win[s, 0], win[s, 1]
        power = live(s, (256, 256)) * (wr * wr + wi * wi)
        for h in (0, 1):
            cov[:, :, :, h] += tiles_of(power[:, h * HALF : (h + 1) * HALF])
        return carry

    lax.fori_loop(0, SLOTS, cut, 0)
    start_core(0)

    def forward(s, carry):
        wr, wi = win[s, 0], win[s, 1]
        for m in range(MODES):
            pr, pi = probe_at(m, 0), probe_at(m, 1)
            er = pr * wr - pi * wi
            ei = pr * wi + pi * wr
            a = jnp.concatenate([er[:, :HALF] + er[:, HALF:], ei[:, :HALF] + ei[:, HALF:]], axis=1)
            b = jnp.concatenate([er[:, :HALF] - er[:, HALF:], ei[:, :HALF] - ei[:, HALF:]], axis=1)
            ye = mul_right(a, direct, 0)
            yo = mul_right(b, direct, 1)
            plus = swap_blocks(ye[:HALF] + ye[HALF:], yo[:HALF] + yo[HALF:])
            minus = swap_blocks(ye[:HALF] - ye[HALF:], yo[:HALF] - yo[HALF:])
            far[s, m, 0] = mul_left(turned, 0, plus)
            far[s, m, 1] = mul_left(turned, 1, minus)
        for p in (0, 1):
            intensity = jnp.zeros((HALF, 256), F32)
            for m in range(MODES):
                fr, fi = far[s, m, p, :HALF], far[s, m, p, HALF:]
                intensity = intensity + (fr * fr + fi * fi)
            root = jnp.concatenate(
                [wanted[s, h, pl.ds(p, HALF, stride=2), :] for h in (0, 1)], axis=1
            )
            factor[s, p] = live(s, (HALF, 256)) * (
                1.0 - root / jnp.sqrt(jnp.maximum(intensity, 1.0))
            )
        return carry

    lax.fori_loop(0, SLOTS, forward, 0)

    def inverse(m, slots):
        for s in slots:
            wr, wi = win[s, 0], win[s, 1]
            e, o = [
                mul_left(
                    direct,
                    p,
                    far[s, m, p] * jnp.concatenate([factor[s, p], factor[s, p]], axis=0),
                )
                for p in (0, 1)
            ]
            top, bottom = e + o, e - o
            ae, ao = [
                jnp.concatenate(
                    [
                        jnp.concatenate([x[:HALF, at : at + HALF], x[HALF:, at : at + HALF]], axis=1)
                        for x in (top, bottom)
                    ],
                    axis=0,
                )
                for at in (0, HALF)
            ]
            e = mul_right(ae, turned, 0)
            o = mul_right(ao, turned, 1)
            left, right = e + o, e - o
            cr = jnp.concatenate([left[:, :HALF], right[:, :HALF]], axis=1)
            ci = jnp.concatenate([left[:, HALF:], right[:, HALF:]], axis=1)
            pr, pi = probe_at(m, 0), probe_at(m, 1)
            go[s, 0] += pr * cr + pi * ci
            go[s, 1] += pr * ci - pi * cr
            for c, g in enumerate((wr * cr + wi * ci, wr * ci - wi * cr)):
                for h in (0, 1):
                    pgrad[2 * m + c, :, :, :, h] += tiles_of(g[:, h * HALF : (h + 1) * HALF])

    for m in range(MODES):

        def of_mode(i, carry, m=m):
            if m >= 2:

                @pl.when(i == 1)
                def _():
                    start_plane(m - 2)

            inverse(m, (2 * i, 2 * i + 1))
            return carry

        lax.fori_loop(0, SLOTS // 2, of_mode, 0)
        start_core(m + 1)

    def turn(s, carry):
        pick = pick_columns(spot(s)[1], (256, 512), 1)
        for c in (0, 1):
            high, low = parts_of(go[s, c])
            strip = jnp.dot(high, pick, preferred_element_type=F32) + jnp.dot(
                low, pick, preferred_element_type=F32
            )
            for k in range(4):
                strips[pl.ds(2 * k + c, 256, stride=8), :] = strip[:, k * HALF : (k + 1) * HALF]
        hx[s, PAD : PAD + 256] = strips[...].reshape(256, 8, HALF)
        return carry

    lax.fori_loop(0, SLOTS, turn, 0)
    start_plane(2)
    start_last(0)

    def added(block):
        out = None
        for s in range(SLOTS):
            start = jnp.clip(block * PAD - spot(s)[0] + PAD, 0, PAD + 256)
            piece = hx[s, pl.ds(start, PAD)]
            out = piece if out is None else out + piece
        return out / peak

    blocks = own // PAD

    def below(i, carry):
        spill[pl.ds(i * PAD, PAD)] = added(blocks + i)
        return carry

    lax.fori_loop(0, edge // PAD, below, 0)
    send("spill", lambda: (spill, arrived, up))
    start_last(1)

    def within(i, carry):
        at = pl.ds(i * PAD, PAD)
        out_ref[at] = ext[at] - added(i)
        return carry

    lax.fori_loop(0, blocks, within, 0)
    finish(0)
    start_last(2)
    finish(1)
    finish(2)
    arrive("spill")

    def rest_of(i, carry):
        at = pl.ds(i * PAD, PAD)
        out_ref[at] = out_ref[at] - arrived[at]
        return carry

    lax.fori_loop(0, edge // PAD, rest_of, 0)
    for u in range(len(UNITS)):
        hand_over(u)
    for u in range(len(UNITS)):
        arrive(("over", u))
    for key in builders:
        remote(key).wait_send()


def tiled(planes):
    return (
        planes.reshape(-1, 32, 8, 2, HALF)
        .transpose(0, 1, 3, 2, 4)
        .reshape(-1, *PLANE)
    )


def untiled(tiles, shape):
    return tiles.reshape(-1, 32, 2, 8, HALF).transpose(0, 1, 3, 2, 4).reshape(shape)


def step(positions, slot_counts, view, probe, diffraction):
    smem = pl.BlockSpec(memory_space=pltpu.SMEM)
    hbm = pl.BlockSpec(memory_space=pltpu.HBM)
    vmem = pl.BlockSpec(memory_space=pltpu.VMEM)
    direct, turned, perm = (jnp.asarray(t) for t in tables())
    own = view.shape[0]
    edge = own // 2
    copies = 2 + 5 + len(UNITS) * (15 + 3 + 15 + 1)
    return pl.pallas_call(
        step_kernel,
        out_shape=(
            jax.ShapeDtypeStruct(view.shape, F32),
            jax.ShapeDtypeStruct((MODES, 2, *PLANE), F32),
        ),
        in_specs=[smem] * 2 + [hbm] * 6,
        out_specs=[vmem] * 2,
        scratch_shapes=[
            pltpu.VMEM((own + edge, 8, HALF), F32),
            pltpu.VMEM((SLOTS, 2, 256, 256), F32),
            pltpu.VMEM((SLOTS, MODES, 2, 256, 256), F32),
            pltpu.VMEM((SLOTS, 2, 256, HALF), F32),
            pltpu.VMEM((8, *PLANE), F32),
            pltpu.VMEM((8, *PLANE), F32),
            pltpu.VMEM(PLANE, F32),
            pltpu.VMEM((SLOTS, 2, 256, 256), F32),
            pltpu.VMEM((SLOTS, 256 + 2 * PAD, 8, HALF), F32),
            pltpu.VMEM((256 * 8, HALF), F32),
            pltpu.VMEM(direct.shape, BF16),
            pltpu.VMEM(turned.shape, BF16),
            pltpu.VMEM(perm.shape, BF16),
            pltpu.VMEM(diffraction.shape, F32),
            pltpu.VMEM((edge, 8, HALF), F32),
            pltpu.VMEM((edge, 8, HALF), F32),
            pltpu.VMEM((5, *PLANE), F32),
            pltpu.VMEM((5, *PLANE), F32),
            pltpu.VMEM((SLOTS, 2, HALF, 256), F32),
            pltpu.VMEM(PLANE[2:], F32),
            pltpu.VMEM((len(OTHERS), 5, *PLANE[2:]), F32),
            pltpu.VMEM((4, 5, *PLANE[2:]), F32),
            pltpu.SemaphoreType.DMA((6,)),
            pltpu.SemaphoreType.DMA((copies,)),
            pltpu.SemaphoreType.DMA((copies,)),
        ],
        compiler_params=pltpu.CompilerParams(
            vmem_limit_bytes=54 << 20, collective_id=0, has_side_effects=True
        ),
        name="step",
    )(positions, slot_counts, view, tiled(probe), diffraction, direct, turned, perm)


def on_device(object_slab, probe, diffraction, positions, slot_counts):
    tile_rows, _, tile_cols = object_slab.shape
    blocks = tile_cols // HALF
    view = (
        object_slab.reshape(tile_rows, 2, blocks, HALF)
        .transpose(0, 2, 1, 3)
        .reshape(tile_rows, blocks * 2, HALF)
    )
    view, new = step(positions.T, slot_counts, view, probe, diffraction)
    nothing = jnp.minimum(positions[0, 1], 0).astype(F32)
    view = view + nothing
    new = new + nothing
    obj = (
        view.reshape(tile_rows, blocks, 2, HALF)
        .transpose(0, 2, 1, 3)
        .reshape(tile_rows, 2, tile_cols)
    )
    return (obj, untiled(new, probe.shape))


def solution(mesh):
    placed = (
        P("region", None, "group"),
        P(),
        P(("region", "group"), None, None),
        P(("region", "group"), None),
        P("group", "region"),
    )
    return jax.shard_map(
        on_device,
        mesh=mesh,
        in_specs=placed,
        out_specs=(P("region", None, "group"), P()),
        check_vma=False,
    )
```

```python
import math

import jax
import jax.numpy as jnp
from jax import lax
from jax.experimental import pallas as pl
from jax.experimental.pallas import tpu as pltpu
from jax.sharding import PartitionSpec as P

F32 = jnp.float32
BF16 = jnp.bfloat16
HALF = 128
SLOTS = 4
MODES = 4
PAD = 64
MESH = pl.DeviceIdType.MESH
PLANE = (4, 4, 2, 2, 8, HALF)
COVERAGE = MODES
OTHERS = tuple((i, j) for i in range(4) for j in range(4) if (i, j) != (0, 0))


def parts_of(x):
    high = x.astype(BF16)
    low = (x - high.astype(F32)).astype(BF16)
    return high, low


def make_tables(direct, turned, perm):
    rows = lax.broadcasted_iota(jnp.int32, (HALF, HALF), 0)
    cols = lax.broadcasted_iota(jnp.int32, (HALF, HALF), 1)
    for parity in (0, 1):
        for table, n, k in ((direct, rows, cols), (turned, cols, rows)):
            angle = lax.rem(n * (2 * k + parity), 256).astype(F32) * (2.0 * math.pi / 256)
            re, im = jnp.cos(angle) / 16, -jnp.sin(angle) / 16
            above, below = (im, -im) if table is direct else (-im, im)
            full = jnp.concatenate(
                [jnp.concatenate([re, above], axis=1), jnp.concatenate([below, re], axis=1)],
                axis=0,
            )
            table[parity, 0], table[parity, 1] = parts_of(full)
    old = lax.broadcasted_iota(jnp.int32, (256, 256), 0)
    new = lax.broadcasted_iota(jnp.int32, (256, 256), 1)
    perm[...] = jnp.where(lax.rem(old, 2) * HALF + old // 2 == new, 1.0, 0.0).astype(BF16)


def mul_right(x, table, p):
    high, low = parts_of(x)
    table = jnp.concatenate([table[p, 0], table[p, 0], table[p, 1]], axis=0)
    return jnp.dot(jnp.concatenate([high, low, high], axis=1), table, preferred_element_type=F32)


def mul_left(table, p, x):
    high, low = parts_of(x)
    table = jnp.concatenate([table[p, 0], table[p, 0], table[p, 1]], axis=1)
    return jnp.dot(table, jnp.concatenate([high, low, high], axis=0), preferred_element_type=F32)


def swap_blocks(a, b):
    return jnp.concatenate(
        [
            jnp.concatenate([a[:, :HALF], b[:, :HALF]], axis=1),
            jnp.concatenate([a[:, HALF:], b[:, HALF:]], axis=1),
        ],
        axis=0,
    )


def place():
    region, group = lax.axis_index("region"), lax.axis_index("group")
    core = lax.rem(region, 2)
    z = lax.rem(region // 2, 4)
    y = (group // 4) * 2 + region // 8
    x = lax.rem(group, 4)
    turned = ((x, y), (y, z), (z, x))
    return tuple(a + core * (b - a) for a, b in turned), core


def device(at, core, counted):
    a, b, c = at
    x, y, z = a + counted * (c - a), b + counted * (a - b), c + counted * (b - c)
    return ((lax.rem(y, 2) * 4 + z) * 2 + core, (y // 2) * 4 + x)


def step_kernel(
    pos_ref, count_ref, object_hbm, probe_hbm, diff_hbm,
    out_ref, arrived, new_ref,
    ext, win, far, wanted, probe, pgrad, cov, go, hx, strips, direct, turned, perm, diff,
    spill, mate, total, factor, covered, *rest,
):
    got, pieces, local_sem, send_sem, recv_sem = rest
    me, core = place()
    regions = lax.axis_size("region")
    region, group = lax.axis_index("region"), lax.axis_index("group")
    sibling = device(me, 1 - core, core)
    up = (lax.rem(region + 1, regions), group)
    down = (lax.rem(region + regions - 1, regions), group)
    own = object_hbm.shape[0]
    edge = spill.shape[0]

    loads = [
        pltpu.make_async_copy(src, dst, local_sem.at[n])
        for n, (src, dst) in enumerate(
            [
                (object_hbm, ext.at[:own]),
                (diff_hbm, diff),
                (probe_hbm, probe),
            ]
        )
    ]
    def shift(n, distance):
        return lax.rem(me[n] + distance, 4)

    plane_peers = [(shift(0, i), shift(1, j)) for i, j in OTHERS]
    plane_devices = [device((p, q, me[2]), core, core) for p, q in plane_peers]
    last_devices = [device((me[0], me[1], shift(2, d)), core, core) for d in (1, 2, 3)]

    barrier = pltpu.get_barrier_semaphore()
    partners = [sibling, up, down, *plane_devices, *last_devices]
    for partner in partners:
        pl.semaphore_signal(barrier, inc=1, device_id=partner, device_id_type=MESH)
    for load in loads:
        load.start()
    pl.semaphore_wait(barrier, len(partners))

    builders = {}

    def remote(key, build=None):
        if build is not None:
            builders[key] = (len(builders), build)
        n, build = builders[key]
        src, dst, to = build()
        return pltpu.make_async_remote_copy(
            src_ref=src, dst_ref=dst, send_sem=send_sem.at[n], recv_sem=recv_sem.at[n],
            device_id=to, device_id_type=MESH,
        )

    def send(key, build):
        remote(key, build).start()

    def arrive(key):
        remote(key).wait_recv()

    send("halo", lambda: (object_hbm.at[:edge], ext.at[own:], down))

    def result(u):
        return new_ref.at[2 * u + core]

    def start_core(u):
        send(
            ("core", u),
            lambda: (cov if u == COVERAGE else pgrad.at[2 * u + 1 - core], mate.at[u], sibling),
        )

    def start_plane(u):
        arrive(("core", u))
        total[u] = (cov[...] if u == COVERAGE else pgrad[2 * u + core]) + mate[u]
        for n, (p, q) in enumerate(plane_peers):
            send(
                ("plane", u, n),
                lambda n=n, p=p, q=q: (total.at[u, p, q], got.at[u, n], plane_devices[n]),
            )

    def start_last(u):
        for n in range(len(OTHERS)):
            arrive(("plane", u, n))
        value = total[u, me[0], me[1]]
        for n in range(len(OTHERS)):
            value = value + got[u, n]
        pieces[u, me[2]] = value
        for n in range(3):
            send(
                ("last", u, n),
                lambda n=n: (pieces.at[u, me[2]], pieces.at[u, me[2]], last_devices[n]),
            )

    def finish(u):
        for n in range(3):
            arrive(("last", u, n))
        reduced = (pieces[u, 0] + pieces[u, 1]) + (pieces[u, 2] + pieces[u, 3])
        if u == COVERAGE:
            covered[...] = reduced + 1e-06
            return
        here = (2 * u + core, me[0], me[1])
        new_ref[here] = probe[here] - reduced / covered[...]
        for n in range(len(OTHERS)):
            send(
                ("back", u, n),
                lambda n=n: (
                    result(u).at[me[0], me[1]],
                    result(u).at[me[0], me[1]],
                    plane_devices[n],
                ),
            )

    def collect(u):
        for n in range(len(OTHERS)):
            arrive(("back", u, n))

    def hand_over(u):
        collect(u)
        send(("over", u), lambda: (result(u), result(u), sibling))

    def tiles_of(x):
        return x.reshape(4, 4, 2, 8, HALF)

    pgrad[...] = jnp.zeros_like(pgrad)
    cov[...] = jnp.zeros_like(cov)
    go[...] = jnp.zeros_like(go)
    hx[:, :PAD] = jnp.zeros((SLOTS, PAD, 8, HALF), F32)
    hx[:, PAD + 256 :] = jnp.zeros((SLOTS, PAD, 8, HALF), F32)
    make_tables(direct, turned, perm)
    loads[1].wait()

    def prepare(s, carry):
        high, low = parts_of(
            jnp.sqrt(
                jnp.concatenate([diff[s, :, h].reshape(256, HALF) for h in (0, 1)], axis=1)
            )
        )
        root = jnp.dot(high, perm[...], preferred_element_type=F32) + jnp.dot(
            low, perm[...], preferred_element_type=F32
        )
        for h in (0, 1):
            wanted[s, h] = root[:, h * HALF : (h + 1) * HALF]
        return carry

    lax.fori_loop(0, SLOTS, prepare, 0)

    loads[2].wait()

    def probe_at(m, c):
        return jnp.concatenate(
            [probe[2 * m + c, :, :, :, h].reshape(256, HALF) for h in (0, 1)], axis=1
        )

    power = jnp.zeros((256, 256), F32)
    for m in range(MODES):
        pr, pi = probe_at(m, 0), probe_at(m, 1)
        power = power + pr * pr + pi * pi
    peak = jnp.max(power)
    loads[0].wait()
    arrive("halo")

    base = region * own

    def spot(s):
        return jnp.clip(pos_ref[0, s] - base, 0, own - 1), pos_ref[1, s]

    def pick_columns(col, shape, wide):
        at = lax.broadcasted_iota(jnp.int32, shape, wide)
        narrow = lax.broadcasted_iota(jnp.int32, shape, 1 - wide)
        return jnp.where(at - narrow == col, 1.0, 0.0).astype(BF16)

    def live(s, shape):
        return jnp.where(jnp.full(shape, s, jnp.int32) < count_ref[0, 0], 1.0, 0.0).astype(F32)

    def cut(s, carry):
        row, col = spot(s)
        strips[...] = ext[pl.ds(row, 256)].reshape(256 * 8, HALF)
        pick = pick_columns(col, (512, 256), 0)
        for c in (0, 1):
            strip = jnp.concatenate(
                [strips[pl.ds(2 * k + c, 256, stride=8), :] for k in range(4)], axis=1
            )
            high, low = parts_of(strip)
            win[s, c] = jnp.dot(high, pick, preferred_element_type=F32) + jnp.dot(
                low, pick, preferred_element_type=F32
            )
        wr, wi = win[s, 0], win[s, 1]
        power = live(s, (256, 256)) * (wr * wr + wi * wi)
        for h in (0, 1):
            cov[:, :, :, h] += tiles_of(power[:, h * HALF : (h + 1) * HALF])
        return carry

    lax.fori_loop(0, SLOTS, cut, 0)
    start_core(COVERAGE)

    def forward(s, carry):
        @pl.when(s == 1)
        def _():
            start_plane(COVERAGE)

        @pl.when(s == 3)
        def _():
            start_last(COVERAGE)

        wr, wi = win[s, 0], win[s, 1]
        for m in range(MODES):
            pr, pi = probe_at(m, 0), probe_at(m, 1)
            er = pr * wr - pi * wi
            ei = pr * wi + pi * wr
            a = jnp.concatenate([er[:, :HALF] + er[:, HALF:], ei[:, :HALF] + ei[:, HALF:]], axis=1)
            b = jnp.concatenate([er[:, :HALF] - er[:, HALF:], ei[:, :HALF] - ei[:, HALF:]], axis=1)
            ye = mul_right(a, direct, 0)
            yo = mul_right(b, direct, 1)
            plus = swap_blocks(ye[:HALF] + ye[HALF:], yo[:HALF] + yo[HALF:])
            minus = swap_blocks(ye[:HALF] - ye[HALF:], yo[:HALF] - yo[HALF:])
            far[s, m, 0] = mul_left(turned, 0, plus)
            far[s, m, 1] = mul_left(turned, 1, minus)
        for p in (0, 1):
            intensity = jnp.zeros((HALF, 256), F32)
            for m in range(MODES):
                fr, fi = far[s, m, p, :HALF], far[s, m, p, HALF:]
                intensity = intensity + (fr * fr + fi * fi)
            root = jnp.concatenate(
                [wanted[s, h, pl.ds(p, HALF, stride=2), :] for h in (0, 1)], axis=1
            )
            factor[s, p] = live(s, (HALF, 256)) * (
                1.0 - root / jnp.sqrt(jnp.maximum(intensity, 1.0))
            )
        return carry

    lax.fori_loop(0, SLOTS, forward, 0)

    def inverse(m, slots):
        for s in slots:
            wr, wi = win[s, 0], win[s, 1]
            e, o = [
                mul_left(
                    direct,
                    p,
                    far[s, m, p] * jnp.concatenate([factor[s, p], factor[s, p]], axis=0),
                )
                for p in (0, 1)
            ]
            top, bottom = e + o, e - o
            ae, ao = [
                jnp.concatenate(
                    [
                        jnp.concatenate([x[:HALF, at : at + HALF], x[HALF:, at : at + HALF]], axis=1)
                        for x in (top, bottom)
                    ],
                    axis=0,
                )
                for at in (0, HALF)
            ]
            e = mul_right(ae, turned, 0)
            o = mul_right(ao, turned, 1)
            left, right = e + o, e - o
            cr = jnp.concatenate([left[:, :HALF], right[:, :HALF]], axis=1)
            ci = jnp.concatenate([left[:, HALF:], right[:, HALF:]], axis=1)
            pr, pi = probe_at(m, 0), probe_at(m, 1)
            go[s, 0] += pr * cr + pi * ci
            go[s, 1] += pr * ci - pi * cr
            for c, g in enumerate((wr * cr + wi * ci, wr * ci - wi * cr)):
                for h in (0, 1):
                    pgrad[2 * m + c, :, :, :, h] += tiles_of(g[:, h * HALF : (h + 1) * HALF])

    for m in range(MODES):

        def of_mode(i, carry, m=m):
            if m == 3:

                @pl.when(i == 0)
                def _():
                    start_last(0)

            @pl.when(i == 1)
            def _():
                if m == 0:
                    finish(COVERAGE)
                else:
                    start_plane(m - 1)

            inverse(m, (2 * i, 2 * i + 1))
            return carry

        lax.fori_loop(0, SLOTS // 2, of_mode, 0)
        start_core(m)

    def turn(s, carry):
        pick = pick_columns(spot(s)[1], (256, 512), 1)
        for c in (0, 1):
            high, low = parts_of(go[s, c])
            strip = jnp.dot(high, pick, preferred_element_type=F32) + jnp.dot(
                low, pick, preferred_element_type=F32
            )
            for k in range(4):
                strips[pl.ds(2 * k + c, 256, stride=8), :] = strip[:, k * HALF : (k + 1) * HALF]
        hx[s, PAD : PAD + 256] = strips[...].reshape(256, 8, HALF)
        return carry

    lax.fori_loop(0, SLOTS, turn, 0)
    start_plane(3)
    finish(0)

    def added(block):
        out = None
        for s in range(SLOTS):
            start = jnp.clip(block * PAD - spot(s)[0] + PAD, 0, PAD + 256)
            piece = hx[s, pl.ds(start, PAD)]
            out = piece if out is None else out + piece
        return out / peak

    blocks = own // PAD

    def below(i, carry):
        spill[pl.ds(i * PAD, PAD)] = added(blocks + i)
        return carry

    lax.fori_loop(0, edge // PAD, below, 0)
    send("spill", lambda: (spill, arrived, up))
    start_last(1)

    def within(i, carry):
        at = pl.ds(i * PAD, PAD)
        out_ref[at] = ext[at] - added(i)
        return carry

    lax.fori_loop(0, blocks, within, 0)
    start_last(2)
    finish(1)
    start_last(3)
    finish(2)
    finish(3)
    for u in range(MODES):
        hand_over(u)
    arrive("spill")
    for u in range(MODES):
        arrive(("over", u))
    for key in builders:
        remote(key).wait_send()


def tiled(planes):
    return (
        planes.reshape(-1, 32, 8, 2, HALF)
        .transpose(0, 1, 3, 2, 4)
        .reshape(-1, *PLANE)
    )


def untiled(tiles, shape):
    return tiles.reshape(-1, 32, 2, 8, HALF).transpose(0, 1, 3, 2, 4).reshape(shape)


def step(positions, slot_counts, view, probe, diffraction):
    smem = pl.BlockSpec(memory_space=pltpu.SMEM)
    hbm = pl.BlockSpec(memory_space=pltpu.HBM)
    vmem = pl.BlockSpec(memory_space=pltpu.VMEM)
    own = view.shape[0]
    diffraction = diffraction.reshape(SLOTS, 32, 8, 2, HALF).transpose(0, 1, 3, 2, 4)
    edge = own // 2
    copies = 2 + (MODES + 1) * (1 + 15 + 3 + 15) + MODES
    return pl.pallas_call(
        step_kernel,
        out_shape=(
            jax.ShapeDtypeStruct(view.shape, F32),
            jax.ShapeDtypeStruct((edge, 8, HALF), F32),
            jax.ShapeDtypeStruct((8, *PLANE), F32),
        ),
        in_specs=[smem] * 2 + [hbm] * 3,
        out_specs=[vmem] * 3,
        scratch_shapes=[
            pltpu.VMEM((own + edge, 8, HALF), F32),
            pltpu.VMEM((SLOTS, 2, 256, 256), F32),
            pltpu.VMEM((SLOTS, MODES, 2, 256, 256), F32),
            pltpu.VMEM((SLOTS, 2, 256, HALF), F32),
            pltpu.VMEM((8, *PLANE), F32),
            pltpu.VMEM((8, *PLANE), F32),
            pltpu.VMEM(PLANE, F32),
            pltpu.VMEM((SLOTS, 2, 256, 256), F32),
            pltpu.VMEM((SLOTS, 256 + 2 * PAD, 8, HALF), F32),
            pltpu.VMEM((256 * 8, HALF), F32),
            pltpu.VMEM((2, 2, 256, 256), BF16),
            pltpu.VMEM((2, 2, 256, 256), BF16),
            pltpu.VMEM((256, 256), BF16),
            pltpu.VMEM(diffraction.shape, F32),
            pltpu.VMEM((edge, 8, HALF), F32),
            pltpu.VMEM((5, *PLANE), F32),
            pltpu.VMEM((5, *PLANE), F32),
            pltpu.VMEM((SLOTS, 2, HALF, 256), F32),
            pltpu.VMEM(PLANE[2:], F32),
            pltpu.VMEM((5, len(OTHERS), *PLANE[2:]), F32),
            pltpu.VMEM((5, 4, *PLANE[2:]), F32),
            pltpu.SemaphoreType.DMA((3,)),
            pltpu.SemaphoreType.DMA((copies,)),
            pltpu.SemaphoreType.DMA((copies,)),
        ],
        compiler_params=pltpu.CompilerParams(
            vmem_limit_bytes=46 << 20, collective_id=0, has_side_effects=True
        ),
        name="step",
    )(positions, slot_counts, view, tiled(probe), diffraction)


def on_device(object_slab, probe, diffraction, positions, slot_counts):
    tile_rows, _, tile_cols = object_slab.shape
    blocks = tile_cols // HALF
    view = (
        object_slab.reshape(tile_rows, 2, blocks, HALF)
        .transpose(0, 2, 1, 3)
        .reshape(tile_rows, blocks * 2, HALF)
    )
    view, arrived, new = step(positions.T, slot_counts, view, probe, diffraction)
    edge = arrived.shape[0]
    view = jnp.concatenate([view[:edge] - arrived, view[edge:]], axis=0)
    obj = (
        view.reshape(tile_rows, blocks, 2, HALF)
        .transpose(0, 2, 1, 3)
        .reshape(tile_rows, 2, tile_cols)
    )
    return (obj, untiled(new, probe.shape))


def solution(mesh):
    placed = (
        P("region", None, "group"),
        P(),
        P(("region", "group"), None, None),
        P(("region", "group"), None),
        P("group", "region"),
    )
    return jax.shard_map(
        on_device,
        mesh=mesh,
        in_specs=placed,
        out_specs=(P("region", None, "group"), P()),
        check_vma=False,
    )
```

```python
import math

import jax
import jax.numpy as jnp
from jax import lax
from jax.experimental import pallas as pl
from jax.experimental.pallas import tpu as pltpu
from jax.sharding import PartitionSpec as P

F32 = jnp.float32
BF16 = jnp.bfloat16
HALF = 128
SLOTS = 4
MODES = 4
PAD = 64
MESH = pl.DeviceIdType.MESH
PLANE = (4, 4, 2, 2, 8, HALF)
COVERAGE = MODES
OTHERS = tuple((i, j) for i in range(4) for j in range(4) if (i, j) != (0, 0))


def parts_of(x):
    high = x.astype(BF16)
    low = (x - high.astype(F32)).astype(BF16)
    return high, low


def make_tables(direct, turned, perm):
    rows = lax.broadcasted_iota(jnp.int32, (HALF, HALF), 0)
    cols = lax.broadcasted_iota(jnp.int32, (HALF, HALF), 1)
    for parity in (0, 1):
        for table, n, k in ((direct, rows, cols), (turned, cols, rows)):
            angle = lax.rem(n * (2 * k + parity), 256).astype(F32) * (2.0 * math.pi / 256)
            re, im = jnp.cos(angle) / 16, -jnp.sin(angle) / 16
            above, below = (im, -im) if table is direct else (-im, im)
            full = jnp.concatenate(
                [jnp.concatenate([re, above], axis=1), jnp.concatenate([below, re], axis=1)],
                axis=0,
            )
            table[parity, 0], table[parity, 1] = parts_of(full)
    old = lax.broadcasted_iota(jnp.int32, (256, 256), 0)
    new = lax.broadcasted_iota(jnp.int32, (256, 256), 1)
    perm[...] = jnp.where(lax.rem(old, 2) * HALF + old // 2 == new, 1.0, 0.0).astype(BF16)


def mul_right(x, table, p):
    high, low = parts_of(x)
    table = jnp.concatenate([table[p, 0], table[p, 0], table[p, 1]], axis=0)
    return jnp.dot(jnp.concatenate([high, low, high], axis=1), table, preferred_element_type=F32)


def mul_left(table, p, x):
    high, low = parts_of(x)
    table = jnp.concatenate([table[p, 0], table[p, 0], table[p, 1]], axis=1)
    return jnp.dot(table, jnp.concatenate([high, low, high], axis=0), preferred_element_type=F32)


def swap_blocks(a, b):
    return jnp.concatenate(
        [
            jnp.concatenate([a[:, :HALF], b[:, :HALF]], axis=1),
            jnp.concatenate([a[:, HALF:], b[:, HALF:]], axis=1),
        ],
        axis=0,
    )


def place():
    region, group = lax.axis_index("region"), lax.axis_index("group")
    core = lax.rem(region, 2)
    z = lax.rem(region // 2, 4)
    y = (group // 4) * 2 + region // 8
    x = lax.rem(group, 4)
    turned = ((x, y), (y, z), (z, x))
    return tuple(a + core * (b - a) for a, b in turned), core


def device(at, core, counted):
    a, b, c = at
    x, y, z = a + counted * (c - a), b + counted * (a - b), c + counted * (b - c)
    return ((lax.rem(y, 2) * 4 + z) * 2 + core, (y // 2) * 4 + x)


def step_kernel(
    pos_ref, count_ref, object_hbm, probe_hbm, diff_hbm,
    out_ref, arrived, new_ref,
    ext, win, far, wanted, probe, pgrad, cov, go, hx, strips, direct, turned, perm, diff,
    spill, mate, total, factor, covered, *rest,
):
    got, pieces, local_sem, send_sem, recv_sem = rest
    me, core = place()
    regions = lax.axis_size("region")
    region, group = lax.axis_index("region"), lax.axis_index("group")
    sibling = device(me, 1 - core, core)
    up = (lax.rem(region + 1, regions), group)
    down = (lax.rem(region + regions - 1, regions), group)
    own = object_hbm.shape[0]
    edge = spill.shape[0]

    loads = [
        pltpu.make_async_copy(src, dst, local_sem.at[n])
        for n, (src, dst) in enumerate(
            [
                (object_hbm, ext.at[:own]),
                (diff_hbm, diff),
                (probe_hbm, probe),
            ]
        )
    ]
    def shift(n, distance):
        return lax.rem(me[n] + distance, 4)

    plane_peers = [(shift(0, i), shift(1, j)) for i, j in OTHERS]
    plane_devices = [device((p, q, me[2]), core, core) for p, q in plane_peers]
    last_devices = [device((me[0], me[1], shift(2, d)), core, core) for d in (1, 2, 3)]

    barrier = pltpu.get_barrier_semaphore()
    partners = [sibling, up, down, *plane_devices, *last_devices]
    for partner in partners:
        pl.semaphore_signal(barrier, inc=1, device_id=partner, device_id_type=MESH)
    for load in loads:
        load.start()
    pl.semaphore_wait(barrier, len(partners))

    builders = {}

    def remote(key, build=None):
        if build is not None:
            builders[key] = (len(builders), build)
        n, build = builders[key]
        src, dst, to = build()
        return pltpu.make_async_remote_copy(
            src_ref=src, dst_ref=dst, send_sem=send_sem.at[n], recv_sem=recv_sem.at[n],
            device_id=to, device_id_type=MESH,
        )

    def send(key, build):
        remote(key, build).start()

    def arrive(key):
        remote(key).wait_recv()

    send("halo", lambda: (object_hbm.at[:edge], ext.at[own:], down))

    def result(u):
        return new_ref.at[2 * u + core]

    def start_core(u):
        send(
            ("core", u),
            lambda: (cov if u == COVERAGE else pgrad.at[2 * u + 1 - core], mate.at[u], sibling),
        )

    def start_plane(u):
        arrive(("core", u))
        total[u] = (cov[...] if u == COVERAGE else pgrad[2 * u + core]) + mate[u]
        for n, (p, q) in enumerate(plane_peers):
            send(
                ("plane", u, n),
                lambda n=n, p=p, q=q: (total.at[u, p, q], got.at[u, n], plane_devices[n]),
            )

    def start_last(u):
        for n in range(len(OTHERS)):
            arrive(("plane", u, n))
        value = total[u, me[0], me[1]]
        for n in range(len(OTHERS)):
            value = value + got[u, n]
        pieces[u, me[2]] = value
        for n in range(3):
            send(
                ("last", u, n),
                lambda n=n: (pieces.at[u, me[2]], pieces.at[u, me[2]], last_devices[n]),
            )

    def finish(u):
        for n in range(3):
            arrive(("last", u, n))
        reduced = (pieces[u, 0] + pieces[u, 1]) + (pieces[u, 2] + pieces[u, 3])
        if u == COVERAGE:
            covered[...] = reduced + 1e-06
            return
        here = (2 * u + core, me[0], me[1])
        new_ref[here] = probe[here] - reduced / covered[...]
        to = range(len(OTHERS)) if u == MODES - 1 else [OTHERS.index((0, d)) for d in (1, 2, 3)]
        for n in to:
            send(
                ("back", u, n),
                lambda n=n: (
                    result(u).at[me[0], me[1]],
                    result(u).at[me[0], me[1]],
                    plane_devices[n],
                ),
            )

    def relay(u):
        for d in (1, 2, 3):
            arrive(("back", u, OTHERS.index((0, d))))
        for d in (1, 2, 3):
            n = OTHERS.index((d, 0))
            send(
                ("back", u, n),
                lambda n=n: (result(u).at[me[0]], result(u).at[me[0]], plane_devices[n]),
            )

    def collect(u):
        to = range(len(OTHERS)) if u == MODES - 1 else [OTHERS.index((d, 0)) for d in (1, 2, 3)]
        for n in to:
            arrive(("back", u, n))

    def hand_over(u):
        collect(u)
        send(("over", u), lambda: (result(u), result(u), sibling))

    def tiles_of(x):
        return x.reshape(4, 4, 2, 8, HALF)

    pgrad[...] = jnp.zeros_like(pgrad)
    cov[...] = jnp.zeros_like(cov)
    go[...] = jnp.zeros_like(go)
    hx[:, :PAD] = jnp.zeros((SLOTS, PAD, 8, HALF), F32)
    hx[:, PAD + 256 :] = jnp.zeros((SLOTS, PAD, 8, HALF), F32)
    make_tables(direct, turned, perm)
    loads[1].wait()

    def prepare(s, carry):
        high, low = parts_of(
            jnp.sqrt(
                jnp.concatenate([diff[s, :, h].reshape(256, HALF) for h in (0, 1)], axis=1)
            )
        )
        root = jnp.dot(high, perm[...], preferred_element_type=F32) + jnp.dot(
            low, perm[...], preferred_element_type=F32
        )
        for h in (0, 1):
            wanted[s, h] = root[:, h * HALF : (h + 1) * HALF]
        return carry

    lax.fori_loop(0, SLOTS, prepare, 0)

    loads[2].wait()

    def probe_at(m, c):
        return jnp.concatenate(
            [probe[2 * m + c, :, :, :, h].reshape(256, HALF) for h in (0, 1)], axis=1
        )

    power = jnp.zeros((256, 256), F32)
    for m in range(MODES):
        pr, pi = probe_at(m, 0), probe_at(m, 1)
        power = power + pr * pr + pi * pi
    peak = jnp.max(power)
    loads[0].wait()
    arrive("halo")

    base = region * own

    def spot(s):
        return jnp.clip(pos_ref[0, s] - base, 0, own - 1), pos_ref[1, s]

    def pick_columns(col, shape, wide):
        at = lax.broadcasted_iota(jnp.int32, shape, wide)
        narrow = lax.broadcasted_iota(jnp.int32, shape, 1 - wide)
        return jnp.where(at - narrow == col, 1.0, 0.0).astype(BF16)

    def live(s, shape):
        return jnp.where(jnp.full(shape, s, jnp.int32) < count_ref[0, 0], 1.0, 0.0).astype(F32)

    def cut(s, carry):
        row, col = spot(s)
        strips[...] = ext[pl.ds(row, 256)].reshape(256 * 8, HALF)
        pick = pick_columns(col, (512, 256), 0)
        for c in (0, 1):
            strip = jnp.concatenate(
                [strips[pl.ds(2 * k + c, 256, stride=8), :] for k in range(4)], axis=1
            )
            high, low = parts_of(strip)
            win[s, c] = jnp.dot(high, pick, preferred_element_type=F32) + jnp.dot(
                low, pick, preferred_element_type=F32
            )
        wr, wi = win[s, 0], win[s, 1]
        power = live(s, (256, 256)) * (wr * wr + wi * wi)
        for h in (0, 1):
            cov[:, :, :, h] += tiles_of(power[:, h * HALF : (h + 1) * HALF])
        return carry

    lax.fori_loop(0, SLOTS, cut, 0)
    start_core(COVERAGE)

    def forward(s, carry):
        @pl.when(s == 1)
        def _():
            start_plane(COVERAGE)

        @pl.when(s == 3)
        def _():
            start_last(COVERAGE)

        wr, wi = win[s, 0], win[s, 1]
        for m in range(MODES):
            pr, pi = probe_at(m, 0), probe_at(m, 1)
            er = pr * wr - pi * wi
            ei = pr * wi + pi * wr
            a = jnp.concatenate([er[:, :HALF] + er[:, HALF:], ei[:, :HALF] + ei[:, HALF:]], axis=1)
            b = jnp.concatenate([er[:, :HALF] - er[:, HALF:], ei[:, :HALF] - ei[:, HALF:]], axis=1)
            ye = mul_right(a, direct, 0)
            yo = mul_right(b, direct, 1)
            plus = swap_blocks(ye[:HALF] + ye[HALF:], yo[:HALF] + yo[HALF:])
            minus = swap_blocks(ye[:HALF] - ye[HALF:], yo[:HALF] - yo[HALF:])
            far[s, m, 0] = mul_left(turned, 0, plus)
            far[s, m, 1] = mul_left(turned, 1, minus)
        for p in (0, 1):
            intensity = jnp.zeros((HALF, 256), F32)
            for m in range(MODES):
                fr, fi = far[s, m, p, :HALF], far[s, m, p, HALF:]
                intensity = intensity + (fr * fr + fi * fi)
            root = jnp.concatenate(
                [wanted[s, h, pl.ds(p, HALF, stride=2), :] for h in (0, 1)], axis=1
            )
            factor[s, p] = live(s, (HALF, 256)) * (
                1.0 - root / jnp.sqrt(jnp.maximum(intensity, 1.0))
            )
        return carry

    lax.fori_loop(0, SLOTS, forward, 0)

    def inverse(m, slots):
        for s in slots:
            wr, wi = win[s, 0], win[s, 1]
            e, o = [
                mul_left(
                    direct,
                    p,
                    far[s, m, p] * jnp.concatenate([factor[s, p], factor[s, p]], axis=0),
                )
                for p in (0, 1)
            ]
            top, bottom = e + o, e - o
            ae, ao = [
                jnp.concatenate(
                    [
                        jnp.concatenate([x[:HALF, at : at + HALF], x[HALF:, at : at + HALF]], axis=1)
                        for x in (top, bottom)
                    ],
                    axis=0,
                )
                for at in (0, HALF)
            ]
            e = mul_right(ae, turned, 0)
            o = mul_right(ao, turned, 1)
            left, right = e + o, e - o
            cr = jnp.concatenate([left[:, :HALF], right[:, :HALF]], axis=1)
            ci = jnp.concatenate([left[:, HALF:], right[:, HALF:]], axis=1)
            pr, pi = probe_at(m, 0), probe_at(m, 1)
            go[s, 0] += pr * cr + pi * ci
            go[s, 1] += pr * ci - pi * cr
            for c, g in enumerate((wr * cr + wi * ci, wr * ci - wi * cr)):
                for h in (0, 1):
                    pgrad[2 * m + c, :, :, :, h] += tiles_of(g[:, h * HALF : (h + 1) * HALF])

    for m in range(MODES):

        def of_mode(i, carry, m=m):
            if m == 3:

                @pl.when(i == 0)
                def _():
                    start_last(0)

            @pl.when(i == 1)
            def _():
                if m == 0:
                    finish(COVERAGE)
                else:
                    start_plane(m - 1)

            inverse(m, (2 * i, 2 * i + 1))
            return carry

        lax.fori_loop(0, SLOTS // 2, of_mode, 0)
        start_core(m)

    def turn(s, carry):
        pick = pick_columns(spot(s)[1], (256, 512), 1)
        for c in (0, 1):
            high, low = parts_of(go[s, c])
            strip = jnp.dot(high, pick, preferred_element_type=F32) + jnp.dot(
                low, pick, preferred_element_type=F32
            )
            for k in range(4):
                strips[pl.ds(2 * k + c, 256, stride=8), :] = strip[:, k * HALF : (k + 1) * HALF]
        hx[s, PAD : PAD + 256] = strips[...].reshape(256, 8, HALF)
        return carry

    lax.fori_loop(0, SLOTS, turn, 0)
    start_plane(3)
    finish(0)

    def added(block):
        out = None
        for s in range(SLOTS):
            start = jnp.clip(block * PAD - spot(s)[0] + PAD, 0, PAD + 256)
            piece = hx[s, pl.ds(start, PAD)]
            out = piece if out is None else out + piece
        return out / peak

    blocks = own // PAD

    def below(i, carry):
        spill[pl.ds(i * PAD, PAD)] = added(blocks + i)
        return carry

    lax.fori_loop(0, edge // PAD, below, 0)
    send("spill", lambda: (spill, arrived, up))
    start_last(1)
    relay(0)

    def within(i, carry):
        at = pl.ds(i * PAD, PAD)
        out_ref[at] = ext[at] - added(i)
        return carry

    lax.fori_loop(0, blocks, within, 0)
    start_last(2)
    finish(1)
    start_last(3)
    finish(2)
    relay(1)
    finish(3)
    relay(2)
    for u in range(MODES):
        hand_over(u)
    arrive("spill")
    for u in range(MODES):
        arrive(("over", u))
    for key in builders:
        remote(key).wait_send()


def tiled(planes):
    return (
        planes.reshape(-1, 32, 8, 2, HALF)
        .transpose(0, 1, 3, 2, 4)
        .reshape(-1, *PLANE)
    )


def untiled(tiles, shape):
    return tiles.reshape(-1, 32, 2, 8, HALF).transpose(0, 1, 3, 2, 4).reshape(shape)


def step(positions, slot_counts, view, probe, diffraction):
    smem = pl.BlockSpec(memory_space=pltpu.SMEM)
    hbm = pl.BlockSpec(memory_space=pltpu.HBM)
    vmem = pl.BlockSpec(memory_space=pltpu.VMEM)
    own = view.shape[0]
    diffraction = diffraction.reshape(SLOTS, 32, 8, 2, HALF).transpose(0, 1, 3, 2, 4)
    edge = own // 2
    copies = 2 + (MODES + 1) * (1 + 15 + 3 + 15) + MODES
    return pl.pallas_call(
        step_kernel,
        out_shape=(
            jax.ShapeDtypeStruct(view.shape, F32),
            jax.ShapeDtypeStruct((edge, 8, HALF), F32),
            jax.ShapeDtypeStruct((8, *PLANE), F32),
        ),
        in_specs=[smem] * 2 + [hbm] * 3,
        out_specs=[vmem] * 3,
        scratch_shapes=[
            pltpu.VMEM((own + edge, 8, HALF), F32),
            pltpu.VMEM((SLOTS, 2, 256, 256), F32),
            pltpu.VMEM((SLOTS, MODES, 2, 256, 256), F32),
            pltpu.VMEM((SLOTS, 2, 256, HALF), F32),
            pltpu.VMEM((8, *PLANE), F32),
            pltpu.VMEM((8, *PLANE), F32),
            pltpu.VMEM(PLANE, F32),
            pltpu.VMEM((SLOTS, 2, 256, 256), F32),
            pltpu.VMEM((SLOTS, 256 + 2 * PAD, 8, HALF), F32),
            pltpu.VMEM((256 * 8, HALF), F32),
            pltpu.VMEM((2, 2, 256, 256), BF16),
            pltpu.VMEM((2, 2, 256, 256), BF16),
            pltpu.VMEM((256, 256), BF16),
            pltpu.VMEM(diffraction.shape, F32),
            pltpu.VMEM((edge, 8, HALF), F32),
            pltpu.VMEM((5, *PLANE), F32),
            pltpu.VMEM((5, *PLANE), F32),
            pltpu.VMEM((SLOTS, 2, HALF, 256), F32),
            pltpu.VMEM(PLANE[2:], F32),
            pltpu.VMEM((5, len(OTHERS), *PLANE[2:]), F32),
            pltpu.VMEM((5, 4, *PLANE[2:]), F32),
            pltpu.SemaphoreType.DMA((3,)),
            pltpu.SemaphoreType.DMA((copies,)),
            pltpu.SemaphoreType.DMA((copies,)),
        ],
        compiler_params=pltpu.CompilerParams(
            vmem_limit_bytes=46 << 20, collective_id=0, has_side_effects=True
        ),
        name="step",
    )(positions, slot_counts, view, tiled(probe), diffraction)


def on_device(object_slab, probe, diffraction, positions, slot_counts):
    tile_rows, _, tile_cols = object_slab.shape
    blocks = tile_cols // HALF
    view = (
        object_slab.reshape(tile_rows, 2, blocks, HALF)
        .transpose(0, 2, 1, 3)
        .reshape(tile_rows, blocks * 2, HALF)
    )
    view, arrived, new = step(positions.T, slot_counts, view, probe, diffraction)
    edge = arrived.shape[0]
    view = jnp.concatenate([view[:edge] - arrived, view[edge:]], axis=0)
    obj = (
        view.reshape(tile_rows, blocks, 2, HALF)
        .transpose(0, 2, 1, 3)
        .reshape(tile_rows, 2, tile_cols)
    )
    return (obj, untiled(new, probe.shape))


def solution(mesh):
    placed = (
        P("region", None, "group"),
        P(),
        P(("region", "group"), None, None),
        P(("region", "group"), None),
        P("group", "region"),
    )
    return jax.shard_map(
        on_device,
        mesh=mesh,
        in_specs=placed,
        out_specs=(P("region", None, "group"), P()),
        check_vma=False,
    )
```

```python
import math

import jax
import jax.numpy as jnp
from jax import lax
from jax.experimental import pallas as pl
from jax.experimental.pallas import tpu as pltpu
from jax.sharding import PartitionSpec as P

F32 = jnp.float32
BF16 = jnp.bfloat16
HALF = 128
SLOTS = 4
MODES = 4
PAD = 64
MESH = pl.DeviceIdType.MESH
PLANE = (4, 4, 2, 2, 8, HALF)
COVERAGE = MODES
OTHERS = tuple((i, j) for i in range(4) for j in range(4) if (i, j) != (0, 0))


def parts_of(x):
    high = x.astype(BF16)
    low = (x - high.astype(F32)).astype(BF16)
    return high, low


def make_tables(direct, turned, perm):
    rows = lax.broadcasted_iota(jnp.int32, (HALF, HALF), 0)
    cols = lax.broadcasted_iota(jnp.int32, (HALF, HALF), 1)
    for parity in (0, 1):
        for table, n, k in ((direct, rows, cols), (turned, cols, rows)):
            angle = lax.rem(n * (2 * k + parity), 256).astype(F32) * (2.0 * math.pi / 256)
            re, im = jnp.cos(angle) / 16, -jnp.sin(angle) / 16
            above, below = (im, -im) if table is direct else (-im, im)
            full = jnp.concatenate(
                [jnp.concatenate([re, above], axis=1), jnp.concatenate([below, re], axis=1)],
                axis=0,
            )
            table[parity, 0], table[parity, 1] = parts_of(full)
    old = lax.broadcasted_iota(jnp.int32, (256, 256), 0)
    new = lax.broadcasted_iota(jnp.int32, (256, 256), 1)
    perm[...] = jnp.where(lax.rem(old, 2) * HALF + old // 2 == new, 1.0, 0.0).astype(BF16)


def mul_right(x, table, p):
    high, low = parts_of(x)
    table = jnp.concatenate([table[p, 0], table[p, 0], table[p, 1]], axis=0)
    return jnp.dot(jnp.concatenate([high, low, high], axis=1), table, preferred_element_type=F32)


def mul_left(table, p, x):
    high, low = parts_of(x)
    table = jnp.concatenate([table[p, 0], table[p, 0], table[p, 1]], axis=1)
    return jnp.dot(table, jnp.concatenate([high, low, high], axis=0), preferred_element_type=F32)


def swap_blocks(a, b):
    return jnp.concatenate(
        [
            jnp.concatenate([a[:, :HALF], b[:, :HALF]], axis=1),
            jnp.concatenate([a[:, HALF:], b[:, HALF:]], axis=1),
        ],
        axis=0,
    )


def place():
    region, group = lax.axis_index("region"), lax.axis_index("group")
    core = lax.rem(region, 2)
    z = lax.rem(region // 2, 4)
    y = (group // 4) * 2 + region // 8
    x = lax.rem(group, 4)
    turned = ((x, y), (y, z), (z, x))
    return tuple(a + core * (b - a) for a, b in turned), core


def device(at, core, counted):
    a, b, c = at
    x, y, z = a + counted * (c - a), b + counted * (a - b), c + counted * (b - c)
    return ((lax.rem(y, 2) * 4 + z) * 2 + core, (y // 2) * 4 + x)


def step_kernel(
    pos_ref, count_ref, object_hbm, probe_hbm, diff_hbm,
    out_ref, arrived, new_ref,
    ext, win, far, wanted, probe, pgrad, cov, go, hx, strips, direct, turned, perm, diff,
    spill, mate, total, factor, covered, *rest,
):
    got, pieces, row_got, row_sum, local_sem, send_sem, recv_sem = rest
    me, core = place()
    regions = lax.axis_size("region")
    region, group = lax.axis_index("region"), lax.axis_index("group")
    sibling = device(me, 1 - core, core)
    up = (lax.rem(region + 1, regions), group)
    down = (lax.rem(region + regions - 1, regions), group)
    own = object_hbm.shape[0]
    edge = spill.shape[0]

    loads = [
        pltpu.make_async_copy(src, dst, local_sem.at[n])
        for n, (src, dst) in enumerate(
            [
                (object_hbm, ext.at[:own]),
                (diff_hbm, diff),
                (probe_hbm, probe),
            ]
        )
    ]
    def shift(n, distance):
        return lax.rem(me[n] + distance, 4)

    plane_peers = [(shift(0, i), shift(1, j)) for i, j in OTHERS]
    plane_devices = [device((p, q, me[2]), core, core) for p, q in plane_peers]
    last_devices = [device((me[0], me[1], shift(2, d)), core, core) for d in (1, 2, 3)]

    barrier = pltpu.get_barrier_semaphore()
    partners = [sibling, up, down, *plane_devices, *last_devices]
    for partner in partners:
        pl.semaphore_signal(barrier, inc=1, device_id=partner, device_id_type=MESH)
    for load in loads:
        load.start()
    pl.semaphore_wait(barrier, len(partners))

    builders = {}

    def remote(key, build=None):
        if build is not None:
            builders[key] = (len(builders), build)
        n, build = builders[key]
        src, dst, to = build()
        return pltpu.make_async_remote_copy(
            src_ref=src, dst_ref=dst, send_sem=send_sem.at[n], recv_sem=recv_sem.at[n],
            device_id=to, device_id_type=MESH,
        )

    def send(key, build):
        remote(key, build).start()

    def arrive(key):
        remote(key).wait_recv()

    send("halo", lambda: (object_hbm.at[:edge], ext.at[own:], down))

    def result(u):
        return new_ref.at[2 * u + core]

    def start_core(u):
        send(
            ("core", u),
            lambda: (cov if u == COVERAGE else pgrad.at[2 * u + 1 - core], mate.at[u], sibling),
        )

    def join(u):
        arrive(("core", u))
        total[u] = (cov[...] if u == COVERAGE else pgrad[2 * u + core]) + mate[u]

    def start_plane(u):
        join(u)
        for n, (p, q) in enumerate(plane_peers):
            send(
                ("plane", u, n),
                lambda n=n, p=p, q=q: (total.at[u, p, q], got.at[u, n], plane_devices[n]),
            )

    def start_row(u):
        join(u)
        for d in (1, 2, 3):
            n = OTHERS.index((d, 0))
            send(
                ("row", u, d),
                lambda n=n, d=d: (
                    total.at[u, plane_peers[n][0]],
                    row_got.at[u, d - 1],
                    plane_devices[n],
                ),
            )

    def start_column(u):
        for d in (1, 2, 3):
            arrive(("row", u, d))
        row_sum[u] = total[u, me[0]] + row_got[u, 0] + row_got[u, 1] + row_got[u, 2]
        for d in (1, 2, 3):
            n = OTHERS.index((0, d))
            send(
                ("plane", u, d - 1),
                lambda n=n, d=d: (
                    row_sum.at[u, plane_peers[n][1]],
                    got.at[u, d - 1],
                    plane_devices[n],
                ),
            )

    def start_last(u):
        count = len(OTHERS) if u == MODES - 1 else 3
        for n in range(count):
            arrive(("plane", u, n))
        value = total[u, me[0], me[1]] if u == MODES - 1 else row_sum[u, me[1]]
        for n in range(count):
            value = value + got[u, n]
        pieces[u, me[2]] = value
        for n in range(3):
            send(
                ("last", u, n),
                lambda n=n: (pieces.at[u, me[2]], pieces.at[u, me[2]], last_devices[n]),
            )

    def finish(u):
        for n in range(3):
            arrive(("last", u, n))
        reduced = (pieces[u, 0] + pieces[u, 1]) + (pieces[u, 2] + pieces[u, 3])
        if u == COVERAGE:
            covered[...] = reduced + 1e-06
            return
        here = (2 * u + core, me[0], me[1])
        new_ref[here] = probe[here] - reduced / covered[...]
        to = range(len(OTHERS)) if u == MODES - 1 else [OTHERS.index((0, d)) for d in (1, 2, 3)]
        for n in to:
            send(
                ("back", u, n),
                lambda n=n: (
                    result(u).at[me[0], me[1]],
                    result(u).at[me[0], me[1]],
                    plane_devices[n],
                ),
            )

    def relay(u):
        for d in (1, 2, 3):
            arrive(("back", u, OTHERS.index((0, d))))
        for d in (1, 2, 3):
            n = OTHERS.index((d, 0))
            send(
                ("back", u, n),
                lambda n=n: (result(u).at[me[0]], result(u).at[me[0]], plane_devices[n]),
            )

    def collect(u):
        to = range(len(OTHERS)) if u == MODES - 1 else [OTHERS.index((d, 0)) for d in (1, 2, 3)]
        for n in to:
            arrive(("back", u, n))

    def hand_over(u):
        collect(u)
        send(("over", u), lambda: (result(u), result(u), sibling))

    def tiles_of(x):
        return x.reshape(4, 4, 2, 8, HALF)

    pgrad[...] = jnp.zeros_like(pgrad)
    cov[...] = jnp.zeros_like(cov)
    go[...] = jnp.zeros_like(go)
    hx[:, :PAD] = jnp.zeros((SLOTS, PAD, 8, HALF), F32)
    hx[:, PAD + 256 :] = jnp.zeros((SLOTS, PAD, 8, HALF), F32)
    make_tables(direct, turned, perm)
    loads[1].wait()

    def prepare(s, carry):
        high, low = parts_of(
            jnp.sqrt(
                jnp.concatenate([diff[s, :, h].reshape(256, HALF) for h in (0, 1)], axis=1)
            )
        )
        root = jnp.dot(high, perm[...], preferred_element_type=F32) + jnp.dot(
            low, perm[...], preferred_element_type=F32
        )
        for h in (0, 1):
            wanted[s, h] = root[:, h * HALF : (h + 1) * HALF]
        return carry

    lax.fori_loop(0, SLOTS, prepare, 0)

    loads[2].wait()

    def probe_at(m, c):
        return jnp.concatenate(
            [probe[2 * m + c, :, :, :, h].reshape(256, HALF) for h in (0, 1)], axis=1
        )

    power = jnp.zeros((256, 256), F32)
    for m in range(MODES):
        pr, pi = probe_at(m, 0), probe_at(m, 1)
        power = power + pr * pr + pi * pi
    peak = jnp.max(power)
    loads[0].wait()
    arrive("halo")

    base = region * own

    def spot(s):
        return jnp.clip(pos_ref[0, s] - base, 0, own - 1), pos_ref[1, s]

    def pick_columns(col, shape, wide):
        at = lax.broadcasted_iota(jnp.int32, shape, wide)
        narrow = lax.broadcasted_iota(jnp.int32, shape, 1 - wide)
        return jnp.where(at - narrow == col, 1.0, 0.0).astype(BF16)

    def live(s, shape):
        return jnp.where(jnp.full(shape, s, jnp.int32) < count_ref[0, 0], 1.0, 0.0).astype(F32)

    def cut(s, carry):
        row, col = spot(s)
        strips[...] = ext[pl.ds(row, 256)].reshape(256 * 8, HALF)
        pick = pick_columns(col, (512, 256), 0)
        for c in (0, 1):
            strip = jnp.concatenate(
                [strips[pl.ds(2 * k + c, 256, stride=8), :] for k in range(4)], axis=1
            )
            high, low = parts_of(strip)
            win[s, c] = jnp.dot(high, pick, preferred_element_type=F32) + jnp.dot(
                low, pick, preferred_element_type=F32
            )
        wr, wi = win[s, 0], win[s, 1]
        power = live(s, (256, 256)) * (wr * wr + wi * wi)
        for h in (0, 1):
            cov[:, :, :, h] += tiles_of(power[:, h * HALF : (h + 1) * HALF])
        return carry

    lax.fori_loop(0, SLOTS, cut, 0)
    start_core(COVERAGE)

    def forward(s, carry):
        @pl.when(s == 1)
        def _():
            start_row(COVERAGE)

        @pl.when(s == 2)
        def _():
            start_column(COVERAGE)

        @pl.when(s == 3)
        def _():
            start_last(COVERAGE)

        wr, wi = win[s, 0], win[s, 1]
        for m in range(MODES):
            pr, pi = probe_at(m, 0), probe_at(m, 1)
            er = pr * wr - pi * wi
            ei = pr * wi + pi * wr
            a = jnp.concatenate([er[:, :HALF] + er[:, HALF:], ei[:, :HALF] + ei[:, HALF:]], axis=1)
            b = jnp.concatenate([er[:, :HALF] - er[:, HALF:], ei[:, :HALF] - ei[:, HALF:]], axis=1)
            ye = mul_right(a, direct, 0)
            yo = mul_right(b, direct, 1)
            plus = swap_blocks(ye[:HALF] + ye[HALF:], yo[:HALF] + yo[HALF:])
            minus = swap_blocks(ye[:HALF] - ye[HALF:], yo[:HALF] - yo[HALF:])
            far[s, m, 0] = mul_left(turned, 0, plus)
            far[s, m, 1] = mul_left(turned, 1, minus)
        for p in (0, 1):
            intensity = jnp.zeros((HALF, 256), F32)
            for m in range(MODES):
                fr, fi = far[s, m, p, :HALF], far[s, m, p, HALF:]
                intensity = intensity + (fr * fr + fi * fi)
            root = jnp.concatenate(
                [wanted[s, h, pl.ds(p, HALF, stride=2), :] for h in (0, 1)], axis=1
            )
            factor[s, p] = live(s, (HALF, 256)) * (
                1.0 - root / jnp.sqrt(jnp.maximum(intensity, 1.0))
            )
        return carry

    lax.fori_loop(0, SLOTS, forward, 0)

    def inverse(m, slots):
        for s in slots:
            wr, wi = win[s, 0], win[s, 1]
            e, o = [
                mul_left(
                    direct,
                    p,
                    far[s, m, p] * jnp.concatenate([factor[s, p], factor[s, p]], axis=0),
                )
                for p in (0, 1)
            ]
            top, bottom = e + o, e - o
            ae, ao = [
                jnp.concatenate(
                    [
                        jnp.concatenate([x[:HALF, at : at + HALF], x[HALF:, at : at + HALF]], axis=1)
                        for x in (top, bottom)
                    ],
                    axis=0,
                )
                for at in (0, HALF)
            ]
            e = mul_right(ae, turned, 0)
            o = mul_right(ao, turned, 1)
            left, right = e + o, e - o
            cr = jnp.concatenate([left[:, :HALF], right[:, :HALF]], axis=1)
            ci = jnp.concatenate([left[:, HALF:], right[:, HALF:]], axis=1)
            pr, pi = probe_at(m, 0), probe_at(m, 1)
            go[s, 0] += pr * cr + pi * ci
            go[s, 1] += pr * ci - pi * cr
            for c, g in enumerate((wr * cr + wi * ci, wr * ci - wi * cr)):
                for h in (0, 1):
                    pgrad[2 * m + c, :, :, :, h] += tiles_of(g[:, h * HALF : (h + 1) * HALF])

    for m in range(MODES):

        def of_mode(i, carry, m=m):
            if m == 3:

                @pl.when(i == 0)
                def _():
                    start_column(0)

            @pl.when(i == 1)
            def _():
                if m == 0:
                    finish(COVERAGE)
                else:
                    start_row(m - 1)

            inverse(m, (2 * i, 2 * i + 1))
            return carry

        lax.fori_loop(0, SLOTS // 2, of_mode, 0)
        start_core(m)

    def turn(s, carry):
        pick = pick_columns(spot(s)[1], (256, 512), 1)
        for c in (0, 1):
            high, low = parts_of(go[s, c])
            strip = jnp.dot(high, pick, preferred_element_type=F32) + jnp.dot(
                low, pick, preferred_element_type=F32
            )
            for k in range(4):
                strips[pl.ds(2 * k + c, 256, stride=8), :] = strip[:, k * HALF : (k + 1) * HALF]
        hx[s, PAD : PAD + 256] = strips[...].reshape(256, 8, HALF)
        return carry

    lax.fori_loop(0, SLOTS, turn, 0)
    start_plane(3)
    start_last(0)
    start_column(1)

    def added(block):
        out = None
        for s in range(SLOTS):
            start = jnp.clip(block * PAD - spot(s)[0] + PAD, 0, PAD + 256)
            piece = hx[s, pl.ds(start, PAD)]
            out = piece if out is None else out + piece
        return out / peak

    blocks = own // PAD

    def below(i, carry):
        spill[pl.ds(i * PAD, PAD)] = added(blocks + i)
        return carry

    lax.fori_loop(0, edge // PAD, below, 0)
    send("spill", lambda: (spill, arrived, up))
    start_column(2)

    def within(i, carry):
        at = pl.ds(i * PAD, PAD)
        out_ref[at] = ext[at] - added(i)
        return carry

    lax.fori_loop(0, blocks, within, 0)
    finish(0)
    start_last(1)
    start_last(2)
    start_last(3)
    relay(0)
    finish(1)
    finish(2)
    finish(3)
    relay(1)
    relay(2)
    for u in range(MODES):
        hand_over(u)
    arrive("spill")
    for u in range(MODES):
        arrive(("over", u))
    for key in builders:
        remote(key).wait_send()


def tiled(planes):
    return (
        planes.reshape(-1, 32, 8, 2, HALF)
        .transpose(0, 1, 3, 2, 4)
        .reshape(-1, *PLANE)
    )


def untiled(tiles, shape):
    return tiles.reshape(-1, 32, 2, 8, HALF).transpose(0, 1, 3, 2, 4).reshape(shape)


def step(positions, slot_counts, view, probe, diffraction):
    smem = pl.BlockSpec(memory_space=pltpu.SMEM)
    hbm = pl.BlockSpec(memory_space=pltpu.HBM)
    vmem = pl.BlockSpec(memory_space=pltpu.VMEM)
    own = view.shape[0]
    diffraction = diffraction.reshape(SLOTS, 32, 8, 2, HALF).transpose(0, 1, 3, 2, 4)
    edge = own // 2
    copies = 2 + (MODES + 1) * (1 + 15 + 3 + 15) + MODES
    return pl.pallas_call(
        step_kernel,
        out_shape=(
            jax.ShapeDtypeStruct(view.shape, F32),
            jax.ShapeDtypeStruct((edge, 8, HALF), F32),
            jax.ShapeDtypeStruct((8, *PLANE), F32),
        ),
        in_specs=[smem] * 2 + [hbm] * 3,
        out_specs=[vmem] * 3,
        scratch_shapes=[
            pltpu.VMEM((own + edge, 8, HALF), F32),
            pltpu.VMEM((SLOTS, 2, 256, 256), F32),
            pltpu.VMEM((SLOTS, MODES, 2, 256, 256), F32),
            pltpu.VMEM((SLOTS, 2, 256, HALF), F32),
            pltpu.VMEM((8, *PLANE), F32),
            pltpu.VMEM((8, *PLANE), F32),
            pltpu.VMEM(PLANE, F32),
            pltpu.VMEM((SLOTS, 2, 256, 256), F32),
            pltpu.VMEM((SLOTS, 256 + 2 * PAD, 8, HALF), F32),
            pltpu.VMEM((256 * 8, HALF), F32),
            pltpu.VMEM((2, 2, 256, 256), BF16),
            pltpu.VMEM((2, 2, 256, 256), BF16),
            pltpu.VMEM((256, 256), BF16),
            pltpu.VMEM(diffraction.shape, F32),
            pltpu.VMEM((edge, 8, HALF), F32),
            pltpu.VMEM((5, *PLANE), F32),
            pltpu.VMEM((5, *PLANE), F32),
            pltpu.VMEM((SLOTS, 2, HALF, 256), F32),
            pltpu.VMEM(PLANE[2:], F32),
            pltpu.VMEM((5, len(OTHERS), *PLANE[2:]), F32),
            pltpu.VMEM((5, 4, *PLANE[2:]), F32),
            pltpu.VMEM((5, 3, *PLANE[1:]), F32),
            pltpu.VMEM((5, *PLANE[1:]), F32),
            pltpu.SemaphoreType.DMA((3,)),
            pltpu.SemaphoreType.DMA((copies,)),
            pltpu.SemaphoreType.DMA((copies,)),
        ],
        compiler_params=pltpu.CompilerParams(
            vmem_limit_bytes=46 << 20, collective_id=0, has_side_effects=True
        ),
        name="step",
    )(positions, slot_counts, view, tiled(probe), diffraction)


def on_device(object_slab, probe, diffraction, positions, slot_counts):
    tile_rows, _, tile_cols = object_slab.shape
    blocks = tile_cols // HALF
    view = (
        object_slab.reshape(tile_rows, 2, blocks, HALF)
        .transpose(0, 2, 1, 3)
        .reshape(tile_rows, blocks * 2, HALF)
    )
    view, arrived, new = step(positions.T, slot_counts, view, probe, diffraction)
    edge = arrived.shape[0]
    view = jnp.concatenate([view[:edge] - arrived, view[edge:]], axis=0)
    obj = (
        view.reshape(tile_rows, blocks, 2, HALF)
        .transpose(0, 2, 1, 3)
        .reshape(tile_rows, 2, tile_cols)
    )
    return (obj, untiled(new, probe.shape))


def solution(mesh):
    placed = (
        P("region", None, "group"),
        P(),
        P(("region", "group"), None, None),
        P(("region", "group"), None),
        P("group", "region"),
    )
    return jax.shard_map(
        on_device,
        mesh=mesh,
        in_specs=placed,
        out_specs=(P("region", None, "group"), P()),
        check_vma=False,
    )
```

```python
import math

import jax
import jax.numpy as jnp
from jax import lax
from jax.experimental import pallas as pl
from jax.experimental.pallas import tpu as pltpu
from jax.sharding import PartitionSpec as P

F32 = jnp.float32
BF16 = jnp.bfloat16
HALF = 128
SLOTS = 4
MODES = 4
PAD = 64
MESH = pl.DeviceIdType.MESH
PLANE = (4, 4, 2, 2, 8, HALF)
COVERAGE = MODES
OTHERS = tuple((i, j) for i in range(4) for j in range(4) if (i, j) != (0, 0))


def parts_of(x):
    high = x.astype(BF16)
    low = (x - high.astype(F32)).astype(BF16)
    return high, low


def make_tables(direct, turned, perm):
    rows = lax.broadcasted_iota(jnp.int32, (HALF, HALF), 0)
    cols = lax.broadcasted_iota(jnp.int32, (HALF, HALF), 1)
    for parity in (0, 1):
        for table, n, k in ((direct, rows, cols), (turned, cols, rows)):
            angle = lax.rem(n * (2 * k + parity), 256).astype(F32) * (2.0 * math.pi / 256)
            re, im = jnp.cos(angle) / 16, -jnp.sin(angle) / 16
            above, below = (im, -im) if table is direct else (-im, im)
            full = jnp.concatenate(
                [jnp.concatenate([re, above], axis=1), jnp.concatenate([below, re], axis=1)],
                axis=0,
            )
            table[parity, 0], table[parity, 1] = parts_of(full)
    old = lax.broadcasted_iota(jnp.int32, (256, 256), 0)
    new = lax.broadcasted_iota(jnp.int32, (256, 256), 1)
    perm[...] = jnp.where(lax.rem(old, 2) * HALF + old // 2 == new, 1.0, 0.0).astype(BF16)


def mul_right(x, table, p):
    high, low = parts_of(x)
    table = jnp.concatenate([table[p, 0], table[p, 0], table[p, 1]], axis=0)
    return jnp.dot(jnp.concatenate([high, low, high], axis=1), table, preferred_element_type=F32)


def mul_left(table, p, x):
    high, low = parts_of(x)
    table = jnp.concatenate([table[p, 0], table[p, 0], table[p, 1]], axis=1)
    return jnp.dot(table, jnp.concatenate([high, low, high], axis=0), preferred_element_type=F32)


def swap_blocks(a, b):
    return jnp.concatenate(
        [
            jnp.concatenate([a[:, :HALF], b[:, :HALF]], axis=1),
            jnp.concatenate([a[:, HALF:], b[:, HALF:]], axis=1),
        ],
        axis=0,
    )


def place():
    region, group = lax.axis_index("region"), lax.axis_index("group")
    core = lax.rem(region, 2)
    z = lax.rem(region // 2, 4)
    y = (group // 4) * 2 + region // 8
    x = lax.rem(group, 4)
    turned = ((x, y), (y, x), (z, z))
    return tuple(a + core * (b - a) for a, b in turned), core


def device(at, core, counted):
    a, b, c = at
    x, y, z = a + counted * (b - a), b + counted * (a - b), c
    return ((lax.rem(y, 2) * 4 + z) * 2 + core, (y // 2) * 4 + x)


def step_kernel(
    pos_ref, count_ref, object_hbm, probe_hbm, diff_hbm,
    out_ref, arrived, new_ref,
    ext, win, far, wanted, probe, pgrad, cov, go, hx, strips, direct, turned, perm, diff,
    spill, mate, total, factor, covered, *rest,
):
    got, pieces, local_sem, send_sem, recv_sem = rest
    me, core = place()
    regions = lax.axis_size("region")
    region, group = lax.axis_index("region"), lax.axis_index("group")
    sibling = device(me, 1 - core, core)
    up = (lax.rem(region + 1, regions), group)
    down = (lax.rem(region + regions - 1, regions), group)
    own = object_hbm.shape[0]
    edge = spill.shape[0]

    loads = [
        pltpu.make_async_copy(src, dst, local_sem.at[n])
        for n, (src, dst) in enumerate(
            [
                (object_hbm, ext.at[:own]),
                (diff_hbm, diff),
                (probe_hbm, probe),
            ]
        )
    ]
    def shift(n, distance):
        return lax.rem(me[n] + distance, 4)

    plane_peers = [(shift(0, i), shift(1, j)) for i, j in OTHERS]
    plane_devices = [device((p, q, me[2]), core, core) for p, q in plane_peers]
    last_devices = [device((me[0], me[1], shift(2, d)), core, core) for d in (1, 2, 3)]

    barrier = pltpu.get_barrier_semaphore()
    partners = [sibling, up, down, *plane_devices, *last_devices]
    for partner in partners:
        pl.semaphore_signal(barrier, inc=1, device_id=partner, device_id_type=MESH)
    for load in loads:
        load.start()
    pl.semaphore_wait(barrier, len(partners))

    builders = {}

    def remote(key, build=None):
        if build is not None:
            builders[key] = (len(builders), build)
        n, build = builders[key]
        src, dst, to = build()
        return pltpu.make_async_remote_copy(
            src_ref=src, dst_ref=dst, send_sem=send_sem.at[n], recv_sem=recv_sem.at[n],
            device_id=to, device_id_type=MESH,
        )

    def send(key, build):
        remote(key, build).start()

    def arrive(key):
        remote(key).wait_recv()

    send("halo", lambda: (object_hbm.at[:edge], ext.at[own:], down))

    def result(u):
        return new_ref.at[2 * u + core]

    def start_core(u):
        send(
            ("core", u),
            lambda: (cov if u == COVERAGE else pgrad.at[2 * u + 1 - core], mate.at[u], sibling),
        )

    def start_plane(u):
        arrive(("core", u))
        total[u] = (cov[...] if u == COVERAGE else pgrad[2 * u + core]) + mate[u]
        for n, (p, q) in enumerate(plane_peers):
            send(
                ("plane", u, n),
                lambda n=n, p=p, q=q: (total.at[u, p, q], got.at[u, n], plane_devices[n]),
            )

    def start_last(u):
        for n in range(len(OTHERS)):
            arrive(("plane", u, n))
        value = total[u, me[0], me[1]]
        for n in range(len(OTHERS)):
            value = value + got[u, n]
        pieces[u, me[2]] = value
        for n in range(3):
            send(
                ("last", u, n),
                lambda n=n: (pieces.at[u, me[2]], pieces.at[u, me[2]], last_devices[n]),
            )

    def finish(u):
        for n in range(3):
            arrive(("last", u, n))
        reduced = (pieces[u, 0] + pieces[u, 1]) + (pieces[u, 2] + pieces[u, 3])
        if u == COVERAGE:
            covered[...] = reduced + 1e-06
            return
        here = (2 * u + core, me[0], me[1])
        new_ref[here] = probe[here] - reduced / covered[...]
        to = range(len(OTHERS)) if u == MODES - 1 else [OTHERS.index((0, d)) for d in (1, 2, 3)]
        for n in to:
            send(
                ("back", u, n),
                lambda n=n: (
                    result(u).at[me[0], me[1]],
                    result(u).at[me[0], me[1]],
                    plane_devices[n],
                ),
            )

    def relay(u):
        for d in (1, 2, 3):
            arrive(("back", u, OTHERS.index((0, d))))
        for d in (1, 2, 3):
            n = OTHERS.index((d, 0))
            send(
                ("back", u, n),
                lambda n=n: (result(u).at[me[0]], result(u).at[me[0]], plane_devices[n]),
            )

    def collect(u):
        to = range(len(OTHERS)) if u == MODES - 1 else [OTHERS.index((d, 0)) for d in (1, 2, 3)]
        for n in to:
            arrive(("back", u, n))

    def hand_over(u):
        collect(u)
        send(("over", u), lambda: (result(u), result(u), sibling))

    def tiles_of(x):
        return x.reshape(4, 4, 2, 8, HALF)

    pgrad[...] = jnp.zeros_like(pgrad)
    cov[...] = jnp.zeros_like(cov)
    go[...] = jnp.zeros_like(go)
    hx[:, :PAD] = jnp.zeros((SLOTS, PAD, 8, HALF), F32)
    hx[:, PAD + 256 :] = jnp.zeros((SLOTS, PAD, 8, HALF), F32)
    make_tables(direct, turned, perm)
    loads[1].wait()

    def prepare(s, carry):
        high, low = parts_of(
            jnp.sqrt(
                jnp.concatenate([diff[s, :, h].reshape(256, HALF) for h in (0, 1)], axis=1)
            )
        )
        root = jnp.dot(high, perm[...], preferred_element_type=F32) + jnp.dot(
            low, perm[...], preferred_element_type=F32
        )
        for h in (0, 1):
            wanted[s, h] = root[:, h * HALF : (h + 1) * HALF]
        return carry

    lax.fori_loop(0, SLOTS, prepare, 0)

    loads[2].wait()

    def probe_at(m, c):
        return jnp.concatenate(
            [probe[2 * m + c, :, :, :, h].reshape(256, HALF) for h in (0, 1)], axis=1
        )

    power = jnp.zeros((256, 256), F32)
    for m in range(MODES):
        pr, pi = probe_at(m, 0), probe_at(m, 1)
        power = power + pr * pr + pi * pi
    peak = jnp.max(power)
    loads[0].wait()
    arrive("halo")

    base = region * own

    def spot(s):
        return jnp.clip(pos_ref[0, s] - base, 0, own - 1), pos_ref[1, s]

    def pick_columns(col, shape, wide):
        at = lax.broadcasted_iota(jnp.int32, shape, wide)
        narrow = lax.broadcasted_iota(jnp.int32, shape, 1 - wide)
        return jnp.where(at - narrow == col, 1.0, 0.0).astype(BF16)

    def live(s, shape):
        return jnp.where(jnp.full(shape, s, jnp.int32) < count_ref[0, 0], 1.0, 0.0).astype(F32)

    def cut(s, carry):
        row, col = spot(s)
        strips[...] = ext[pl.ds(row, 256)].reshape(256 * 8, HALF)
        pick = pick_columns(col, (512, 256), 0)
        for c in (0, 1):
            strip = jnp.concatenate(
                [strips[pl.ds(2 * k + c, 256, stride=8), :] for k in range(4)], axis=1
            )
            high, low = parts_of(strip)
            win[s, c] = jnp.dot(high, pick, preferred_element_type=F32) + jnp.dot(
                low, pick, preferred_element_type=F32
            )
        wr, wi = win[s, 0], win[s, 1]
        power = live(s, (256, 256)) * (wr * wr + wi * wi)
        for h in (0, 1):
            cov[:, :, :, h] += tiles_of(power[:, h * HALF : (h + 1) * HALF])
        return carry

    lax.fori_loop(0, SLOTS, cut, 0)
    start_core(COVERAGE)

    def forward(s, carry):
        @pl.when(s == 1)
        def _():
            start_plane(COVERAGE)

        @pl.when(s == 3)
        def _():
            start_last(COVERAGE)

        wr, wi = win[s, 0], win[s, 1]
        for m in range(MODES):
            pr, pi = probe_at(m, 0), probe_at(m, 1)
            er = pr * wr - pi * wi
            ei = pr * wi + pi * wr
            a = jnp.concatenate([er[:, :HALF] + er[:, HALF:], ei[:, :HALF] + ei[:, HALF:]], axis=1)
            b = jnp.concatenate([er[:, :HALF] - er[:, HALF:], ei[:, :HALF] - ei[:, HALF:]], axis=1)
            ye = mul_right(a, direct, 0)
            yo = mul_right(b, direct, 1)
            plus = swap_blocks(ye[:HALF] + ye[HALF:], yo[:HALF] + yo[HALF:])
            minus = swap_blocks(ye[:HALF] - ye[HALF:], yo[:HALF] - yo[HALF:])
            far[s, m, 0] = mul_left(turned, 0, plus)
            far[s, m, 1] = mul_left(turned, 1, minus)
        for p in (0, 1):
            intensity = jnp.zeros((HALF, 256), F32)
            for m in range(MODES):
                fr, fi = far[s, m, p, :HALF], far[s, m, p, HALF:]
                intensity = intensity + (fr * fr + fi * fi)
            root = jnp.concatenate(
                [wanted[s, h, pl.ds(p, HALF, stride=2), :] for h in (0, 1)], axis=1
            )
            factor[s, p] = live(s, (HALF, 256)) * (
                1.0 - root / jnp.sqrt(jnp.maximum(intensity, 1.0))
            )
        return carry

    lax.fori_loop(0, SLOTS, forward, 0)

    def inverse(m, slots):
        for s in slots:
            wr, wi = win[s, 0], win[s, 1]
            e, o = [
                mul_left(
                    direct,
                    p,
                    far[s, m, p] * jnp.concatenate([factor[s, p], factor[s, p]], axis=0),
                )
                for p in (0, 1)
            ]
            top, bottom = e + o, e - o
            ae, ao = [
                jnp.concatenate(
                    [
                        jnp.concatenate([x[:HALF, at : at + HALF], x[HALF:, at : at + HALF]], axis=1)
                        for x in (top, bottom)
                    ],
                    axis=0,
                )
                for at in (0, HALF)
            ]
            e = mul_right(ae, turned, 0)
            o = mul_right(ao, turned, 1)
            left, right = e + o, e - o
            cr = jnp.concatenate([left[:, :HALF], right[:, :HALF]], axis=1)
            ci = jnp.concatenate([left[:, HALF:], right[:, HALF:]], axis=1)
            pr, pi = probe_at(m, 0), probe_at(m, 1)
            go[s, 0] += pr * cr + pi * ci
            go[s, 1] += pr * ci - pi * cr
            for c, g in enumerate((wr * cr + wi * ci, wr * ci - wi * cr)):
                for h in (0, 1):
                    pgrad[2 * m + c, :, :, :, h] += tiles_of(g[:, h * HALF : (h + 1) * HALF])

    for m in range(MODES):

        def of_mode(i, carry, m=m):
            if m == 3:

                @pl.when(i == 0)
                def _():
                    start_last(0)

            @pl.when(i == 1)
            def _():
                if m == 0:
                    finish(COVERAGE)
                else:
                    start_plane(m - 1)

            inverse(m, (2 * i, 2 * i + 1))
            return carry

        lax.fori_loop(0, SLOTS // 2, of_mode, 0)
        start_core(m)

    def turn(s, carry):
        pick = pick_columns(spot(s)[1], (256, 512), 1)
        for c in (0, 1):
            high, low = parts_of(go[s, c])
            strip = jnp.dot(high, pick, preferred_element_type=F32) + jnp.dot(
                low, pick, preferred_element_type=F32
            )
            for k in range(4):
                strips[pl.ds(2 * k + c, 256, stride=8), :] = strip[:, k * HALF : (k + 1) * HALF]
        hx[s, PAD : PAD + 256] = strips[...].reshape(256, 8, HALF)
        return carry

    lax.fori_loop(0, SLOTS, turn, 0)
    start_plane(3)
    finish(0)

    def added(block):
        out = None
        for s in range(SLOTS):
            start = jnp.clip(block * PAD - spot(s)[0] + PAD, 0, PAD + 256)
            piece = hx[s, pl.ds(start, PAD)]
            out = piece if out is None else out + piece
        return out / peak

    blocks = own // PAD

    def below(i, carry):
        spill[pl.ds(i * PAD, PAD)] = added(blocks + i)
        return carry

    lax.fori_loop(0, edge // PAD, below, 0)
    send("spill", lambda: (spill, arrived, up))
    start_last(1)
    relay(0)

    def within(i, carry):
        at = pl.ds(i * PAD, PAD)
        out_ref[at] = ext[at] - added(i)
        return carry

    lax.fori_loop(0, blocks, within, 0)
    start_last(2)
    finish(1)
    start_last(3)
    finish(2)
    finish(3)
    relay(1)
    relay(2)
    for u in range(MODES):
        hand_over(u)
    arrive("spill")
    for u in range(MODES):
        arrive(("over", u))
    for key in builders:
        remote(key).wait_send()


def tiled(planes):
    return (
        planes.reshape(-1, 32, 8, 2, HALF)
        .transpose(0, 1, 3, 2, 4)
        .reshape(-1, *PLANE)
    )


def untiled(tiles, shape):
    return tiles.reshape(-1, 32, 2, 8, HALF).transpose(0, 1, 3, 2, 4).reshape(shape)


def step(positions, slot_counts, view, probe, diffraction):
    smem = pl.BlockSpec(memory_space=pltpu.SMEM)
    hbm = pl.BlockSpec(memory_space=pltpu.HBM)
    vmem = pl.BlockSpec(memory_space=pltpu.VMEM)
    own = view.shape[0]
    diffraction = diffraction.reshape(SLOTS, 32, 8, 2, HALF).transpose(0, 1, 3, 2, 4)
    edge = own // 2
    copies = 2 + (MODES + 1) * (1 + 15 + 3 + 15) + MODES
    return pl.pallas_call(
        step_kernel,
        out_shape=(
            jax.ShapeDtypeStruct(view.shape, F32),
            jax.ShapeDtypeStruct((edge, 8, HALF), F32),
            jax.ShapeDtypeStruct((8, *PLANE), F32),
        ),
        in_specs=[smem] * 2 + [hbm] * 3,
        out_specs=[vmem] * 3,
        scratch_shapes=[
            pltpu.VMEM((own + edge, 8, HALF), F32),
            pltpu.VMEM((SLOTS, 2, 256, 256), F32),
            pltpu.VMEM((SLOTS, MODES, 2, 256, 256), F32),
            pltpu.VMEM((SLOTS, 2, 256, HALF), F32),
            pltpu.VMEM((8, *PLANE), F32),
            pltpu.VMEM((8, *PLANE), F32),
            pltpu.VMEM(PLANE, F32),
            pltpu.VMEM((SLOTS, 2, 256, 256), F32),
            pltpu.VMEM((SLOTS, 256 + 2 * PAD, 8, HALF), F32),
            pltpu.VMEM((256 * 8, HALF), F32),
            pltpu.VMEM((2, 2, 256, 256), BF16),
            pltpu.VMEM((2, 2, 256, 256), BF16),
            pltpu.VMEM((256, 256), BF16),
            pltpu.VMEM(diffraction.shape, F32),
            pltpu.VMEM((edge, 8, HALF), F32),
            pltpu.VMEM((5, *PLANE), F32),
            pltpu.VMEM((5, *PLANE), F32),
            pltpu.VMEM((SLOTS, 2, HALF, 256), F32),
            pltpu.VMEM(PLANE[2:], F32),
            pltpu.VMEM((5, len(OTHERS), *PLANE[2:]), F32),
            pltpu.VMEM((5, 4, *PLANE[2:]), F32),
            pltpu.SemaphoreType.DMA((3,)),
            pltpu.SemaphoreType.DMA((copies,)),
            pltpu.SemaphoreType.DMA((copies,)),
        ],
        compiler_params=pltpu.CompilerParams(
            vmem_limit_bytes=46 << 20, collective_id=0, has_side_effects=True
        ),
        name="step",
    )(positions, slot_counts, view, tiled(probe), diffraction)


def on_device(object_slab, probe, diffraction, positions, slot_counts):
    tile_rows, _, tile_cols = object_slab.shape
    blocks = tile_cols // HALF
    view = (
        object_slab.reshape(tile_rows, 2, blocks, HALF)
        .transpose(0, 2, 1, 3)
        .reshape(tile_rows, blocks * 2, HALF)
    )
    view, arrived, new = step(positions.T, slot_counts, view, probe, diffraction)
    edge = arrived.shape[0]
    view = jnp.concatenate([view[:edge] - arrived, view[edge:]], axis=0)
    obj = (
        view.reshape(tile_rows, blocks, 2, HALF)
        .transpose(0, 2, 1, 3)
        .reshape(tile_rows, 2, tile_cols)
    )
    return (obj, untiled(new, probe.shape))


def solution(mesh):
    placed = (
        P("region", None, "group"),
        P(),
        P(("region", "group"), None, None),
        P(("region", "group"), None),
        P("group", "region"),
    )
    return jax.shard_map(
        on_device,
        mesh=mesh,
        in_specs=placed,
        out_specs=(P("region", None, "group"), P()),
        check_vma=False,
    )
```

```python
import math

import jax
import jax.numpy as jnp
from jax import lax
from jax.experimental import pallas as pl
from jax.experimental.pallas import tpu as pltpu
from jax.sharding import PartitionSpec as P

F32 = jnp.float32
BF16 = jnp.bfloat16
HALF = 128
SLOTS = 4
MODES = 4
PAD = 64
MESH = pl.DeviceIdType.MESH
PLANE = (4, 4, 2, 2, 8, HALF)
COVERAGE = MODES
OTHERS = tuple((i, j) for i in range(4) for j in range(4) if (i, j) != (0, 0))


def parts_of(x):
    high = x.astype(BF16)
    low = (x - high.astype(F32)).astype(BF16)
    return high, low


def make_tables(direct, turned, perm):
    rows = lax.broadcasted_iota(jnp.int32, (HALF, HALF), 0)
    cols = lax.broadcasted_iota(jnp.int32, (HALF, HALF), 1)
    for parity in (0, 1):
        for table, n, k in ((direct, rows, cols), (turned, cols, rows)):
            angle = lax.rem(n * (2 * k + parity), 256).astype(F32) * (2.0 * math.pi / 256)
            re, im = jnp.cos(angle) / 16, -jnp.sin(angle) / 16
            above, below = (im, -im) if table is direct else (-im, im)
            full = jnp.concatenate(
                [jnp.concatenate([re, above], axis=1), jnp.concatenate([below, re], axis=1)],
                axis=0,
            )
            table[parity, 0], table[parity, 1] = parts_of(full)
    old = lax.broadcasted_iota(jnp.int32, (256, 256), 0)
    new = lax.broadcasted_iota(jnp.int32, (256, 256), 1)
    perm[...] = jnp.where(lax.rem(old, 2) * HALF + old // 2 == new, 1.0, 0.0).astype(BF16)


def mul_right(x, table, p):
    high, low = parts_of(x)
    table = jnp.concatenate([table[p, 0], table[p, 0], table[p, 1]], axis=0)
    return jnp.dot(jnp.concatenate([high, low, high], axis=1), table, preferred_element_type=F32)


def mul_left(table, p, x):
    high, low = parts_of(x)
    table = jnp.concatenate([table[p, 0], table[p, 0], table[p, 1]], axis=1)
    return jnp.dot(table, jnp.concatenate([high, low, high], axis=0), preferred_element_type=F32)


def swap_blocks(a, b):
    return jnp.concatenate(
        [
            jnp.concatenate([a[:, :HALF], b[:, :HALF]], axis=1),
            jnp.concatenate([a[:, HALF:], b[:, HALF:]], axis=1),
        ],
        axis=0,
    )


def place():
    region, group = lax.axis_index("region"), lax.axis_index("group")
    core = lax.rem(region, 2)
    z = lax.rem(region // 2, 4)
    y = (group // 4) * 2 + region // 8
    x = lax.rem(group, 4)
    turned = ((x, y), (y, z), (z, x))
    return tuple(a + core * (b - a) for a, b in turned), core


def device(at, core, counted):
    a, b, c = at
    x, y, z = a + counted * (c - a), b + counted * (a - b), c + counted * (b - c)
    return ((lax.rem(y, 2) * 4 + z) * 2 + core, (y // 2) * 4 + x)


def step_kernel(
    pos_ref, count_ref, object_hbm, probe_hbm, diff_hbm,
    out_ref, arrived, new_ref,
    ext, win, far, wanted, probe, pgrad, cov, go, hx, strips, direct, turned, perm, diff,
    spill, mate, total, factor, covered, *rest,
):
    got, pieces, row_got, row_sum, local_sem, send_sem, recv_sem = rest
    me, core = place()
    regions = lax.axis_size("region")
    region, group = lax.axis_index("region"), lax.axis_index("group")
    sibling = device(me, 1 - core, core)
    up = (lax.rem(region + 1, regions), group)
    down = (lax.rem(region + regions - 1, regions), group)
    own = object_hbm.shape[0]
    edge = spill.shape[0]

    loads = [
        pltpu.make_async_copy(src, dst, local_sem.at[n])
        for n, (src, dst) in enumerate(
            [
                (object_hbm, ext.at[:own]),
                (diff_hbm, diff),
                (probe_hbm, probe),
            ]
        )
    ]
    def shift(n, distance):
        return lax.rem(me[n] + distance, 4)

    plane_peers = [(shift(0, i), shift(1, j)) for i, j in OTHERS]
    plane_devices = [device((p, q, me[2]), core, core) for p, q in plane_peers]
    last_devices = [device((me[0], me[1], shift(2, d)), core, core) for d in (1, 2, 3)]

    barrier = pltpu.get_barrier_semaphore()
    partners = [sibling, up, down, *plane_devices, *last_devices]
    for partner in partners:
        pl.semaphore_signal(barrier, inc=1, device_id=partner, device_id_type=MESH)
    for load in loads:
        load.start()
    pl.semaphore_wait(barrier, len(partners))

    builders = {}

    def remote(key, build=None):
        if build is not None:
            builders[key] = (len(builders), build)
        n, build = builders[key]
        src, dst, to = build()
        return pltpu.make_async_remote_copy(
            src_ref=src, dst_ref=dst, send_sem=send_sem.at[n], recv_sem=recv_sem.at[n],
            device_id=to, device_id_type=MESH,
        )

    def send(key, build):
        remote(key, build).start()

    def arrive(key):
        remote(key).wait_recv()

    send("halo", lambda: (object_hbm.at[:edge], ext.at[own:], down))

    def result(u):
        return new_ref.at[2 * u + core]

    def start_core(u):
        send(
            ("core", u),
            lambda: (cov if u == COVERAGE else pgrad.at[2 * u + 1 - core], mate.at[u], sibling),
        )

    def join(u):
        arrive(("core", u))
        total[u] = (cov[...] if u == COVERAGE else pgrad[2 * u + core]) + mate[u]

    def start_plane(u):
        join(u)
        for n, (p, q) in enumerate(plane_peers):
            send(
                ("plane", u, n),
                lambda n=n, p=p, q=q: (total.at[u, p, q], got.at[u, n], plane_devices[n]),
            )

    def start_row():
        join(COVERAGE)
        for d in (1, 2, 3):
            n = OTHERS.index((d, 0))
            send(
                ("row", d),
                lambda n=n, d=d: (
                    total.at[COVERAGE, plane_peers[n][0]],
                    row_got.at[d - 1],
                    plane_devices[n],
                ),
            )

    def start_column():
        for d in (1, 2, 3):
            arrive(("row", d))
        row_sum[...] = total[COVERAGE, me[0]] + row_got[0] + row_got[1] + row_got[2]
        for d in (1, 2, 3):
            n = OTHERS.index((0, d))
            send(
                ("plane", COVERAGE, d - 1),
                lambda n=n, d=d: (
                    row_sum.at[plane_peers[n][1]],
                    got.at[COVERAGE, d - 1],
                    plane_devices[n],
                ),
            )

    def start_last(u):
        count = 3 if u == COVERAGE else len(OTHERS)
        for n in range(count):
            arrive(("plane", u, n))
        value = row_sum[me[1]] if u == COVERAGE else total[u, me[0], me[1]]
        for n in range(count):
            value = value + got[u, n]
        pieces[u, me[2]] = value
        for n in range(3):
            send(
                ("last", u, n),
                lambda n=n: (pieces.at[u, me[2]], pieces.at[u, me[2]], last_devices[n]),
            )

    def finish(u):
        for n in range(3):
            arrive(("last", u, n))
        reduced = (pieces[u, 0] + pieces[u, 1]) + (pieces[u, 2] + pieces[u, 3])
        if u == COVERAGE:
            covered[...] = reduced + 1e-06
            return
        here = (2 * u + core, me[0], me[1])
        new_ref[here] = probe[here] - reduced / covered[...]
        to = range(len(OTHERS)) if u == MODES - 1 else [OTHERS.index((0, d)) for d in (1, 2, 3)]
        for n in to:
            send(
                ("back", u, n),
                lambda n=n: (
                    result(u).at[me[0], me[1]],
                    result(u).at[me[0], me[1]],
                    plane_devices[n],
                ),
            )

    def relay(u):
        for d in (1, 2, 3):
            arrive(("back", u, OTHERS.index((0, d))))
        for d in (1, 2, 3):
            n = OTHERS.index((d, 0))
            send(
                ("back", u, n),
                lambda n=n: (result(u).at[me[0]], result(u).at[me[0]], plane_devices[n]),
            )

    def collect(u):
        to = range(len(OTHERS)) if u == MODES - 1 else [OTHERS.index((d, 0)) for d in (1, 2, 3)]
        for n in to:
            arrive(("back", u, n))

    def hand_over(u):
        collect(u)
        send(("over", u), lambda: (result(u), result(u), sibling))

    def tiles_of(x):
        return x.reshape(4, 4, 2, 8, HALF)

    pgrad[...] = jnp.zeros_like(pgrad)
    cov[...] = jnp.zeros_like(cov)
    go[...] = jnp.zeros_like(go)
    hx[:, :PAD] = jnp.zeros((SLOTS, PAD, 8, HALF), F32)
    hx[:, PAD + 256 :] = jnp.zeros((SLOTS, PAD, 8, HALF), F32)
    make_tables(direct, turned, perm)
    loads[1].wait()

    def prepare(s, carry):
        high, low = parts_of(
            jnp.sqrt(
                jnp.concatenate([diff[s, :, h].reshape(256, HALF) for h in (0, 1)], axis=1)
            )
        )
        root = jnp.dot(high, perm[...], preferred_element_type=F32) + jnp.dot(
            low, perm[...], preferred_element_type=F32
        )
        for h in (0, 1):
            wanted[s, h] = root[:, h * HALF : (h + 1) * HALF]
        return carry

    lax.fori_loop(0, SLOTS, prepare, 0)

    loads[2].wait()

    def probe_at(m, c):
        return jnp.concatenate(
            [probe[2 * m + c, :, :, :, h].reshape(256, HALF) for h in (0, 1)], axis=1
        )

    power = jnp.zeros((256, 256), F32)
    for m in range(MODES):
        pr, pi = probe_at(m, 0), probe_at(m, 1)
        power = power + pr * pr + pi * pi
    peak = jnp.max(power)
    loads[0].wait()
    arrive("halo")

    base = region * own

    def spot(s):
        return jnp.clip(pos_ref[0, s] - base, 0, own - 1), pos_ref[1, s]

    def pick_columns(col, shape, wide):
        at = lax.broadcasted_iota(jnp.int32, shape, wide)
        narrow = lax.broadcasted_iota(jnp.int32, shape, 1 - wide)
        return jnp.where(at - narrow == col, 1.0, 0.0).astype(BF16)

    def live(s, shape):
        return jnp.where(jnp.full(shape, s, jnp.int32) < count_ref[0, 0], 1.0, 0.0).astype(F32)

    def cut(s, carry):
        row, col = spot(s)
        strips[...] = ext[pl.ds(row, 256)].reshape(256 * 8, HALF)
        pick = pick_columns(col, (512, 256), 0)
        for c in (0, 1):
            strip = jnp.concatenate(
                [strips[pl.ds(2 * k + c, 256, stride=8), :] for k in range(4)], axis=1
            )
            high, low = parts_of(strip)
            win[s, c] = jnp.dot(high, pick, preferred_element_type=F32) + jnp.dot(
                low, pick, preferred_element_type=F32
            )
        wr, wi = win[s, 0], win[s, 1]
        power = live(s, (256, 256)) * (wr * wr + wi * wi)
        for h in (0, 1):
            cov[:, :, :, h] += tiles_of(power[:, h * HALF : (h + 1) * HALF])
        return carry

    lax.fori_loop(0, SLOTS, cut, 0)
    start_core(COVERAGE)

    def forward(s, carry):
        @pl.when(s == 1)
        def _():
            start_row()

        @pl.when(s == 2)
        def _():
            start_column()

        @pl.when(s == 3)
        def _():
            start_last(COVERAGE)

        wr, wi = win[s, 0], win[s, 1]
        for m in range(MODES):
            pr, pi = probe_at(m, 0), probe_at(m, 1)
            er = pr * wr - pi * wi
            ei = pr * wi + pi * wr
            a = jnp.concatenate([er[:, :HALF] + er[:, HALF:], ei[:, :HALF] + ei[:, HALF:]], axis=1)
            b = jnp.concatenate([er[:, :HALF] - er[:, HALF:], ei[:, :HALF] - ei[:, HALF:]], axis=1)
            ye = mul_right(a, direct, 0)
            yo = mul_right(b, direct, 1)
            plus = swap_blocks(ye[:HALF] + ye[HALF:], yo[:HALF] + yo[HALF:])
            minus = swap_blocks(ye[:HALF] - ye[HALF:], yo[:HALF] - yo[HALF:])
            far[s, m, 0] = mul_left(turned, 0, plus)
            far[s, m, 1] = mul_left(turned, 1, minus)
        for p in (0, 1):
            intensity = jnp.zeros((HALF, 256), F32)
            for m in range(MODES):
                fr, fi = far[s, m, p, :HALF], far[s, m, p, HALF:]
                intensity = intensity + (fr * fr + fi * fi)
            root = jnp.concatenate(
                [wanted[s, h, pl.ds(p, HALF, stride=2), :] for h in (0, 1)], axis=1
            )
            factor[s, p] = live(s, (HALF, 256)) * (
                1.0 - root / jnp.sqrt(jnp.maximum(intensity, 1.0))
            )
        return carry

    lax.fori_loop(0, SLOTS, forward, 0)

    def inverse(m, slots):
        for s in slots:
            wr, wi = win[s, 0], win[s, 1]
            e, o = [
                mul_left(
                    direct,
                    p,
                    far[s, m, p] * jnp.concatenate([factor[s, p], factor[s, p]], axis=0),
                )
                for p in (0, 1)
            ]
            top, bottom = e + o, e - o
            ae, ao = [
                jnp.concatenate(
                    [
                        jnp.concatenate([x[:HALF, at : at + HALF], x[HALF:, at : at + HALF]], axis=1)
                        for x in (top, bottom)
                    ],
                    axis=0,
                )
                for at in (0, HALF)
            ]
            e = mul_right(ae, turned, 0)
            o = mul_right(ao, turned, 1)
            left, right = e + o, e - o
            cr = jnp.concatenate([left[:, :HALF], right[:, :HALF]], axis=1)
            ci = jnp.concatenate([left[:, HALF:], right[:, HALF:]], axis=1)
            pr, pi = probe_at(m, 0), probe_at(m, 1)
            go[s, 0] += pr * cr + pi * ci
            go[s, 1] += pr * ci - pi * cr
            for c, g in enumerate((wr * cr + wi * ci, wr * ci - wi * cr)):
                for h in (0, 1):
                    pgrad[2 * m + c, :, :, :, h] += tiles_of(g[:, h * HALF : (h + 1) * HALF])

    for m in range(MODES):

        def of_mode(i, carry, m=m):
            if m == 3:

                @pl.when(i == 0)
                def _():
                    start_last(0)

            @pl.when(i == 1)
            def _():
                if m == 0:
                    finish(COVERAGE)
                else:
                    start_plane(m - 1)

            inverse(m, (2 * i, 2 * i + 1))
            return carry

        lax.fori_loop(0, SLOTS // 2, of_mode, 0)
        start_core(m)

    finish(0)

    def turn(s, carry):
        pick = pick_columns(spot(s)[1], (256, 512), 1)
        for c in (0, 1):
            high, low = parts_of(go[s, c])
            strip = jnp.dot(high, pick, preferred_element_type=F32) + jnp.dot(
                low, pick, preferred_element_type=F32
            )
            for k in range(4):
                strips[pl.ds(2 * k + c, 256, stride=8), :] = strip[:, k * HALF : (k + 1) * HALF]
        hx[s, PAD : PAD + 256] = strips[...].reshape(256, 8, HALF)
        return carry

    lax.fori_loop(0, SLOTS // 2, turn, 0)
    start_plane(3)
    lax.fori_loop(SLOTS // 2, SLOTS, turn, 0)
    start_last(1)

    def added(block):
        out = None
        for s in range(SLOTS):
            start = jnp.clip(block * PAD - spot(s)[0] + PAD, 0, PAD + 256)
            piece = hx[s, pl.ds(start, PAD)]
            out = piece if out is None else out + piece
        return out / peak

    blocks = own // PAD

    def below(i, carry):
        spill[pl.ds(i * PAD, PAD)] = added(blocks + i)
        return carry

    lax.fori_loop(0, edge // PAD, below, 0)
    send("spill", lambda: (spill, arrived, up))
    relay(0)

    def within(i, carry):
        at = pl.ds(i * PAD, PAD)
        out_ref[at] = ext[at] - added(i)
        return carry

    lax.fori_loop(0, blocks, within, 0)
    start_last(2)
    finish(1)
    start_last(3)
    finish(2)
    relay(1)
    finish(3)
    relay(2)
    for u in range(MODES):
        hand_over(u)
    arrive("spill")
    for u in range(MODES):
        arrive(("over", u))
    for key in builders:
        remote(key).wait_send()


def tiled(planes):
    return (
        planes.reshape(-1, 32, 8, 2, HALF)
        .transpose(0, 1, 3, 2, 4)
        .reshape(-1, *PLANE)
    )


def untiled(tiles, shape):
    return tiles.reshape(-1, 32, 2, 8, HALF).transpose(0, 1, 3, 2, 4).reshape(shape)


def step(positions, slot_counts, view, probe, diffraction):
    smem = pl.BlockSpec(memory_space=pltpu.SMEM)
    hbm = pl.BlockSpec(memory_space=pltpu.HBM)
    vmem = pl.BlockSpec(memory_space=pltpu.VMEM)
    own = view.shape[0]
    diffraction = diffraction.reshape(SLOTS, 32, 8, 2, HALF).transpose(0, 1, 3, 2, 4)
    edge = own // 2
    copies = 2 + (MODES + 1) * (1 + 15 + 3 + 15) + MODES
    return pl.pallas_call(
        step_kernel,
        out_shape=(
            jax.ShapeDtypeStruct(view.shape, F32),
            jax.ShapeDtypeStruct((edge, 8, HALF), F32),
            jax.ShapeDtypeStruct((8, *PLANE), F32),
        ),
        in_specs=[smem] * 2 + [hbm] * 3,
        out_specs=[vmem] * 3,
        scratch_shapes=[
            pltpu.VMEM((own + edge, 8, HALF), F32),
            pltpu.VMEM((SLOTS, 2, 256, 256), F32),
            pltpu.VMEM((SLOTS, MODES, 2, 256, 256), F32),
            pltpu.VMEM((SLOTS, 2, 256, HALF), F32),
            pltpu.VMEM((8, *PLANE), F32),
            pltpu.VMEM((8, *PLANE), F32),
            pltpu.VMEM(PLANE, F32),
            pltpu.VMEM((SLOTS, 2, 256, 256), F32),
            pltpu.VMEM((SLOTS, 256 + 2 * PAD, 8, HALF), F32),
            pltpu.VMEM((256 * 8, HALF), F32),
            pltpu.VMEM((2, 2, 256, 256), BF16),
            pltpu.VMEM((2, 2, 256, 256), BF16),
            pltpu.VMEM((256, 256), BF16),
            pltpu.VMEM(diffraction.shape, F32),
            pltpu.VMEM((edge, 8, HALF), F32),
            pltpu.VMEM((5, *PLANE), F32),
            pltpu.VMEM((5, *PLANE), F32),
            pltpu.VMEM((SLOTS, 2, HALF, 256), F32),
            pltpu.VMEM(PLANE[2:], F32),
            pltpu.VMEM((5, len(OTHERS), *PLANE[2:]), F32),
            pltpu.VMEM((5, 4, *PLANE[2:]), F32),
            pltpu.VMEM((3, *PLANE[1:]), F32),
            pltpu.VMEM(PLANE[1:], F32),
            pltpu.SemaphoreType.DMA((3,)),
            pltpu.SemaphoreType.DMA((copies,)),
            pltpu.SemaphoreType.DMA((copies,)),
        ],
        compiler_params=pltpu.CompilerParams(
            vmem_limit_bytes=46 << 20, collective_id=0, has_side_effects=True
        ),
        name="step",
    )(positions, slot_counts, view, tiled(probe), diffraction)


def on_device(object_slab, probe, diffraction, positions, slot_counts):
    tile_rows, _, tile_cols = object_slab.shape
    blocks = tile_cols // HALF
    view = (
        object_slab.reshape(tile_rows, 2, blocks, HALF)
        .transpose(0, 2, 1, 3)
        .reshape(tile_rows, blocks * 2, HALF)
    )
    view, arrived, new = step(positions.T, slot_counts, view, probe, diffraction)
    edge = arrived.shape[0]
    view = jnp.concatenate([view[:edge] - arrived, view[edge:]], axis=0)
    obj = (
        view.reshape(tile_rows, blocks, 2, HALF)
        .transpose(0, 2, 1, 3)
        .reshape(tile_rows, 2, tile_cols)
    )
    return (obj, untiled(new, probe.shape))


def solution(mesh):
    placed = (
        P("region", None, "group"),
        P(),
        P(("region", "group"), None, None),
        P(("region", "group"), None),
        P("group", "region"),
    )
    return jax.shard_map(
        on_device,
        mesh=mesh,
        in_specs=placed,
        out_specs=(P("region", None, "group"), P()),
        check_vma=False,
    )
```

```python
import math

import jax
import jax.numpy as jnp
from jax import lax
from jax.experimental import pallas as pl
from jax.experimental.pallas import tpu as pltpu
from jax.sharding import PartitionSpec as P

F32 = jnp.float32
BF16 = jnp.bfloat16
HALF = 128
SLOTS = 4
MODES = 4
PAD = 64
MESH = pl.DeviceIdType.MESH
PLANE = (4, 4, 2, 2, 8, HALF)
COVERAGE = MODES
OTHERS = tuple((i, j) for i in range(4) for j in range(4) if (i, j) != (0, 0))


def parts_of(x):
    high = x.astype(BF16)
    low = (x - high.astype(F32)).astype(BF16)
    return high, low


def make_tables(direct, turned, perm):
    rows = lax.broadcasted_iota(jnp.int32, (HALF, HALF), 0)
    cols = lax.broadcasted_iota(jnp.int32, (HALF, HALF), 1)
    for parity in (0, 1):
        for table, n, k in ((direct, rows, cols), (turned, cols, rows)):
            angle = lax.rem(n * (2 * k + parity), 256).astype(F32) * (2.0 * math.pi / 256)
            re, im = jnp.cos(angle) / 16, -jnp.sin(angle) / 16
            above, below = (im, -im) if table is direct else (-im, im)
            full = jnp.concatenate(
                [jnp.concatenate([re, above], axis=1), jnp.concatenate([below, re], axis=1)],
                axis=0,
            )
            table[parity, 0], table[parity, 1] = parts_of(full)
    old = lax.broadcasted_iota(jnp.int32, (256, 256), 0)
    new = lax.broadcasted_iota(jnp.int32, (256, 256), 1)
    perm[...] = jnp.where(lax.rem(old, 2) * HALF + old // 2 == new, 1.0, 0.0).astype(BF16)


def mul_right(x, table, p):
    high, low = parts_of(x)
    table = jnp.concatenate([table[p, 0], table[p, 0], table[p, 1]], axis=0)
    return jnp.dot(jnp.concatenate([high, low, high], axis=1), table, preferred_element_type=F32)


def mul_left(table, p, x):
    high, low = parts_of(x)
    table = jnp.concatenate([table[p, 0], table[p, 0], table[p, 1]], axis=1)
    return jnp.dot(table, jnp.concatenate([high, low, high], axis=0), preferred_element_type=F32)


def swap_blocks(a, b):
    return jnp.concatenate(
        [
            jnp.concatenate([a[:, :HALF], b[:, :HALF]], axis=1),
            jnp.concatenate([a[:, HALF:], b[:, HALF:]], axis=1),
        ],
        axis=0,
    )


def place():
    region, group = lax.axis_index("region"), lax.axis_index("group")
    core = lax.rem(region, 2)
    z = lax.rem(region // 2, 4)
    y = (group // 4) * 2 + region // 8
    x = lax.rem(group, 4)
    turned = ((x, y), (y, z), (z, x))
    return tuple(a + core * (b - a) for a, b in turned), core


def device(at, core, counted):
    a, b, c = at
    x, y, z = a + counted * (c - a), b + counted * (a - b), c + counted * (b - c)
    return ((lax.rem(y, 2) * 4 + z) * 2 + core, (y // 2) * 4 + x)


def step_kernel(
    pos_ref, count_ref, object_hbm, probe_hbm, diff_hbm,
    out_ref, arrived, new_ref,
    ext, win, far, wanted, probe, pgrad, cov, go, hx, strips, direct, turned, perm, diff,
    spill, mate, total, factor, covered, *rest,
):
    got, pieces, local_sem, send_sem, recv_sem = rest
    me, core = place()
    regions = lax.axis_size("region")
    region, group = lax.axis_index("region"), lax.axis_index("group")
    sibling = device(me, 1 - core, core)
    up = (lax.rem(region + 1, regions), group)
    down = (lax.rem(region + regions - 1, regions), group)
    own = object_hbm.shape[0]
    edge = spill.shape[0]

    loads = [
        pltpu.make_async_copy(src, dst, local_sem.at[n])
        for n, (src, dst) in enumerate(
            [
                (object_hbm, ext.at[:own]),
                (diff_hbm, diff),
                (probe_hbm, probe),
            ]
        )
    ]
    def shift(n, distance):
        return lax.rem(me[n] + distance, 4)

    plane_peers = [(shift(0, i), shift(1, j)) for i, j in OTHERS]
    plane_devices = [device((p, q, me[2]), core, core) for p, q in plane_peers]
    last_devices = [device((me[0], me[1], shift(2, d)), core, core) for d in (1, 2, 3)]

    barrier = pltpu.get_barrier_semaphore()
    partners = [sibling, up, down, *plane_devices, *last_devices]
    for partner in partners:
        pl.semaphore_signal(barrier, inc=1, device_id=partner, device_id_type=MESH)
    for load in loads:
        load.start()
    pl.semaphore_wait(barrier, len(partners))

    builders = {}

    def remote(key, build=None):
        if build is not None:
            builders[key] = (len(builders), build)
        n, build = builders[key]
        src, dst, to = build()
        return pltpu.make_async_remote_copy(
            src_ref=src, dst_ref=dst, send_sem=send_sem.at[n], recv_sem=recv_sem.at[n],
            device_id=to, device_id_type=MESH,
        )

    def send(key, build):
        remote(key, build).start()

    def arrive(key):
        remote(key).wait_recv()

    send("halo", lambda: (object_hbm.at[:edge], ext.at[own:], down))

    def result(u):
        return new_ref.at[2 * u + core]

    def start_core(u):
        send(
            ("core", u),
            lambda: (cov if u == COVERAGE else pgrad.at[2 * u + 1 - core], mate.at[u], sibling),
        )

    def start_plane(u):
        arrive(("core", u))
        total[u] = (cov[...] if u == COVERAGE else pgrad[2 * u + core]) + mate[u]
        for n, (p, q) in enumerate(plane_peers):
            send(
                ("plane", u, n),
                lambda n=n, p=p, q=q: (total.at[u, p, q], got.at[u, n], plane_devices[n]),
            )

    def start_last(u):
        for n in range(len(OTHERS)):
            arrive(("plane", u, n))
        value = total[u, me[0], me[1]]
        for n in range(len(OTHERS)):
            value = value + got[u, n]
        pieces[u, me[2]] = value
        for n in range(3):
            send(
                ("last", u, n),
                lambda n=n: (pieces.at[u, me[2]], pieces.at[u, me[2]], last_devices[n]),
            )

    def finish(u):
        for n in range(3):
            arrive(("last", u, n))
        reduced = (pieces[u, 0] + pieces[u, 1]) + (pieces[u, 2] + pieces[u, 3])
        if u == COVERAGE:
            covered[...] = reduced + 1e-06
            return
        here = (2 * u + core, me[0], me[1])
        new_ref[here] = probe[here] - reduced / covered[...]
        to = range(len(OTHERS)) if u == MODES - 1 else [OTHERS.index((0, d)) for d in (1, 2, 3)]
        for n in to:
            send(
                ("back", u, n),
                lambda n=n: (
                    result(u).at[me[0], me[1]],
                    result(u).at[me[0], me[1]],
                    plane_devices[n],
                ),
            )

    def relay(u):
        for d in (1, 2, 3):
            arrive(("back", u, OTHERS.index((0, d))))
        for d in (1, 2, 3):
            n = OTHERS.index((d, 0))
            send(
                ("back", u, n),
                lambda n=n: (result(u).at[me[0]], result(u).at[me[0]], plane_devices[n]),
            )

    def collect(u):
        to = range(len(OTHERS)) if u == MODES - 1 else [OTHERS.index((d, 0)) for d in (1, 2, 3)]
        for n in to:
            arrive(("back", u, n))

    def hand_over(u):
        collect(u)
        send(("over", u), lambda: (result(u), result(u), sibling))

    def tiles_of(x):
        return x.reshape(4, 4, 2, 8, HALF)

    pgrad[...] = jnp.zeros_like(pgrad)
    cov[...] = jnp.zeros_like(cov)
    go[...] = jnp.zeros_like(go)
    hx[:, :PAD] = jnp.zeros((SLOTS, PAD, 8, HALF), F32)
    hx[:, PAD + 256 :] = jnp.zeros((SLOTS, PAD, 8, HALF), F32)
    make_tables(direct, turned, perm)
    loads[1].wait()

    def prepare(s, carry):
        high, low = parts_of(
            jnp.sqrt(
                jnp.concatenate([diff[s, :, h].reshape(256, HALF) for h in (0, 1)], axis=1)
            )
        )
        root = jnp.dot(high, perm[...], preferred_element_type=F32) + jnp.dot(
            low, perm[...], preferred_element_type=F32
        )
        for h in (0, 1):
            wanted[s, h] = root[:, h * HALF : (h + 1) * HALF]
        return carry

    lax.fori_loop(0, SLOTS, prepare, 0)

    loads[2].wait()

    def probe_at(m, c):
        return jnp.concatenate(
            [probe[2 * m + c, :, :, :, h].reshape(256, HALF) for h in (0, 1)], axis=1
        )

    power = jnp.zeros((256, 256), F32)
    for m in range(MODES):
        pr, pi = probe_at(m, 0), probe_at(m, 1)
        power = power + pr * pr + pi * pi
    peak = jnp.max(power)
    loads[0].wait()
    arrive("halo")

    base = region * own

    def spot(s):
        return jnp.clip(pos_ref[0, s] - base, 0, own - 1), pos_ref[1, s]

    def pick_columns(col, shape, wide):
        at = lax.broadcasted_iota(jnp.int32, shape, wide)
        narrow = lax.broadcasted_iota(jnp.int32, shape, 1 - wide)
        return jnp.where(at - narrow == col, 1.0, 0.0).astype(BF16)

    def live(s, shape):
        return jnp.where(jnp.full(shape, s, jnp.int32) < count_ref[0, 0], 1.0, 0.0).astype(F32)

    def cut(s, carry):
        row, col = spot(s)
        strips[...] = ext[pl.ds(row, 256)].reshape(256 * 8, HALF)
        pick = pick_columns(col, (512, 256), 0)
        for c in (0, 1):
            strip = jnp.concatenate(
                [strips[pl.ds(2 * k + c, 256, stride=8), :] for k in range(4)], axis=1
            )
            high, low = parts_of(strip)
            win[s, c] = jnp.dot(high, pick, preferred_element_type=F32) + jnp.dot(
                low, pick, preferred_element_type=F32
            )
        wr, wi = win[s, 0], win[s, 1]
        power = live(s, (256, 256)) * (wr * wr + wi * wi)
        for h in (0, 1):
            cov[:, :, :, h] += tiles_of(power[:, h * HALF : (h + 1) * HALF])
        return carry

    lax.fori_loop(0, SLOTS, cut, 0)
    start_core(COVERAGE)

    def forward(s, carry):
        @pl.when(s == 1)
        def _():
            start_plane(COVERAGE)

        @pl.when(s == 3)
        def _():
            start_last(COVERAGE)

        wr, wi = win[s, 0], win[s, 1]
        for m in range(MODES):
            pr, pi = probe_at(m, 0), probe_at(m, 1)
            er = pr * wr - pi * wi
            ei = pr * wi + pi * wr
            a = jnp.concatenate([er[:, :HALF] + er[:, HALF:], ei[:, :HALF] + ei[:, HALF:]], axis=1)
            b = jnp.concatenate([er[:, :HALF] - er[:, HALF:], ei[:, :HALF] - ei[:, HALF:]], axis=1)
            ye = mul_right(a, direct, 0)
            yo = mul_right(b, direct, 1)
            plus = swap_blocks(ye[:HALF] + ye[HALF:], yo[:HALF] + yo[HALF:])
            minus = swap_blocks(ye[:HALF] - ye[HALF:], yo[:HALF] - yo[HALF:])
            far[s, m, 0] = mul_left(turned, 0, plus)
            far[s, m, 1] = mul_left(turned, 1, minus)
        for p in (0, 1):
            intensity = jnp.zeros((HALF, 256), F32)
            for m in range(MODES):
                fr, fi = far[s, m, p, :HALF], far[s, m, p, HALF:]
                intensity = intensity + (fr * fr + fi * fi)
            root = jnp.concatenate(
                [wanted[s, h, pl.ds(p, HALF, stride=2), :] for h in (0, 1)], axis=1
            )
            factor[s, p] = live(s, (HALF, 256)) * (
                1.0 - root / jnp.sqrt(jnp.maximum(intensity, 1.0))
            )
        return carry

    lax.fori_loop(0, SLOTS, forward, 0)

    def inverse(m, slots):
        for s in slots:
            wr, wi = win[s, 0], win[s, 1]
            e, o = [
                mul_left(
                    direct,
                    p,
                    far[s, m, p] * jnp.concatenate([factor[s, p], factor[s, p]], axis=0),
                )
                for p in (0, 1)
            ]
            top, bottom = e + o, e - o
            ae, ao = [
                jnp.concatenate(
                    [
                        jnp.concatenate([x[:HALF, at : at + HALF], x[HALF:, at : at + HALF]], axis=1)
                        for x in (top, bottom)
                    ],
                    axis=0,
                )
                for at in (0, HALF)
            ]
            e = mul_right(ae, turned, 0)
            o = mul_right(ao, turned, 1)
            left, right = e + o, e - o
            cr = jnp.concatenate([left[:, :HALF], right[:, :HALF]], axis=1)
            ci = jnp.concatenate([left[:, HALF:], right[:, HALF:]], axis=1)
            pr, pi = probe_at(m, 0), probe_at(m, 1)
            go[s, 0] += pr * cr + pi * ci
            go[s, 1] += pr * ci - pi * cr
            for c, g in enumerate((wr * cr + wi * ci, wr * ci - wi * cr)):
                for h in (0, 1):
                    pgrad[2 * m + c, :, :, :, h] += tiles_of(g[:, h * HALF : (h + 1) * HALF])

    for m in range(MODES):

        def of_mode(i, carry, m=m):
            if m == 3:

                @pl.when(i == 0)
                def _():
                    start_last(0)

            @pl.when(i == 1)
            def _():
                if m == 0:
                    finish(COVERAGE)
                else:
                    start_plane(m - 1)

            inverse(m, (2 * i, 2 * i + 1))
            return carry

        lax.fori_loop(0, SLOTS // 2, of_mode, 0)
        start_core(m)

    def turn(s, carry):
        pick = pick_columns(spot(s)[1], (256, 512), 1)
        for c in (0, 1):
            high, low = parts_of(go[s, c])
            strip = jnp.dot(high, pick, preferred_element_type=F32) + jnp.dot(
                low, pick, preferred_element_type=F32
            )
            for k in range(4):
                strips[pl.ds(2 * k + c, 256, stride=8), :] = strip[:, k * HALF : (k + 1) * HALF]
        hx[s, PAD : PAD + 256] = strips[...].reshape(256, 8, HALF)
        return carry

    lax.fori_loop(0, SLOTS // 2, turn, 0)
    start_plane(3)
    lax.fori_loop(SLOTS // 2, SLOTS, turn, 0)
    finish(0)

    def added(block):
        out = None
        for s in range(SLOTS):
            start = jnp.clip(block * PAD - spot(s)[0] + PAD, 0, PAD + 256)
            piece = hx[s, pl.ds(start, PAD)]
            out = piece if out is None else out + piece
        return out / peak

    blocks = own // PAD

    def below(i, carry):
        spill[pl.ds(i * PAD, PAD)] = added(blocks + i)
        return carry

    lax.fori_loop(0, edge // PAD, below, 0)
    send("spill", lambda: (spill, arrived, up))
    start_last(1)
    relay(0)

    def within(i, carry):
        at = pl.ds(i * PAD, PAD)
        out_ref[at] = ext[at] - added(i)
        return carry

    lax.fori_loop(0, blocks, within, 0)
    start_last(2)
    finish(1)
    start_last(3)
    finish(2)
    relay(1)
    finish(3)
    relay(2)
    for u in range(MODES):
        hand_over(u)
    arrive("spill")
    for u in range(MODES):
        arrive(("over", u))
    for key in builders:
        remote(key).wait_send()


def tiled(planes):
    return (
        planes.reshape(-1, 32, 8, 2, HALF)
        .transpose(0, 1, 3, 2, 4)
        .reshape(-1, *PLANE)
    )


def untiled(tiles, shape):
    return tiles.reshape(-1, 32, 2, 8, HALF).transpose(0, 1, 3, 2, 4).reshape(shape)


def step(positions, slot_counts, view, probe, diffraction):
    smem = pl.BlockSpec(memory_space=pltpu.SMEM)
    hbm = pl.BlockSpec(memory_space=pltpu.HBM)
    vmem = pl.BlockSpec(memory_space=pltpu.VMEM)
    own = view.shape[0]
    diffraction = diffraction.reshape(SLOTS, 32, 8, 2, HALF).transpose(0, 1, 3, 2, 4)
    edge = own // 2
    copies = 2 + (MODES + 1) * (1 + 15 + 3 + 15) + MODES
    return pl.pallas_call(
        step_kernel,
        out_shape=(
            jax.ShapeDtypeStruct(view.shape, F32),
            jax.ShapeDtypeStruct((edge, 8, HALF), F32),
            jax.ShapeDtypeStruct((8, *PLANE), F32),
        ),
        in_specs=[smem] * 2 + [hbm] * 3,
        out_specs=[vmem] * 3,
        scratch_shapes=[
            pltpu.VMEM((own + edge, 8, HALF), F32),
            pltpu.VMEM((SLOTS, 2, 256, 256), F32),
            pltpu.VMEM((SLOTS, MODES, 2, 256, 256), F32),
            pltpu.VMEM((SLOTS, 2, 256, HALF), F32),
            pltpu.VMEM((8, *PLANE), F32),
            pltpu.VMEM((8, *PLANE), F32),
            pltpu.VMEM(PLANE, F32),
            pltpu.VMEM((SLOTS, 2, 256, 256), F32),
            pltpu.VMEM((SLOTS, 256 + 2 * PAD, 8, HALF), F32),
            pltpu.VMEM((256 * 8, HALF), F32),
            pltpu.VMEM((2, 2, 256, 256), BF16),
            pltpu.VMEM((2, 2, 256, 256), BF16),
            pltpu.VMEM((256, 256), BF16),
            pltpu.VMEM(diffraction.shape, F32),
            pltpu.VMEM((edge, 8, HALF), F32),
            pltpu.VMEM((5, *PLANE), F32),
            pltpu.VMEM((5, *PLANE), F32),
            pltpu.VMEM((SLOTS, 2, HALF, 256), F32),
            pltpu.VMEM(PLANE[2:], F32),
            pltpu.VMEM((5, len(OTHERS), *PLANE[2:]), F32),
            pltpu.VMEM((5, 4, *PLANE[2:]), F32),
            pltpu.SemaphoreType.DMA((3,)),
            pltpu.SemaphoreType.DMA((copies,)),
            pltpu.SemaphoreType.DMA((copies,)),
        ],
        compiler_params=pltpu.CompilerParams(
            vmem_limit_bytes=46 << 20, collective_id=0, has_side_effects=True
        ),
        name="step",
    )(positions, slot_counts, view, tiled(probe), diffraction)


def on_device(object_slab, probe, diffraction, positions, slot_counts):
    tile_rows, _, tile_cols = object_slab.shape
    blocks = tile_cols // HALF
    view = (
        object_slab.reshape(tile_rows, 2, blocks, HALF)
        .transpose(0, 2, 1, 3)
        .reshape(tile_rows, blocks * 2, HALF)
    )
    view, arrived, new = step(positions.T, slot_counts, view, probe, diffraction)
    edge = arrived.shape[0]
    view = jnp.concatenate([view[:edge] - arrived, view[edge:]], axis=0)
    obj = (
        view.reshape(tile_rows, blocks, 2, HALF)
        .transpose(0, 2, 1, 3)
        .reshape(tile_rows, 2, tile_cols)
    )
    return (obj, untiled(new, probe.shape))


def solution(mesh):
    placed = (
        P("region", None, "group"),
        P(),
        P(("region", "group"), None, None),
        P(("region", "group"), None),
        P("group", "region"),
    )
    return jax.shard_map(
        on_device,
        mesh=mesh,
        in_specs=placed,
        out_specs=(P("region", None, "group"), P()),
        check_vma=False,
    )
```
